256 devices in a mesh: tm: 8 (over y, x_hi), space: 32 (over z, x_lo, core).
Axes of the slice: x: 4 (x_hi: 2, x_lo: 2; x = x_hi * 2 + x_lo), y: 4, z: 8, core: 2. Of those that a mesh axis runs over, the one named last changes fastest.
Arguments:
- wave_field: bfloat16 [16, 8192, 256], P('tm', 'space'), may hold values from -600 to 600
- cotangent: bfloat16 [16, 8192, 256], P('tm', 'space'), may hold values from -6 to 6
- block_lists: int32 [16, 64, 4], P('tm', 'space'), may hold values from 0 to 63, as said below
- project_weights: bfloat16 [2, 256, 768], replicated, may hold values from -2 to 2
- combine_weights: bfloat16 [2, 256, 256], replicated, may hold values from -0.375 to 0.375
Outputs:
- mixed_field: bfloat16 [16, 8192, 256], P('tm', 'space')
- field_grad: bfloat16 [16, 8192, 256], P('tm', 'space')
- project_grad: float32 [2, 256, 768], replicated
- combine_grad: float32 [2, 256, 256], replicated
The draws below stay inside these ranges and needn't reach their ends.
Inputs may be any that keep to these rules, and one draw needn't show every extreme that they name: `block_lists`: for frame f and block b, entry 0 is b itself, entry 1 is b - 2 or b + 2, and every entry lies within 2 blocks of b; entries may repeat.
All inputs are finite; a program needn't handle non-finite values.
Results may differ from the reference program's by a relative error of at most 0.012.
Values may be sent and summed in bfloat16 or wider, within the bound.
A program may use at most 128 MiB of HBM per device.

```python
import math
import jax
import jax.numpy as jnp
from jax import lax

D = 256
HEADS = 8
BLOCK = 128
KB = 4
HREACH = 2
ROWS_DEV = 256
FRAMES = 16
TOKENS_F = 8192


def draw_wave_field(key, part):
    key_base = jax.random.fold_in(key, 0)
    full_shape = (FRAMES, TOKENS_F, D)
    drawn = jnp.clip(jax.random.normal(key_base, full_shape, jnp.float32), -4.0, 4.0)
    return drawn.astype(jnp.bfloat16)


def draw_project_weights(key, part):
    key_base = jax.random.fold_in(key, 0)
    drawn = jnp.clip(jax.random.normal(key_base, (2, D, 3 * D), jnp.float32), -4.0, 4.0) / math.sqrt(D)
    return drawn.astype(jnp.bfloat16)


def draw_block_lists(key, part):
    key_sign, key_rest = jax.random.split(key)
    total_blocks = TOKENS_F // BLOCK
    own_block = jnp.broadcast_to(jnp.arange(total_blocks, dtype=jnp.int32)[None, :, None], (FRAMES, total_blocks, 1))
    direction = jax.random.randint(key_sign, (FRAMES, total_blocks, 1), 0, 2).astype(jnp.int32) * 2 - 1
    far_block = own_block + direction * HREACH
    far_block = jnp.where((far_block < 0) | (far_block >= total_blocks), own_block - direction * HREACH, far_block)
    offsets = jax.random.randint(key_rest, (FRAMES, total_blocks, KB - 2), -HREACH, HREACH + 1).astype(jnp.int32)
    others = jnp.clip(own_block + offsets, 0, total_blocks - 1)
    return jnp.concatenate([own_block, far_block, others], axis=2).astype(jnp.int32)


def shard_levels(stream_key, shape, cuts, least, largest):
    def one(dim, blocks):
        heights = jax.random.uniform(jax.random.fold_in(jax.random.fold_in(stream_key, 6), dim), (blocks,), jnp.float32, least / len(cuts), largest / len(cuts))
        return jnp.repeat(jnp.exp(heights), shape[dim] // blocks).reshape((-1,) + (1,) * (len(shape) - dim - 1))

    level = one(*cuts[0])
    for cut in cuts[1:]:
        level = level * one(*cut)
    return level


def bell_draw(rng, shape, scale, reach, cuts=(), held_as=jnp.bfloat16):
    entries = scale * jax.random.normal(rng, shape, jnp.float32)
    if cuts:
        entries = entries * shard_levels(rng, shape, cuts, -0.22, 0.18)
    return jnp.clip(entries, -reach, reach).astype(held_as)


def setup_inputs(seed: int = 0) -> dict:
    seeds = jax.random.split(jax.random.key(seed), 6)
    return {
        "wave_field": draw_wave_field(jax.random.fold_in(seeds[5], 71), 0),
        "cotangent": bell_draw(seeds[1], (FRAMES, TOKENS_F, D), 1.0, 6.0, ((0, 8), (1, 32))),
        "block_lists": draw_block_lists(jax.random.fold_in(seeds[5], 71), 0),
        "project_weights": draw_project_weights(jax.random.fold_in(seeds[5], 71), 0),
        "combine_weights": bell_draw(seeds[4], (2, D, D), D ** -0.5, 0.375),
    }


epsilon = 1e-05

def layer_norm(tok_rows):
    widened = tok_rows.astype(jnp.float32)
    centered = widened - lax.optimization_barrier(jnp.mean(widened, axis=-1, keepdims=True))
    inverse = lax.rsqrt(lax.optimization_barrier(jnp.mean(centered * centered, axis=-1, keepdims=True)) + epsilon)
    return (centered * inverse, inverse)

def norm_backward(upstream, normed, inverse):
    mean_grad = lax.optimization_barrier(jnp.mean(upstream, axis=-1, keepdims=True))
    mean_cross = lax.optimization_barrier(jnp.mean(upstream * normed, axis=-1, keepdims=True))
    return inverse * (upstream - mean_grad - normed * mean_cross)

def matmul(left_op, right_op):
    return jnp.dot(left_op, right_op, preferred_element_type=jnp.float32)

def wide_dot(left_op, right_op):
    return jnp.dot(left_op.astype(jnp.float32), right_op.astype(jnp.float32), precision=lax.Precision.HIGHEST)

def to_wide(values_in):
    return values_in.astype(jnp.float32)

def rounded_wide(values_in):
    return to_wide(lax.optimization_barrier(values_in.astype(jnp.bfloat16)))

def softmax_rows(scores, reduce_axis):
    row_max = lax.optimization_barrier(jnp.max(scores, axis=reduce_axis, keepdims=True))
    exp_scores = jnp.exp(scores - row_max)
    return lax.optimization_barrier((exp_scores / lax.optimization_barrier(jnp.sum(exp_scores, axis=reduce_axis, keepdims=True))).astype(jnp.bfloat16))

def spatial_forward(tok_rows, key_lists, project, combine, score_scale):
    tokens, features = tok_rows.shape
    head_width = features // HEADS
    normed, inverse = layer_norm(tok_rows)
    normed_act = normed.astype(jnp.bfloat16)
    projected = matmul(normed_act, project).astype(jnp.bfloat16)
    blocks = projected.reshape(tokens // BLOCK, BLOCK, 3, HEADS, head_width)

    def one_block(element):
        query_block, key_list = element
        picked = blocks[key_list].reshape(KB * BLOCK, 3, HEADS, head_width)
        scores = jnp.einsum('qhe,khe->hqk', to_wide(query_block[:, 0]), to_wide(picked[:, 1])) * score_scale
        attn_probs = softmax_rows(scores, 2)
        return jnp.einsum('hqk,khe->qhe', to_wide(attn_probs), to_wide(picked[:, 2])).astype(jnp.bfloat16)
    attended = lax.map(one_block, (blocks, key_lists)).reshape(tokens, features)
    mixed = (to_wide(tok_rows) + matmul(attended, combine)).astype(jnp.bfloat16)
    return (mixed, attended, normed, inverse, normed_act, blocks)

def spatial_backward(tok_rows, key_lists, mixed_grad, project, combine, score_scale):
    tokens, features = tok_rows.shape
    head_width = features // HEADS
    block_count = tokens // BLOCK
    mixed, attended, normed, inverse, normed_act, blocks = spatial_forward(tok_rows, key_lists, project, combine, score_scale)
    outward = matmul(attended.T, mixed_grad)
    attn_grad = matmul(mixed_grad, combine.T).astype(jnp.bfloat16).reshape(block_count, BLOCK, HEADS, head_width)

    def one_block(element):
        query_block, key_list, block_grad = element
        picked = blocks[key_list].reshape(KB * BLOCK, 3, HEADS, head_width)
        queries = to_wide(query_block[:, 0])
        key_part = to_wide(picked[:, 1])
        value_part = to_wide(picked[:, 2])
        prob_wide = to_wide(softmax_rows(jnp.einsum('qhe,khe->hqk', queries, key_part) * score_scale, 2))
        grad_wide = to_wide(block_grad)
        grad_probs = jnp.einsum('qhe,khe->hqk', grad_wide, value_part)
        row_delta = lax.optimization_barrier(jnp.sum(prob_wide * grad_probs, axis=2, keepdims=True))
        grad_scores = rounded_wide(prob_wide * (grad_probs - row_delta) * score_scale)
        grad_query = jnp.einsum('hqk,khe->qhe', grad_scores, key_part).astype(jnp.bfloat16)
        grad_keys = jnp.einsum('hqk,qhe->khe', grad_scores, queries)
        grad_values = jnp.einsum('hqk,qhe->khe', prob_wide, grad_wide)
        key_tiles = jnp.stack([grad_keys, grad_values], axis=1).reshape(KB, BLOCK * 2 * features)
        return (grad_query, key_tiles)
    grad_query, key_tiles = lax.map(one_block, (blocks, key_lists, attn_grad))
    summed = jax.ops.segment_sum(key_tiles.reshape(block_count * KB, BLOCK * 2 * features), key_lists.reshape(-1).astype(jnp.int32), num_segments=block_count)
    pair_flat = summed.reshape(tokens, 2 * features)
    query_flat = grad_query.reshape(tokens, features)
    inward = jnp.concatenate([matmul(normed_act.T, query_flat), wide_dot(normed_act.T, pair_flat)], axis=1)
    act_grad = matmul(query_flat, project[:, :features].T) + wide_dot(pair_flat, project[:, features:].T)
    field_rows = (to_wide(mixed_grad) + norm_backward(act_grad, normed, inverse)).astype(jnp.bfloat16)
    return (field_rows, inward, outward)

def temporal_pair(tok_rows, cot_rows, project, combine, score_scale):
    frame_count, row_count, features = tok_rows.shape
    head_width = features // HEADS
    normed, inverse = layer_norm(tok_rows)
    normed_act = normed.astype(jnp.bfloat16).reshape(frame_count * row_count, features)
    projected = matmul(normed_act, project).astype(jnp.bfloat16).reshape(frame_count, row_count, 3, HEADS, head_width)
    queries = to_wide(projected[:, :, 0])
    key_part = to_wide(projected[:, :, 1])
    value_part = to_wide(projected[:, :, 2])
    prob_wide = to_wide(softmax_rows(jnp.einsum('frhe,grhe->hfgr', queries, key_part) * score_scale, 2))
    attended = jnp.einsum('hfgr,grhe->frhe', prob_wide, value_part).astype(jnp.bfloat16).reshape(frame_count * row_count, features)
    mixed = (to_wide(tok_rows) + matmul(attended, combine).reshape(frame_count, row_count, features)).astype(jnp.bfloat16)
    flat_cot = cot_rows.reshape(frame_count * row_count, features)
    outward = matmul(attended.T, flat_cot)
    attn_grad = rounded_wide(matmul(flat_cot, combine.T)).reshape(frame_count, row_count, HEADS, head_width)
    grad_probs = jnp.einsum('frhe,grhe->hfgr', attn_grad, value_part)
    row_delta = lax.optimization_barrier(jnp.sum(prob_wide * grad_probs, axis=2, keepdims=True))
    grad_scores = rounded_wide(prob_wide * (grad_probs - row_delta) * score_scale)
    grad_query = jnp.einsum('hfgr,grhe->frhe', grad_scores, key_part)
    grad_keys = jnp.einsum('hfgr,frhe->grhe', grad_scores, queries)
    grad_values = jnp.einsum('hfgr,frhe->grhe', prob_wide, attn_grad)
    project_rows = jnp.stack([grad_query, grad_keys, grad_values], axis=2).astype(jnp.bfloat16).reshape(frame_count * row_count, 3 * features)
    inward = matmul(normed_act.T, project_rows)
    act_grad = matmul(project_rows, project.T).reshape(frame_count, row_count, features)
    field_rows = (to_wide(cot_rows) + norm_backward(act_grad, normed, inverse)).astype(jnp.bfloat16)
    return (mixed, field_rows, inward, outward)

def reference(wave_field, cotangent, block_lists, project_weights, combine_weights):
    frame_count, tokens, features = wave_field.shape
    score_scale = 1.0 / math.sqrt(features // HEADS)

    def forward_frame(element):
        return spatial_forward(element[0], element[1], project_weights[0], combine_weights[0], score_scale)[0]
    mixed_space = lax.map(forward_frame, (wave_field, block_lists))
    pieces = tokens // ROWS_DEV
    space_pieces = mixed_space.reshape(frame_count, pieces, ROWS_DEV, features).transpose(1, 0, 2, 3)
    cot_pieces = cotangent.reshape(frame_count, pieces, ROWS_DEV, features).transpose(1, 0, 2, 3)

    def time_step(running, element):
        mixed, field_rows, inward, outward = temporal_pair(element[0], element[1], project_weights[1], combine_weights[1], score_scale)
        return ((running[0] + inward, running[1] + outward), (mixed, field_rows))
    zero_grads = (jnp.zeros((features, 3 * features), jnp.float32), jnp.zeros((features, features), jnp.float32))
    (time_inward, time_outward), (mixed_pieces, grad_pieces) = lax.scan(time_step, zero_grads, (space_pieces, cot_pieces))
    mixed_field = mixed_pieces.transpose(1, 0, 2, 3).reshape(frame_count, tokens, features)
    mixed_grad = grad_pieces.transpose(1, 0, 2, 3).reshape(frame_count, tokens, features)

    def space_step(running, element):
        field_rows, inward, outward = spatial_backward(element[0], element[1], element[2], project_weights[0], combine_weights[0], score_scale)
        return ((running[0] + inward, running[1] + outward), field_rows)
    (space_inward, space_outward), field_grad = lax.scan(space_step, zero_grads, (wave_field, block_lists, mixed_grad))
    factor = 1.0 / math.sqrt(frame_count * tokens)
    project_grad = jnp.stack([space_inward, time_inward]) * factor
    combine_grad = jnp.stack([space_outward, time_outward]) * factor
    return (mixed_field, field_grad, project_grad, combine_grad)
```

```python
import functools
import math

import jax
import jax.numpy as jnp
from jax import lax
from jax.experimental import pallas as pl
from jax.experimental.pallas import tpu as pltpu
from jax.sharding import PartitionSpec as P

HEADS = 8
BLOCK = 128
SPAN = 5
KEYS = SPAN * BLOCK
D = 256
HD = 32
ROWS = 256
FR = 2
GROUPS = 4
CORES = 4
EPS = 1e-05
NEG = -1e30
SCALE = 1.0 / math.sqrt(HD)
SCALE2 = SCALE * math.log2(math.e)

MESH = pl.DeviceIdType.MESH
F32 = jnp.float32
BF16 = jnp.bfloat16


def nn(left, right):
    return jnp.dot(left, right, preferred_element_type=F32)


def nt(left, right):
    return lax.dot_general(left, right, (((1,), (1,)), ((), ())), preferred_element_type=F32)


def norm(rows):
    centered = rows - jnp.mean(rows, axis=-1, keepdims=True)
    inverse = lax.rsqrt(jnp.mean(centered * centered, axis=-1, keepdims=True) + EPS)
    return centered * inverse, inverse


def norm_back(upstream, normed, inverse):
    mean_grad = jnp.mean(upstream, axis=-1, keepdims=True)
    mean_cross = jnp.mean(upstream * normed, axis=-1, keepdims=True)
    return inverse * (upstream - mean_grad - normed * mean_cross)


def diag(pair):
    return jnp.concatenate([pair[0:HD, 0:BLOCK], pair[HD : 2 * HD, BLOCK : 2 * BLOCK]], axis=0)


def head_sums(prod):
    return jnp.sum(prod.reshape(HEADS, HD, BLOCK), axis=1)


def scratch_shapes(ntm, nsp):
    nz = nsp // CORES
    npl = ntm * CORES
    part = ROWS // ntm
    chunk = 512 // npl
    dma = pltpu.SemaphoreType.DMA
    vm = pltpu.VMEM
    return dict(
        xe=vm((3, FR, ROWS, D), BF16),
        act=vm((3, FR, ROWS, D), BF16),
        act_t=vm((FR, D, 3 * ROWS), BF16),
        nrm=vm((FR, ROWS, D), F32),
        rinv=vm((FR, ROWS, 1), F32),
        wv=vm((2, D, 3 * D), BF16),
        cv=vm((2, D, D), BF16),
        wt=vm((2, 2 * D, D), BF16),
        hm=vm((HEADS, BLOCK, D), BF16),
        q=vm((FR, ROWS, D), BF16),
        kv=vm((FR, 3 * ROWS, 2 * D), BF16),
        kvt=vm((FR, 2 * D, 3 * ROWS), BF16),
        qs=vm((4, HEADS * BLOCK, D), BF16),
        dos=vm((HEADS * BLOCK, D), BF16),
        probs=vm((4, KEYS, HEADS * BLOCK), BF16),
        ds=vm((KEYS, HEADS * BLOCK), BF16),
        s=vm((2, KEYS, 2 * BLOCK), F32),
        ot=vm((4, D, BLOCK), F32),
        otb=vm((D, 4 * BLOCK), BF16),
        att=vm((FR, ROWS, D), BF16),
        ms=vm((FR, ROWS, D), BF16),
        hist=vm((ntm, FR, part, D), BF16),
        hcot=vm((ntm, FR, part, D), BF16),
        xt=vm((GROUPS, BLOCK, D), F32),
        ct=vm((GROUPS, BLOCK, D), F32),
        tb=vm((BLOCK, 2 * BLOCK), F32),
        tnrm=vm((GROUPS * BLOCK, D), F32),
        trinv=vm((GROUPS * BLOCK, 1), F32),
        tact=vm((GROUPS * BLOCK, D), BF16),
        tp=vm((GROUPS * BLOCK, 3 * D), BF16),
        tkvt=vm((2 * D, GROUPS * BLOCK), BF16),
        tdo=vm((GROUPS * BLOCK, D), BF16),
        tdot=vm((D, GROUPS * BLOCK), BF16),
        tot=vm((D, GROUPS * BLOCK), BF16),
        tatt=vm((GROUPS * BLOCK, D), BF16),
        tdp=vm((GROUPS * BLOCK, 3 * D), BF16),
        tqs=vm((HEADS * BLOCK, D), BF16),
        tmix=vm((GROUPS, BLOCK, D), F32),
        mfs=vm((ntm, FR, part, D), BF16),
        mgs=vm((ntm, FR, part, D), BF16),
        mg=vm((FR, ROWS, D), BF16),
        do=vm((FR, ROWS, D), BF16),
        dot_t=vm((D, FR * ROWS), BF16),
        dq=vm((FR, ROWS, D), BF16),
        dkv=vm((FR, 3 * ROWS, 2 * D), F32),
        dkvb=vm((FR, 3 * ROWS, 2 * D), BF16),
        er=vm((FR, 2, ROWS, 2 * D), BF16),
        g=vm((2, 512, 512), BF16),
        rs=vm((2, npl - 1, chunk, 512), BF16),
        zb=vm((2, nz, chunk, 512), BF16),
        fin=vm((2, 512, 512), BF16),
        ld_sem=dma((6,)),
        halo_s=dma((2,)),
        halo_r=dma((2,)),
        cot_s=dma((ntm - 1,)),
        cot_r=dma((ntm - 1,)),
        ms_s=dma((FR, ntm - 1)),
        ms_r=dma((FR, ntm - 1)),
        mf_s=dma((ntm - 1,)),
        mf_r=dma((ntm - 1,)),
        mg_s=dma((ntm - 1,)),
        mg_r=dma((ntm - 1,)),
        ed_s=dma((FR, 2)),
        ed_r=dma((FR, 2)),
        rs_s=dma((2,)),
        rs_r=dma((2,)),
        z_s=dma((2,)),
        z_r=dma((2,)),
        ag_s=dma((2,)),
        ag_r=dma((2,)),
    )


def step_kernel(ntm, nsp, names, lists, x_hbm, cot_hbm, w_hbm, c_hbm, mixed_out, fg_out, pg_out, cg_out, *refs):
    r = dict(zip(names, refs))
    nz = nsp // CORES
    npl = ntm * CORES
    part = ROWS // ntm
    chunk = 512 // npl
    frames = FR * ntm
    per = BLOCK // frames
    factor = 1.0 / math.sqrt(frames * ROWS * nsp)

    tm = lax.axis_index("tm")
    sp = lax.axis_index("space")
    z = lax.div(sp, CORES)
    core = lax.rem(sp, CORES)
    left = lax.rem(sp + (nsp - 1), nsp)
    right = lax.rem(sp + 1, nsp)
    place = tm * CORES + core

    def plane_peer(d):
        other = lax.rem(place + d, npl)
        return (lax.div(other, CORES), z * CORES + lax.rem(other, CORES)), other

    def z_peer(d):
        return (tm, lax.rem(z + d, nz) * CORES + core)

    def remote(src, dst, send, recv, device):
        return pltpu.make_async_remote_copy(
            src_ref=src, dst_ref=dst, send_sem=send, recv_sem=recv, device_id=device, device_id_type=MESH
        )

    def loop(count, body):
        def wrapped(i, carry):
            body(i)
            return carry

        lax.fori_loop(0, count, wrapped, 0)

    barrier = pltpu.get_barrier_semaphore()
    pl.semaphore_signal(barrier, inc=1, device_id=(tm, left), device_id_type=MESH)
    pl.semaphore_signal(barrier, inc=1, device_id=(tm, right), device_id_type=MESH)
    loop(npl - 1, lambda i: pl.semaphore_signal(barrier, inc=1, device_id=plane_peer(i + 1)[0], device_id_type=MESH))
    loop(nz - 1, lambda i: pl.semaphore_signal(barrier, inc=1, device_id=z_peer(i + 1), device_id_type=MESH))

    ld = r["ld_sem"]
    own = pl.ds(pl.multiple_of(tm * part, part), part)
    loads = [
        pltpu.make_async_copy(w_hbm.at[0], r["wv"].at[0], ld.at[0]),
        pltpu.make_async_copy(x_hbm, r["xe"].at[1], ld.at[1]),
        pltpu.make_async_copy(c_hbm, r["cv"], ld.at[2]),
        pltpu.make_async_copy(w_hbm.at[1], r["wv"].at[1], ld.at[3]),
        pltpu.make_async_copy(cot_hbm.at[:, own, :], r["hcot"].at[0], ld.at[4]),
    ]
    for item in loads:
        item.start()

    lane_head = lax.broadcasted_iota(jnp.int32, (BLOCK, D), 1) // HD
    for h in range(HEADS):
        r["hm"][h] = jnp.where(lane_head == h, 1.0, 0.0).astype(BF16)
    key_pos = lax.broadcasted_iota(jnp.int32, (BLOCK, 2 * BLOCK), 0) % per
    query_pos = lax.broadcasted_iota(jnp.int32, (BLOCK, 2 * BLOCK), 1) % per
    r["tb"][...] = jnp.where(key_pos == query_pos, 0.0, NEG)

    loads[0].wait()
    r["wt"][0] = r["wv"][0, :, D:].astype(F32).T.astype(BF16)

    pl.semaphore_wait(barrier, 2 + (npl - 1) + (nz - 1))

    halos = [
        remote(x_hbm, r["xe"].at[2], r["halo_s"].at[0], r["halo_r"].at[0], (tm, left)),
        remote(x_hbm, r["xe"].at[0], r["halo_s"].at[1], r["halo_r"].at[1], (tm, right)),
    ]
    for item in halos:
        item.start()

    def cot_copy(d):
        to = lax.rem(tm + d, ntm)
        rows = pl.ds(pl.multiple_of(to * part, part), part)
        return remote(
            cot_hbm.at[:, rows, :], r["hcot"].at[d], r["cot_s"].at[d - 1], r["cot_r"].at[d - 1], (to, sp)
        )

    loop(ntm - 1, lambda i: cot_copy(i + 1).start())

    def project(slot, f):
        normed, inverse = norm(r["xe"][slot, f].astype(F32))
        rows = slice(slot * ROWS, (slot + 1) * ROWS)
        act = normed.astype(BF16)
        r["act"][slot, f] = act
        if slot == 1:
            r["nrm"][f] = normed
            r["rinv"][f] = inverse
            r["q"][f] = nn(act, r["wv"][0, :, 0:D]).astype(BF16)
        r["kv"][f, rows, :] = nn(act, r["wv"][0, :, D:]).astype(BF16)
        r["kvt"][f, :, rows] = nt(r["wt"][0], act).astype(BF16)

    loads[1].wait()
    for f in range(FR):
        project(1, f)
    for f in range(FR):
        for j in range(2):
            for h in range(HEADS):
                r["qs"][2 * f + j, h * BLOCK : (h + 1) * BLOCK, :] = (
                    r["q"][f, j * BLOCK : (j + 1) * BLOCK, :] * r["hm"][h]
                )
    halos[0].wait_recv()
    for f in range(FR):
        project(2, f)
    halos[1].wait_recv()
    for f in range(FR):
        project(0, f)

    def key_rows(j):
        return pl.ds(pl.multiple_of(j * BLOCK, BLOCK), KEYS)

    def biases(f, j):
        out = []
        first = sp * 2 + j - 2
        for e in range(SPAN):
            count = jnp.int32(0)
            for k in range(4):
                count = count + jnp.where(lists[f, j, k] == first + e, 1, 0)
            out.append(
                jnp.where(
                    count == 0,
                    NEG,
                    jnp.where(count == 1, 0.0, jnp.where(count == 2, 1.0, jnp.where(count == 3, math.log2(3.0), 2.0))),
                ).astype(F32)
            )
        return out

    def forward_block(f, j):
        i = 2 * f + j
        rows = key_rows(j)
        bias = biases(f, j)
        outs = []
        for pair in range(HEADS // 2):
            cols = slice(pair * 2 * BLOCK, (pair + 1) * 2 * BLOCK)
            s = r["s"].at[pair % 2]
            s[...] = nt(r["kv"][f, rows, 0:D], r["qs"][i, cols, :])
            top = None
            for e in range(SPAN):
                here = jnp.max(s[e * BLOCK : (e + 1) * BLOCK, :], axis=0, keepdims=True) * SCALE2 + bias[e]
                top = here if top is None else jnp.maximum(top, here)
            total = jnp.zeros((1, 2 * BLOCK), F32)
            for e in range(SPAN):
                block = slice(e * BLOCK, (e + 1) * BLOCK)
                grown = jnp.exp2(s[block, :] * SCALE2 + (bias[e] - top))
                s[block, :] = grown
                total = total + jnp.sum(grown, axis=0, keepdims=True)
            share = 1.0 / total
            for e in range(SPAN):
                block = slice(e * BLOCK, (e + 1) * BLOCK)
                r["probs"][i, block, cols] = (s[block, :] * share).astype(BF16)
            values = r["kvt"][f, D + pair * 2 * HD : D + (pair + 1) * 2 * HD, rows]
            outs.append(diag(nn(values, r["probs"][i, :, cols])))
        out = jnp.concatenate(outs, axis=0)
        r["ot"][i] = out
        r["otb"][:, pl.ds(pl.multiple_of(i * BLOCK, BLOCK), BLOCK)] = out.astype(BF16)
        r["att"][f, pl.ds(pl.multiple_of(j * BLOCK, BLOCK), BLOCK), :] = out.T.astype(BF16)

    def ms_copy(f, d):
        to = lax.rem(tm + d, ntm)
        rows = pl.ds(pl.multiple_of(to * part, part), part)
        return remote(
            r["ms"].at[f, rows, :], r["hist"].at[d, f], r["ms_s"].at[f, d - 1], r["ms_r"].at[f, d - 1], (to, sp)
        )

    loads[2].wait()

    def forward_frame(f):
        loop(2, lambda j: forward_block(f, j))
        mixed = r["xe"][1, f].astype(F32) + nn(r["att"][f], r["cv"][0])
        r["ms"][f] = mixed.astype(BF16)
        r["hist"][0, f] = r["ms"][f, own, :]
        loop(ntm - 1, lambda i: ms_copy(f, i + 1).start())

    loop(FR, forward_frame)

    for f in range(FR):
        for slot in range(3):
            r["act_t"][f, :, slot * ROWS : (slot + 1) * ROWS] = r["act"][slot, f].astype(F32).T.astype(BF16)
    loads[3].wait()
    r["wt"][1] = r["wv"][1, :, D:].astype(F32).T.astype(BF16)
    loads[4].wait()
    loop(ntm - 1, lambda i: cot_copy(i + 1).wait_recv())

    def regroup(src, dst):
        for d in range(ntm):
            for f in range(FR):
                frame = d * FR + f
                rows = src[d, f].astype(F32)
                for g in range(GROUPS):
                    dst[g, frame * per : (frame + 1) * per, :] = rows[g * per : (g + 1) * per]

    def ungroup(src, dst):
        for d in range(ntm):
            for f in range(FR):
                frame = d * FR + f
                dst[d, f] = jnp.concatenate(
                    [src[g, frame * per : (frame + 1) * per, :] for g in range(GROUPS)], axis=0
                ).astype(BF16)

    regroup(r["hcot"], r["ct"])
    for g in range(GROUPS):
        rows = slice(g * BLOCK, (g + 1) * BLOCK)
        cot = r["ct"][g].astype(BF16)
        r["tdo"][rows, :] = nt(cot, r["cv"][1]).astype(BF16)
        r["tdot"][:, rows] = nt(r["cv"][1], cot).astype(BF16)

    for f in range(FR):
        loop(ntm - 1, lambda i, f=f: ms_copy(f, i + 1).wait_recv())
    regroup(r["hist"], r["xt"])
    for g in range(GROUPS):
        rows = slice(g * BLOCK, (g + 1) * BLOCK)
        normed, inverse = norm(r["xt"][g])
        r["tnrm"][rows, :] = normed
        r["trinv"][rows, :] = inverse
        r["tact"][rows, :] = normed.astype(BF16)
    r["tp"][...] = nn(r["tact"][...], r["wv"][1]).astype(BF16)
    r["tkvt"][...] = nt(r["wt"][1], r["tact"][...]).astype(BF16)

    def time_group(g):
        rows = pl.ds(pl.multiple_of(g * BLOCK, BLOCK), BLOCK)
        query = r["tp"][rows, 0:D]
        keys = r["tp"][rows, D : 2 * D]
        values = r["tp"][rows, 2 * D : 3 * D]
        grad = r["tdo"][rows, :]
        for h in range(HEADS):
            r["tqs"][h * BLOCK : (h + 1) * BLOCK, :] = query * r["hm"][h]
            r["dos"][h * BLOCK : (h + 1) * BLOCK, :] = grad * r["hm"][h]
        outs = []
        parts = []
        for pair in range(HEADS // 2):
            cols = slice(pair * 2 * BLOCK, (pair + 1) * 2 * BLOCK)
            scores = nt(keys, r["tqs"][cols, :]) * SCALE2 + r["tb"][...]
            grown = jnp.exp2(scores - jnp.max(scores, axis=0, keepdims=True))
            share = 1.0 / jnp.sum(grown, axis=0, keepdims=True)
            probs = (grown * share).astype(BF16)
            parts.append(probs)
            outs.append(diag(nn(r["tkvt"][D + pair * 2 * HD : D + (pair + 1) * 2 * HD, rows], probs)))
        out = jnp.concatenate(outs, axis=0)
        r["tot"][:, rows] = out.astype(BF16)
        r["tatt"][rows, :] = out.T.astype(BF16)
        delta = head_sums(out * r["tdot"][:, rows].astype(F32))
        query_grads = []
        key_grad = None
        value_grad = None
        for pair in range(HEADS // 2):
            cols = slice(pair * 2 * BLOCK, (pair + 1) * 2 * BLOCK)
            dprob = nt(values, r["dos"][cols, :])
            shift = jnp.concatenate([delta[2 * pair : 2 * pair + 1], delta[2 * pair + 1 : 2 * pair + 2]], axis=1)
            dscore = (parts[pair].astype(F32) * (dprob - shift)).astype(BF16)
            query_grads.append(diag(nn(r["tkvt"][pair * 2 * HD : (pair + 1) * 2 * HD, rows], dscore)))
            more_key = nn(dscore, r["tqs"][cols, :])
            more_value = nn(parts[pair], r["dos"][cols, :])
            key_grad = more_key if key_grad is None else key_grad + more_key
            value_grad = more_value if value_grad is None else value_grad + more_value
        query_grad = jnp.concatenate(query_grads, axis=0).T
        r["tdp"][rows, 0:D] = (query_grad * SCALE).astype(BF16)
        r["tdp"][rows, D : 2 * D] = (key_grad * SCALE).astype(BF16)
        r["tdp"][rows, 2 * D : 3 * D] = value_grad.astype(BF16)

    loop(GROUPS, time_group)

    def back_rows(base, d):
        return base.at[:, own, :]

    def mg_copy(d):
        return remote(
            r["mgs"].at[d], r["mg"].at[:, own, :], r["mg_s"].at[d - 1], r["mg_r"].at[d - 1],
            (lax.rem(tm + (ntm - d), ntm), sp),
        )

    def mf_copy(d):
        return remote(
            r["mfs"].at[d], mixed_out.at[:, own, :], r["mf_s"].at[d - 1], r["mf_r"].at[d - 1],
            (lax.rem(tm + (ntm - d), ntm), sp),
        )

    for g in range(GROUPS):
        rows = slice(g * BLOCK, (g + 1) * BLOCK)
        act_grad = nt(r["tdp"][rows, :], r["wv"][1])
        r["tmix"][g] = r["ct"][g] + norm_back(act_grad, r["tnrm"][rows, :], r["trinv"][rows, :])
    ungroup(r["tmix"], r["mgs"])
    loop(ntm - 1, lambda i: mg_copy(i + 1).start())
    r["mg"][:, own, :] = r["mgs"][0]

    for g in range(GROUPS):
        rows = slice(g * BLOCK, (g + 1) * BLOCK)
        r["tmix"][g] = r["xt"][g] + nn(r["tatt"][rows, :], r["cv"][1])
    ungroup(r["tmix"], r["mfs"])
    loop(ntm - 1, lambda i: mf_copy(i + 1).start())
    keep = pltpu.make_async_copy(r["mfs"].at[0], mixed_out.at[:, own, :], ld.at[5])
    keep.start()

    turned = r["tact"][...].astype(F32).T.astype(BF16)
    r["g"][0, 0:D, :] = nn(turned, r["tdp"][:, D:]).astype(BF16)
    r["g"][0, D:, 0:D] = nn(turned, r["tdp"][:, 0:D]).astype(BF16)
    cots = r["ct"][...].reshape(GROUPS * BLOCK, D).astype(BF16)
    r["g"][0, D:, D:] = nn(r["tot"][...], cots).astype(BF16)

    my_chunk = pl.ds(pl.multiple_of(place * chunk, chunk), chunk)

    def rs_copy(a, d):
        device, other = plane_peer(d)
        rows = pl.ds(pl.multiple_of(other * chunk, chunk), chunk)
        return remote(r["g"].at[a, rows, :], r["rs"].at[a, d - 1], r["rs_s"].at[a], r["rs_r"].at[a], device)

    def z_copy(a, d):
        return remote(r["zb"].at[a, z], r["zb"].at[a, z], r["z_s"].at[a], r["z_r"].at[a], z_peer(d))

    def ag_copy(a, d):
        device, _ = plane_peer(d)
        return remote(r["fin"].at[a, my_chunk, :], r["fin"].at[a, my_chunk, :], r["ag_s"].at[a], r["ag_r"].at[a], device)

    def drain(ref, sem):
        pltpu.make_async_copy(ref, ref, sem).wait()

    def reduce_start(a):
        loop(npl - 1, lambda i: rs_copy(a, i + 1).start())

    def reduce_middle(a):
        drain(r["rs"].at[a], r["rs_r"].at[a])
        total = r["g"][a, my_chunk, :].astype(F32)
        for d in range(npl - 1):
            total = total + r["rs"][a, d].astype(F32)
        r["zb"][a, z] = total.astype(BF16)
        loop(nz - 1, lambda i: z_copy(a, i + 1).start())

    def reduce_share(a):
        drain(r["zb"].at[a, 0 : nz - 1], r["z_r"].at[a])
        total = r["zb"][a, 0].astype(F32)
        for k in range(1, nz):
            total = total + r["zb"][a, k].astype(F32)
        r["fin"][a, my_chunk, :] = total.astype(BF16)
        loop(npl - 1, lambda i: ag_copy(a, i + 1).start())

    def reduce_end(a, layer):
        drain(r["fin"].at[a, 0 : (npl - 1) * chunk, :], r["ag_r"].at[a])
        pg_out[layer, :, D:] = r["fin"][a, 0:D, :].astype(F32) * factor
        pg_out[layer, :, 0:D] = r["fin"][a, D:, 0:D].astype(F32) * factor
        cg_out[layer] = r["fin"][a, D:, D:].astype(F32) * factor

    def reduce_drain(a):
        drain(r["rs"].at[a], r["rs_s"].at[a])
        drain(r["zb"].at[a, 0 : nz - 1], r["z_s"].at[a])
        drain(r["fin"].at[a, 0 : (npl - 1) * chunk, :], r["ag_s"].at[a])

    reduce_start(0)

    r["dkv"][...] = jnp.zeros_like(r["dkv"])

    def mg_arrival(d):
        rows = pl.ds(pl.multiple_of(lax.rem(tm + d, ntm) * part, part), part)
        return remote(r["mgs"].at[d], r["mg"].at[:, rows, :], r["mg_s"].at[d - 1], r["mg_r"].at[d - 1], (tm, sp))

    loop(ntm - 1, lambda i: mg_arrival(i + 1).wait_recv())

    for f in range(FR):
        grad = r["mg"][f]
        r["do"][f] = nt(grad, r["cv"][0]).astype(BF16)
        r["dot_t"][:, f * ROWS : (f + 1) * ROWS] = nt(r["cv"][0], grad).astype(BF16)

    def backward_block(f, j):
        i = 2 * f + j
        rows = key_rows(j)
        mine = pl.ds(pl.multiple_of(j * BLOCK, BLOCK), BLOCK)
        grad = r["do"][f, mine, :]
        for h in range(HEADS):
            r["dos"][h * BLOCK : (h + 1) * BLOCK, :] = grad * r["hm"][h]
        lanes = pl.ds(pl.multiple_of(i * BLOCK, BLOCK), BLOCK)
        delta = head_sums(r["ot"][i] * r["dot_t"][:, lanes].astype(F32))
        outs = []
        for pair in range(HEADS // 2):
            cols = slice(pair * 2 * BLOCK, (pair + 1) * 2 * BLOCK)
            s = r["s"].at[pair % 2]
            s[...] = nt(r["kv"][f, rows, D:], r["dos"][cols, :])
            shift = jnp.concatenate([delta[2 * pair : 2 * pair + 1], delta[2 * pair + 1 : 2 * pair + 2]], axis=1)
            for e in range(SPAN):
                block = slice(e * BLOCK, (e + 1) * BLOCK)
                r["ds"][block, cols] = (r["probs"][i, block, cols].astype(F32) * (s[block, :] - shift)).astype(BF16)
            outs.append(diag(nn(r["kvt"][f, pair * 2 * HD : (pair + 1) * 2 * HD, rows], r["ds"][:, cols])))
        r["dq"][f, mine, :] = (jnp.concatenate(outs, axis=0) * SCALE).T.astype(BF16)
        r["dkv"][f, rows, 0:D] += nn(r["ds"][...], r["qs"][i]) * SCALE
        r["dkv"][f, rows, D:] += nn(r["probs"][i], r["dos"][...])

    def edge_copies(f):
        return [
            remote(r["dkvb"].at[f, 0:ROWS, :], r["er"].at[f, 1], r["ed_s"].at[f, 0], r["ed_r"].at[f, 0], (tm, left)),
            remote(
                r["dkvb"].at[f, 2 * ROWS :, :], r["er"].at[f, 0], r["ed_s"].at[f, 1], r["ed_r"].at[f, 1], (tm, right)
            ),
        ]

    def backward_frame(f):
        loop(2, lambda j: backward_block(f, j))
        r["dkvb"][f] = r["dkv"][f].astype(BF16)
        for item in edge_copies(f):
            item.start()

    backward_frame(0)
    reduce_middle(0)
    backward_frame(1)
    reduce_share(0)

    inward = nn(r["act_t"][0], r["dkvb"][0]) + nn(r["act_t"][1], r["dkvb"][1])
    r["g"][1, 0:D, :] = inward.astype(BF16)
    inward = nn(r["act_t"][0, :, ROWS : 2 * ROWS], r["dq"][0]) + nn(r["act_t"][1, :, ROWS : 2 * ROWS], r["dq"][1])
    r["g"][1, D:, 0:D] = inward.astype(BF16)
    outward = nn(r["otb"][:, 0:ROWS], r["mg"][0]) + nn(r["otb"][:, ROWS:], r["mg"][1])
    r["g"][1, D:, D:] = outward.astype(BF16)
    reduce_start(1)

    for f in range(FR):
        for item in edge_copies(f):
            item.wait_recv()
        pair_grad = r["dkv"][f, ROWS : 2 * ROWS, :] + r["er"][f, 0].astype(F32) + r["er"][f, 1].astype(F32)
        act_grad = nt(r["dq"][f], r["wv"][0, :, 0:D]) + nt(pair_grad.astype(BF16), r["wv"][0, :, D:])
        fg_out[f] = (r["mg"][f].astype(F32) + norm_back(act_grad, r["nrm"][f], r["rinv"][f])).astype(BF16)

    reduce_middle(1)
    reduce_end(0, 1)
    reduce_share(1)

    keep.wait()

    def mf_arrival(d):
        rows = pl.ds(pl.multiple_of(lax.rem(tm + d, ntm) * part, part), part)
        return remote(r["mfs"].at[d], mixed_out.at[:, rows, :], r["mf_s"].at[d - 1], r["mf_r"].at[d - 1], (tm, sp))

    loop(ntm - 1, lambda i: mf_arrival(i + 1).wait_recv())
    loop(ntm - 1, lambda i: mf_copy(i + 1).wait_send())
    loop(ntm - 1, lambda i: mg_copy(i + 1).wait_send())
    loop(ntm - 1, lambda i: cot_copy(i + 1).wait_send())
    for f in range(FR):
        loop(ntm - 1, lambda i, f=f: ms_copy(f, i + 1).wait_send())
        for item in edge_copies(f):
            item.wait_send()
    for item in halos:
        item.wait_send()
    reduce_drain(0)

    reduce_end(1, 0)
    reduce_drain(1)


def per_device(ntm, nsp, wave_field, cotangent, block_lists, project_weights, combine_weights):
    shapes = scratch_shapes(ntm, nsp)
    names = tuple(shapes)
    anywhere = pl.BlockSpec(memory_space=pl.ANY)
    vmem = pl.BlockSpec(memory_space=pltpu.VMEM)
    return pl.pallas_call(
        functools.partial(step_kernel, ntm, nsp, names),
        out_shape=(
            jax.ShapeDtypeStruct((FR, ROWS, D), BF16),
            jax.ShapeDtypeStruct((FR, ROWS, D), BF16),
            jax.ShapeDtypeStruct((2, D, 3 * D), F32),
            jax.ShapeDtypeStruct((2, D, D), F32),
        ),
        in_specs=[pl.BlockSpec(memory_space=pltpu.SMEM), anywhere, anywhere, anywhere, anywhere],
        out_specs=(anywhere, vmem, vmem, vmem),
        scratch_shapes=list(shapes.values()),
        compiler_params=pltpu.CompilerParams(
            collective_id=0, has_side_effects=True, vmem_limit_bytes=60 * 1024 * 1024
        ),
        name="cuboid_step",
    )(block_lists, wave_field, cotangent, project_weights, combine_weights)


def solution(mesh):
    in_specs = (P("tm", "space", None), P("tm", "space", None), P("tm", "space", None), P(), P())
    out_specs = (P("tm", "space", None), P("tm", "space", None), P(), P())
    return jax.shard_map(
        functools.partial(per_device, mesh.shape["tm"], mesh.shape["space"]),
        mesh=mesh,
        in_specs=in_specs,
        out_specs=out_specs,
        check_vma=False,
    )
```

```python
import functools
import math

import jax
import jax.numpy as jnp
from jax import lax
from jax.experimental import pallas as pl
from jax.experimental.pallas import tpu as pltpu
from jax.sharding import PartitionSpec as P

HEADS = 8
BLOCK = 128
SPAN = 5
KEYS = SPAN * BLOCK
D = 256
HD = 32
ROWS = 256
FR = 2
GROUPS = 4
CORES = 4
EPS = 1e-05
NEG = -1e30
SCALE = 1.0 / math.sqrt(HD)
SCALE2 = SCALE * math.log2(math.e)

MESH = pl.DeviceIdType.MESH
F32 = jnp.float32
BF16 = jnp.bfloat16


def nn(left, right):
    return jnp.dot(left, right, preferred_element_type=F32)


def nt(left, right):
    return lax.dot_general(left, right, (((1,), (1,)), ((), ())), preferred_element_type=F32)


def norm(rows):
    centered = rows - jnp.mean(rows, axis=-1, keepdims=True)
    inverse = lax.rsqrt(jnp.mean(centered * centered, axis=-1, keepdims=True) + EPS)
    return centered * inverse, inverse


def norm_back(upstream, normed, inverse):
    mean_grad = jnp.mean(upstream, axis=-1, keepdims=True)
    mean_cross = jnp.mean(upstream * normed, axis=-1, keepdims=True)
    return inverse * (upstream - mean_grad - normed * mean_cross)


def diag(pair):
    return jnp.concatenate([pair[0:HD, 0:BLOCK], pair[HD : 2 * HD, BLOCK : 2 * BLOCK]], axis=0)


def head_sums(prod):
    return jnp.sum(prod.reshape(HEADS, HD, BLOCK), axis=1)


def scratch_shapes(ntm, nsp):
    nz = nsp // CORES
    npl = ntm * 2
    part = ROWS // ntm
    chunk = 256 // npl
    dma = pltpu.SemaphoreType.DMA
    vm = pltpu.VMEM
    return dict(
        xe=vm((3, FR, ROWS, D), BF16),
        act=vm((3, FR, ROWS, D), BF16),
        act_t=vm((FR, D, 3 * ROWS), BF16),
        nrm=vm((FR, ROWS, D), F32),
        rinv=vm((FR, ROWS, 1), F32),
        wv=vm((2, D, 3 * D), BF16),
        cv=vm((2, D, D), BF16),
        wt=vm((2, 2 * D, D), BF16),
        hm=vm((HEADS, BLOCK, D), BF16),
        q=vm((FR, ROWS, D), BF16),
        kv=vm((FR, 3 * ROWS, 2 * D), BF16),
        kvt=vm((FR, 2 * D, 3 * ROWS), BF16),
        qs=vm((4, HEADS * BLOCK, D), BF16),
        dos=vm((4, HEADS * BLOCK, D), BF16),
        share=vm((4, HEADS, BLOCK), F32),
        delta=vm((4, HEADS, BLOCK), F32),
        probs=vm((4, KEYS, HEADS * BLOCK), BF16),
        ds=vm((KEYS, HEADS * BLOCK), BF16),
        s=vm((2, KEYS, 2 * BLOCK), F32),
        ot=vm((4, D, BLOCK), F32),
        otb=vm((D, 4 * BLOCK), BF16),
        att=vm((FR, ROWS, D), BF16),
        ms=vm((FR, ROWS, D), BF16),
        hist=vm((ntm, FR, part, D), BF16),
        hcot=vm((ntm, FR, part, D), BF16),
        xt=vm((GROUPS, BLOCK, D), F32),
        ct=vm((GROUPS, BLOCK, D), F32),
        tb=vm((BLOCK, 2 * BLOCK), F32),
        tnrm=vm((GROUPS * BLOCK, D), F32),
        trinv=vm((GROUPS * BLOCK, 1), F32),
        tact=vm((GROUPS * BLOCK, D), BF16),
        tp=vm((GROUPS * BLOCK, 3 * D), BF16),
        tkvt=vm((2 * D, GROUPS * BLOCK), BF16),
        tdo=vm((GROUPS * BLOCK, D), BF16),
        tdot=vm((D, GROUPS * BLOCK), BF16),
        tot=vm((D, GROUPS * BLOCK), BF16),
        tatt=vm((GROUPS * BLOCK, D), BF16),
        tdp=vm((GROUPS * BLOCK, 3 * D), BF16),
        tqs=vm((GROUPS, HEADS * BLOCK, D), BF16),
        tdos=vm((GROUPS, HEADS * BLOCK, D), BF16),
        tprobs=vm((GROUPS, BLOCK, HEADS * BLOCK), BF16),
        tds=vm((GROUPS, BLOCK, HEADS * BLOCK), BF16),
        tmix=vm((GROUPS, BLOCK, D), F32),
        mfs=vm((ntm, FR, part, D), BF16),
        mgs=vm((ntm, FR, part, D), BF16),
        mg=vm((FR, ROWS, D), BF16),
        dq=vm((FR, ROWS, D), BF16),
        dkv=vm((FR, 3 * ROWS, 2 * D), F32),
        dkvb=vm((FR, 3 * ROWS, 2 * D), BF16),
        er=vm((FR, 2, ROWS, 2 * D), BF16),
        g=vm((2, 512, 512), BF16),
        pr=vm((2, 256, 512), BF16),
        h=vm((2, 256, 512), BF16),
        fg=vm((FR, ROWS, D), BF16),
        rs=vm((2, npl - 1, chunk, 512), BF16),
        zb=vm((2, nz, chunk, 512), BF16),
        fin=vm((2, 512, 512), BF16),
        ld_sem=dma((6,)),
        halo_s=dma((2,)),
        halo_r=dma((2,)),
        cot_s=dma((ntm - 1,)),
        cot_r=dma((ntm - 1,)),
        ms_s=dma((FR, ntm - 1)),
        ms_r=dma((FR, ntm - 1)),
        mf_s=dma((ntm - 1,)),
        mf_r=dma((ntm - 1,)),
        mg_s=dma((ntm - 1,)),
        mg_r=dma((ntm - 1,)),
        ed_s=dma((FR, 2)),
        ed_r=dma((FR, 2)),
        pr_s=dma((2,)),
        pr_r=dma((2,)),
        pg_s=dma((2,)),
        pg_r=dma((2,)),
        out_s=dma((4,)),
        rs_s=dma((2,)),
        rs_r=dma((2,)),
        z_s=dma((2,)),
        z_r=dma((2,)),
        ag_s=dma((2,)),
        ag_r=dma((2,)),
    )


def step_kernel(ntm, nsp, names, lists, x_hbm, cot_hbm, w_hbm, c_hbm, mixed_out, fg_out, fin_out, *refs):
    r = dict(zip(names, refs))
    nz = nsp // CORES
    npl = ntm * 2
    part = ROWS // ntm
    chunk = 256 // npl
    frames = FR * ntm
    per = BLOCK // frames

    tm = lax.axis_index("tm")
    sp = lax.axis_index("space")
    z = lax.div(sp, CORES)
    quarter = lax.rem(sp, CORES)
    core = lax.rem(sp, 2)
    partner = sp + 1 - 2 * core
    left = lax.rem(sp + (nsp - 1), nsp)
    right = lax.rem(sp + 1, nsp)
    place = tm * 2 + lax.div(quarter, 2)

    def plane_peer(d):
        other = lax.rem(place + d, npl)
        return (lax.div(other, 2), z * CORES + lax.rem(other, 2) * 2 + core), other

    def z_peer(d):
        return (tm, lax.rem(z + d, nz) * CORES + quarter)

    def remote(src, dst, send, recv, device):
        return pltpu.make_async_remote_copy(
            src_ref=src, dst_ref=dst, send_sem=send, recv_sem=recv, device_id=device, device_id_type=MESH
        )

    def loop(count, body):
        def wrapped(i, carry):
            body(i)
            return carry

        lax.fori_loop(0, count, wrapped, 0)

    barrier = pltpu.get_barrier_semaphore()
    pl.semaphore_signal(barrier, inc=1, device_id=(tm, left), device_id_type=MESH)
    pl.semaphore_signal(barrier, inc=1, device_id=(tm, right), device_id_type=MESH)
    loop(npl - 1, lambda i: pl.semaphore_signal(barrier, inc=1, device_id=plane_peer(i + 1)[0], device_id_type=MESH))
    loop(nz - 1, lambda i: pl.semaphore_signal(barrier, inc=1, device_id=z_peer(i + 1), device_id_type=MESH))

    ld = r["ld_sem"]
    own = pl.ds(pl.multiple_of(tm * part, part), part)
    loads = [
        pltpu.make_async_copy(w_hbm.at[0], r["wv"].at[0], ld.at[0]),
        pltpu.make_async_copy(x_hbm, r["xe"].at[1], ld.at[1]),
        pltpu.make_async_copy(c_hbm, r["cv"], ld.at[2]),
        pltpu.make_async_copy(w_hbm.at[1], r["wv"].at[1], ld.at[3]),
        pltpu.make_async_copy(cot_hbm.at[:, own, :], r["hcot"].at[0], ld.at[4]),
    ]
    for item in loads:
        item.start()

    lane_head = lax.broadcasted_iota(jnp.int32, (BLOCK, D), 1) // HD
    for h in range(HEADS):
        r["hm"][h] = jnp.where(lane_head == h, 1.0, 0.0).astype(BF16)
    key_pos = lax.broadcasted_iota(jnp.int32, (BLOCK, 2 * BLOCK), 0) % per
    query_pos = lax.broadcasted_iota(jnp.int32, (BLOCK, 2 * BLOCK), 1) % per
    r["tb"][...] = jnp.where(key_pos == query_pos, 0.0, NEG)

    loads[0].wait()
    r["wt"][0] = r["wv"][0, :, D:].astype(F32).T.astype(BF16)

    pl.semaphore_wait(barrier, 2 + (npl - 1) + (nz - 1))

    halos = [
        remote(x_hbm, r["xe"].at[2], r["halo_s"].at[0], r["halo_r"].at[0], (tm, left)),
        remote(x_hbm, r["xe"].at[0], r["halo_s"].at[1], r["halo_r"].at[1], (tm, right)),
    ]
    for item in halos:
        item.start()

    def cot_copy(d):
        to = lax.rem(tm + d, ntm)
        rows = pl.ds(pl.multiple_of(to * part, part), part)
        return remote(
            cot_hbm.at[:, rows, :], r["hcot"].at[d], r["cot_s"].at[d - 1], r["cot_r"].at[d - 1], (to, sp)
        )

    def project(slot, f):
        normed, inverse = norm(r["xe"][slot, f].astype(F32))
        rows = slice(slot * ROWS, (slot + 1) * ROWS)
        act = normed.astype(BF16)
        r["act"][slot, f] = act
        if slot == 1:
            r["nrm"][f] = normed
            r["rinv"][f] = inverse
            r["q"][f] = nn(act, r["wv"][0, :, 0:D]).astype(BF16)
        r["kv"][f, rows, :] = nn(act, r["wv"][0, :, D:]).astype(BF16)
        r["kvt"][f, :, rows] = nt(r["wt"][0], act).astype(BF16)

    loads[1].wait()
    for f in range(FR):
        project(1, f)
    for f in range(FR):
        for j in range(2):
            for h in range(HEADS):
                r["qs"][2 * f + j, h * BLOCK : (h + 1) * BLOCK, :] = (
                    r["q"][f, j * BLOCK : (j + 1) * BLOCK, :] * r["hm"][h]
                )
    halos[0].wait_recv()
    for f in range(FR):
        project(2, f)
    halos[1].wait_recv()
    loop(ntm - 1, lambda i: cot_copy(i + 1).start())
    for f in range(FR):
        project(0, f)

    def key_rows(j):
        return pl.ds(pl.multiple_of(j * BLOCK, BLOCK), KEYS)

    def biases(f, j):
        out = []
        first = sp * 2 + j - 2
        for e in range(SPAN):
            count = jnp.int32(0)
            for k in range(4):
                count = count + jnp.where(lists[f, j, k] == first + e, 1, 0)
            out.append(
                jnp.where(
                    count == 0,
                    NEG,
                    jnp.where(count == 1, 0.0, jnp.where(count == 2, 1.0, jnp.where(count == 3, math.log2(3.0), 2.0))),
                ).astype(F32)
            )
        return out

    def forward_block(f, j):
        i = 2 * f + j
        rows = key_rows(j)
        bias = biases(f, j)
        outs = []
        for pair in range(HEADS // 2):
            cols = slice(pair * 2 * BLOCK, (pair + 1) * 2 * BLOCK)
            s = r["s"].at[pair % 2]
            scores = nt(r["kv"][f, rows, 0:D], r["qs"][i, cols, :])
            s[...] = scores
            top = None
            for e in range(SPAN):
                here = jnp.max(scores[e * BLOCK : (e + 1) * BLOCK, :], axis=0, keepdims=True) * SCALE2 + bias[e]
                top = here if top is None else jnp.maximum(top, here)
            total = jnp.zeros((1, 2 * BLOCK), F32)
            for e in range(SPAN):
                block = slice(e * BLOCK, (e + 1) * BLOCK)
                grown = jnp.exp2(s[block, :] * SCALE2 + (bias[e] - top))
                r["probs"][i, block, cols] = grown.astype(BF16)
                total = total + jnp.sum(grown, axis=0, keepdims=True)
            share = 1.0 / total
            r["share"][i, 2 * pair : 2 * pair + 1, :] = share[:, 0:BLOCK]
            r["share"][i, 2 * pair + 1 : 2 * pair + 2, :] = share[:, BLOCK:]
            values = r["kvt"][f, D + pair * 2 * HD : D + (pair + 1) * 2 * HD, rows]
            outs.append(diag(nn(values, r["probs"][i, :, cols]) * share))
        out = jnp.concatenate(outs, axis=0)
        r["ot"][i] = out
        r["otb"][:, pl.ds(pl.multiple_of(i * BLOCK, BLOCK), BLOCK)] = out.astype(BF16)
        r["att"][f, pl.ds(pl.multiple_of(j * BLOCK, BLOCK), BLOCK), :] = out.T.astype(BF16)

    def ms_copy(f, d):
        to = lax.rem(tm + d, ntm)
        rows = pl.ds(pl.multiple_of(to * part, part), part)
        return remote(
            r["ms"].at[f, rows, :], r["hist"].at[d, f], r["ms_s"].at[f, d - 1], r["ms_r"].at[f, d - 1], (to, sp)
        )

    loads[2].wait()

    def forward_frame(f):
        loop(2, lambda j: forward_block(f, j))
        mixed = r["xe"][1, f].astype(F32) + nn(r["att"][f], r["cv"][0])
        r["ms"][f] = mixed.astype(BF16)
        r["hist"][0, f] = r["ms"][f, own, :]
        loop(ntm - 1, lambda i: ms_copy(f, i + 1).start())

    loop(FR, forward_frame)

    for f in range(FR):
        for slot in range(3):
            r["act_t"][f, :, slot * ROWS : (slot + 1) * ROWS] = r["act"][slot, f].astype(F32).T.astype(BF16)
    loads[3].wait()
    r["wt"][1] = r["wv"][1, :, D:].astype(F32).T.astype(BF16)
    loads[4].wait()
    loop(ntm - 1, lambda i: cot_copy(i + 1).wait_recv())

    def regroup(src, dst):
        for d in range(ntm):
            for f in range(FR):
                frame = d * FR + f
                rows = src[d, f].astype(F32)
                for g in range(GROUPS):
                    dst[g, frame * per : (frame + 1) * per, :] = rows[g * per : (g + 1) * per]

    def ungroup(src, dst):
        for d in range(ntm):
            for f in range(FR):
                frame = d * FR + f
                dst[d, f] = jnp.concatenate(
                    [src[g, frame * per : (frame + 1) * per, :] for g in range(GROUPS)], axis=0
                ).astype(BF16)

    regroup(r["hcot"], r["ct"])
    for g in range(GROUPS):
        rows = slice(g * BLOCK, (g + 1) * BLOCK)
        cot = r["ct"][g].astype(BF16)
        grad = nt(cot, r["cv"][1]).astype(BF16)
        for h in range(HEADS):
            r["tdos"][g, h * BLOCK : (h + 1) * BLOCK, :] = grad * r["hm"][h]
        r["tdot"][:, rows] = nt(r["cv"][1], cot).astype(BF16)

    for f in range(FR):
        loop(ntm - 1, lambda i, f=f: ms_copy(f, i + 1).wait_recv())
        for d in range(ntm):
            frame = d * FR + f
            block = r["hist"][d, f].astype(F32)
            normed, inverse = norm(block)
            for g in range(GROUPS):
                to = slice(frame * per, (frame + 1) * per)
                at = slice(g * BLOCK + frame * per, g * BLOCK + (frame + 1) * per)
                mine = slice(g * per, (g + 1) * per)
                r["xt"][g, to, :] = block[mine]
                r["tnrm"][at, :] = normed[mine]
                r["trinv"][at, :] = inverse[mine]
    r["tact"][...] = r["tnrm"][...].astype(BF16)
    r["tp"][...] = nn(r["tact"][...], r["wv"][1]).astype(BF16)
    r["tkvt"][...] = nt(r["wt"][1], r["tact"][...]).astype(BF16)

    def time_scores(g):
        rows = slice(g * BLOCK, (g + 1) * BLOCK)
        query = r["tp"][rows, 0:D]
        for h in range(HEADS):
            r["tqs"][g, h * BLOCK : (h + 1) * BLOCK, :] = query * r["hm"][h]
        for pair in range(HEADS // 2):
            cols = slice(pair * 2 * BLOCK, (pair + 1) * 2 * BLOCK)
            scores = nt(r["tp"][rows, D : 2 * D], r["tqs"][g, cols, :]) * SCALE2 + r["tb"][...]
            grown = jnp.exp2(scores - jnp.max(scores, axis=0, keepdims=True))
            share = 1.0 / jnp.sum(grown, axis=0, keepdims=True)
            r["tprobs"][g, :, cols] = (grown * share).astype(BF16)

    def time_out(g):
        rows = slice(g * BLOCK, (g + 1) * BLOCK)
        outs = []
        for pair in range(HEADS // 2):
            cols = slice(pair * 2 * BLOCK, (pair + 1) * 2 * BLOCK)
            values = r["tkvt"][D + pair * 2 * HD : D + (pair + 1) * 2 * HD, rows]
            outs.append(diag(nn(values, r["tprobs"][g, :, cols])))
        out = jnp.concatenate(outs, axis=0)
        r["tot"][:, rows] = out.astype(BF16)
        r["tatt"][rows, :] = out.T.astype(BF16)
        delta = head_sums(out * r["tdot"][:, rows].astype(F32))
        for pair in range(HEADS // 2):
            cols = slice(pair * 2 * BLOCK, (pair + 1) * 2 * BLOCK)
            dprob = nt(r["tp"][rows, 2 * D :], r["tdos"][g, cols, :])
            shift = jnp.concatenate([delta[2 * pair : 2 * pair + 1], delta[2 * pair + 1 : 2 * pair + 2]], axis=1)
            r["tds"][g, :, cols] = (r["tprobs"][g, :, cols].astype(F32) * (dprob - shift)).astype(BF16)

    def time_grads(g):
        rows = slice(g * BLOCK, (g + 1) * BLOCK)
        outs = []
        for pair in range(HEADS // 2):
            cols = slice(pair * 2 * BLOCK, (pair + 1) * 2 * BLOCK)
            outs.append(diag(nn(r["tkvt"][pair * 2 * HD : (pair + 1) * 2 * HD, rows], r["tds"][g, :, cols])))
        r["tdp"][rows, 0:D] = (jnp.concatenate(outs, axis=0) * SCALE).T.astype(BF16)
        r["tdp"][rows, D : 2 * D] = (nn(r["tds"][g], r["tqs"][g]) * SCALE).astype(BF16)
        r["tdp"][rows, 2 * D : 3 * D] = nn(r["tprobs"][g], r["tdos"][g]).astype(BF16)

    for g in range(GROUPS):
        time_scores(g)
    for g in range(GROUPS):
        time_out(g)
    for g in range(GROUPS):
        time_grads(g)

    def mg_copy(d):
        return remote(
            r["mgs"].at[d], r["mg"].at[:, own, :], r["mg_s"].at[d - 1], r["mg_r"].at[d - 1],
            (lax.rem(tm + (ntm - d), ntm), sp),
        )

    def mf_copy(d):
        return remote(
            r["mfs"].at[d], mixed_out.at[:, own, :], r["mf_s"].at[d - 1], r["mf_r"].at[d - 1],
            (lax.rem(tm + (ntm - d), ntm), sp),
        )

    for g in range(GROUPS):
        rows = slice(g * BLOCK, (g + 1) * BLOCK)
        act_grad = nt(r["tdp"][rows, :], r["wv"][1])
        r["tmix"][g] = r["ct"][g] + norm_back(act_grad, r["tnrm"][rows, :], r["trinv"][rows, :])
    ungroup(r["tmix"], r["mgs"])
    loop(ntm - 1, lambda i: mg_copy(i + 1).start())
    r["mg"][:, own, :] = r["mgs"][0]

    for g in range(GROUPS):
        rows = slice(g * BLOCK, (g + 1) * BLOCK)
        r["tmix"][g] = r["xt"][g] + nn(r["tatt"][rows, :], r["cv"][1])
    ungroup(r["tmix"], r["mfs"])
    keep = pltpu.make_async_copy(r["mfs"].at[0], mixed_out.at[:, own, :], ld.at[5])
    keep.start()

    turned = r["tact"][...].astype(F32).T.astype(BF16)
    r["g"][0, 0:D, :] = nn(turned, r["tdp"][:, D:]).astype(BF16)
    r["g"][0, D:, 0:D] = nn(turned, r["tdp"][:, 0:D]).astype(BF16)
    cots = r["ct"][...].reshape(GROUPS * BLOCK, D).astype(BF16)
    r["g"][0, D:, D:] = nn(r["tot"][...], cots).astype(BF16)

    my_half = pl.ds(pl.multiple_of(core * 256, 256), 256)
    other_half = pl.ds(pl.multiple_of((1 - core) * 256, 256), 256)
    in_half = pl.ds(pl.multiple_of(place * chunk, chunk), chunk)
    my_chunk = pl.ds(pl.multiple_of(core * 256 + place * chunk, chunk), chunk)

    def pair_copy(a):
        return remote(r["g"].at[a, other_half, :], r["pr"].at[a], r["pr_s"].at[a], r["pr_r"].at[a], (tm, partner))

    def rs_copy(a, d):
        device, other = plane_peer(d)
        rows = pl.ds(pl.multiple_of(other * chunk, chunk), chunk)
        return remote(r["h"].at[a, rows, :], r["rs"].at[a, d - 1], r["rs_s"].at[a], r["rs_r"].at[a], device)

    def z_copy(a, d):
        return remote(r["zb"].at[a, z], r["zb"].at[a, z], r["z_s"].at[a], r["z_r"].at[a], z_peer(d))

    def ag_copy(a, d):
        device, _ = plane_peer(d)
        return remote(r["fin"].at[a, my_chunk, :], r["fin"].at[a, my_chunk, :], r["ag_s"].at[a], r["ag_r"].at[a], device)

    def join_copy(a):
        return remote(
            r["fin"].at[a, my_half, :], r["fin"].at[a, my_half, :], r["pg_s"].at[a], r["pg_r"].at[a], (tm, partner)
        )

    def drain(ref, sem):
        pltpu.make_async_copy(ref, ref, sem).wait()

    def reduce_pair(a):
        pair_copy(a).wait_recv()
        r["h"][a] = (r["g"][a, my_half, :].astype(F32) + r["pr"][a].astype(F32)).astype(BF16)
        loop(npl - 1, lambda i: rs_copy(a, i + 1).start())

    def reduce_middle(a):
        drain(r["rs"].at[a], r["rs_r"].at[a])
        total = r["h"][a, in_half, :].astype(F32)
        for d in range(npl - 1):
            total = total + r["rs"][a, d].astype(F32)
        r["zb"][a, z] = total.astype(BF16)
        loop(nz - 1, lambda i: z_copy(a, i + 1).start())

    def reduce_share(a):
        drain(r["zb"].at[a, 0 : nz - 1], r["z_r"].at[a])
        total = r["zb"][a, 0].astype(F32)
        for k in range(1, nz):
            total = total + r["zb"][a, k].astype(F32)
        r["fin"][a, my_chunk, :] = total.astype(BF16)
        loop(npl - 1, lambda i: ag_copy(a, i + 1).start())

    def reduce_join(a):
        drain(r["fin"].at[a, 0 : (npl - 1) * chunk, :], r["ag_r"].at[a])
        join_copy(a).start()

    def fin_copy(a):
        return pltpu.make_async_copy(r["fin"].at[a], fin_out.at[a], r["out_s"].at[a])

    def reduce_end(a):
        join_copy(a).wait_recv()
        fin_copy(a).start()

    def reduce_drain(a):
        pair_copy(a).wait_send()
        drain(r["rs"].at[a], r["rs_s"].at[a])
        drain(r["zb"].at[a, 0 : nz - 1], r["z_s"].at[a])
        drain(r["fin"].at[a, 0 : (npl - 1) * chunk, :], r["ag_s"].at[a])
        join_copy(a).wait_send()

    pair_copy(0).start()

    r["dkv"][...] = jnp.zeros_like(r["dkv"])

    def mg_arrival(d):
        rows = pl.ds(pl.multiple_of(lax.rem(tm + d, ntm) * part, part), part)
        return remote(r["mgs"].at[d], r["mg"].at[:, rows, :], r["mg_s"].at[d - 1], r["mg_r"].at[d - 1], (tm, sp))

    loop(ntm - 1, lambda i: mg_arrival(i + 1).wait_recv())

    reduce_pair(0)
    loop(ntm - 1, lambda i: mf_copy(i + 1).start())

    for i in range(4):
        f, j = i // 2, i % 2
        turned = nt(r["cv"][0], r["mg"][f, j * BLOCK : (j + 1) * BLOCK, :])
        share = jnp.broadcast_to(r["share"][i][:, None, :], (HEADS, HD, BLOCK)).reshape(D, BLOCK)
        turned = turned * share
        r["delta"][i] = head_sums(r["ot"][i] * turned.astype(BF16).astype(F32))
        grad = turned.T.astype(BF16)
        for h in range(HEADS):
            r["dos"][i, h * BLOCK : (h + 1) * BLOCK, :] = grad * r["hm"][h]

    def edge_copies(f):
        return [
            remote(r["dkvb"].at[f, 0:ROWS, :], r["er"].at[f, 1], r["ed_s"].at[f, 0], r["ed_r"].at[f, 0], (tm, left)),
            remote(
                r["dkvb"].at[f, 2 * ROWS :, :], r["er"].at[f, 0], r["ed_s"].at[f, 1], r["ed_r"].at[f, 1], (tm, right)
            ),
        ]

    def backward_block(i):
        f = lax.div(i, 2)
        j = lax.rem(i, 2)
        rows = key_rows(j)
        mine = pl.ds(pl.multiple_of(j * BLOCK, BLOCK), BLOCK)
        delta = r["delta"][i]
        outs = []
        for pair in range(HEADS // 2):
            cols = slice(pair * 2 * BLOCK, (pair + 1) * 2 * BLOCK)
            s = r["s"].at[pair % 2]
            s[...] = nt(r["kv"][f, rows, D:], r["dos"][i, cols, :])
            shift = jnp.concatenate([delta[2 * pair : 2 * pair + 1], delta[2 * pair + 1 : 2 * pair + 2]], axis=1)
            for e in range(SPAN):
                block = slice(e * BLOCK, (e + 1) * BLOCK)
                r["ds"][block, cols] = (r["probs"][i, block, cols].astype(F32) * (s[block, :] - shift)).astype(BF16)
            outs.append(diag(nn(r["kvt"][f, pair * 2 * HD : (pair + 1) * 2 * HD, rows], r["ds"][:, cols])))
        r["dq"][f, mine, :] = (jnp.concatenate(outs, axis=0) * SCALE).T.astype(BF16)
        r["dkv"][f, rows, 0:D] += nn(r["ds"][...], r["qs"][i]) * SCALE
        r["dkv"][f, rows, D:] += nn(r["probs"][i], r["dos"][i])

        @pl.when(i == 1)
        def _():
            r["dkvb"][0] = r["dkv"][0].astype(BF16)
            for item in edge_copies(0):
                item.start()
            reduce_middle(0)

        @pl.when(i == 2)
        def _():
            reduce_share(0)

    loop(4, backward_block)

    r["dkvb"][1] = r["dkv"][1].astype(BF16)
    inward = nn(r["act_t"][0], r["dkvb"][0]) + nn(r["act_t"][1], r["dkvb"][1])
    r["g"][1, 0:D, :] = inward.astype(BF16)
    inward = nn(r["act_t"][0, :, ROWS : 2 * ROWS], r["dq"][0]) + nn(r["act_t"][1, :, ROWS : 2 * ROWS], r["dq"][1])
    r["g"][1, D:, 0:D] = inward.astype(BF16)
    outward = nn(r["otb"][:, 0:ROWS], r["mg"][0]) + nn(r["otb"][:, ROWS:], r["mg"][1])
    r["g"][1, D:, D:] = outward.astype(BF16)
    pair_copy(1).start()
    reduce_pair(1)
    reduce_middle(1)
    for item in edge_copies(1):
        item.start()
    reduce_join(0)
    reduce_end(0)
    reduce_share(1)

    for f in range(FR):
        for item in edge_copies(f):
            item.wait_recv()
        pair_grad = r["dkv"][f, ROWS : 2 * ROWS, :] + r["er"][f, 0].astype(F32) + r["er"][f, 1].astype(F32)
        act_grad = nt(r["dq"][f], r["wv"][0, :, 0:D]) + nt(pair_grad.astype(BF16), r["wv"][0, :, D:])
        r["fg"][f] = (r["mg"][f].astype(F32) + norm_back(act_grad, r["nrm"][f], r["rinv"][f])).astype(BF16)
    field_copy = pltpu.make_async_copy(r["fg"], fg_out, r["out_s"].at[2])
    field_copy.start()

    def mf_arrival(d):
        rows = pl.ds(pl.multiple_of(lax.rem(tm + d, ntm) * part, part), part)
        return remote(r["mfs"].at[d], mixed_out.at[:, rows, :], r["mf_s"].at[d - 1], r["mf_r"].at[d - 1], (tm, sp))

    keep.wait()
    loop(ntm - 1, lambda i: mf_arrival(i + 1).wait_recv())
    loop(ntm - 1, lambda i: mf_copy(i + 1).wait_send())
    loop(ntm - 1, lambda i: mg_copy(i + 1).wait_send())
    loop(ntm - 1, lambda i: cot_copy(i + 1).wait_send())
    for f in range(FR):
        loop(ntm - 1, lambda i, f=f: ms_copy(f, i + 1).wait_send())
        for item in edge_copies(f):
            item.wait_send()
    for item in halos:
        item.wait_send()
    reduce_drain(0)

    reduce_join(1)
    reduce_end(1)
    reduce_drain(1)
    field_copy.wait()
    fin_copy(0).wait()
    fin_copy(1).wait()


def finish_kernel(factor, mixed, field, fin, mixed_out, field_out, project_out, combine_out):
    mixed_out[...] = mixed[...]
    field_out[...] = field[...]
    for layer in range(2):
        part = 1 - layer
        project_out[layer, :, D:] = fin[part, 0:D, :].astype(F32) * factor
        project_out[layer, :, 0:D] = fin[part, D:, 0:D].astype(F32) * factor
        combine_out[layer] = fin[part, D:, D:].astype(F32) * factor


def per_device(ntm, nsp, wave_field, cotangent, block_lists, project_weights, combine_weights):
    shapes = scratch_shapes(ntm, nsp)
    names = tuple(shapes)
    anywhere = pl.BlockSpec(memory_space=pl.ANY)
    vmem = pl.BlockSpec(memory_space=pltpu.VMEM)
    rows = jax.ShapeDtypeStruct((FR, ROWS, D), BF16)
    mixed, field, fin = pl.pallas_call(
        functools.partial(step_kernel, ntm, nsp, names),
        out_shape=(rows, rows, jax.ShapeDtypeStruct((2, 512, 512), BF16)),
        in_specs=[pl.BlockSpec(memory_space=pltpu.SMEM), anywhere, anywhere, anywhere, anywhere],
        out_specs=(anywhere, anywhere, anywhere),
        scratch_shapes=list(shapes.values()),
        compiler_params=pltpu.CompilerParams(
            collective_id=0, has_side_effects=True, vmem_limit_bytes=60 * 1024 * 1024
        ),
        name="cuboid_step",
    )(block_lists, wave_field, cotangent, project_weights, combine_weights)
    factor = 1.0 / math.sqrt(FR * ntm * ROWS * nsp)
    return pl.pallas_call(
        functools.partial(finish_kernel, factor),
        out_shape=(
            rows,
            rows,
            jax.ShapeDtypeStruct((2, D, 3 * D), F32),
            jax.ShapeDtypeStruct((2, D, D), F32),
        ),
        in_specs=[vmem] * 3,
        out_specs=(vmem,) * 4,
        name="finish",
    )(mixed, field, fin)


def solution(mesh):
    in_specs = (P("tm", "space", None), P("tm", "space", None), P("tm", "space", None), P(), P())
    out_specs = (P("tm", "space", None), P("tm", "space", None), P(), P())
    return jax.shard_map(
        functools.partial(per_device, mesh.shape["tm"], mesh.shape["space"]),
        mesh=mesh,
        in_specs=in_specs,
        out_specs=out_specs,
        check_vma=False,
    )
```

```python
import functools
import math

import jax
import jax.numpy as jnp
from jax import lax
from jax.experimental import pallas as pl
from jax.experimental.pallas import tpu as pltpu
from jax.sharding import PartitionSpec as P

HEADS = 8
BLOCK = 128
SPAN = 5
KEYS = SPAN * BLOCK
D = 256
HD = 32
ROWS = 256
FR = 2
GROUPS = 4
CORES = 4
EPS = 1e-05
NEG = -1e30
PADS = 80
LIMIT = 60 * 1024 * 1024
LANES = (512, 256, 128, 128)
SCALE = 1.0 / math.sqrt(HD)
SCALE2 = SCALE * math.log2(math.e)

MESH = pl.DeviceIdType.MESH
F32 = jnp.float32
BF16 = jnp.bfloat16


def nn(left, right):
    return jnp.dot(left, right, preferred_element_type=F32)


def nt(left, right):
    return lax.dot_general(left, right, (((1,), (1,)), ((), ())), preferred_element_type=F32)


def norm(rows):
    centered = rows - jnp.mean(rows, axis=-1, keepdims=True)
    inverse = lax.rsqrt(jnp.mean(centered * centered, axis=-1, keepdims=True) + EPS)
    return centered * inverse, inverse


def norm_back(upstream, normed, inverse):
    mean_grad = jnp.mean(upstream, axis=-1, keepdims=True)
    mean_cross = jnp.mean(upstream * normed, axis=-1, keepdims=True)
    return inverse * (upstream - mean_grad - normed * mean_cross)


def diag(pair):
    return jnp.concatenate([pair[0:HD, 0:BLOCK], pair[HD : 2 * HD, BLOCK : 2 * BLOCK]], axis=0)


def head_sums(prod):
    return jnp.sum(prod.reshape(HEADS, HD, BLOCK), axis=1)


def scratch_shapes(ntm, nsp):
    nz = nsp // CORES
    npl = ntm * 2
    part = ROWS // ntm
    chunk = 256 // npl
    dma = pltpu.SemaphoreType.DMA
    vm = pltpu.VMEM
    return dict(
        xe=vm((3, FR, ROWS, D), BF16),
        act=vm((3, FR, ROWS, D), BF16),
        act_t=vm((FR, D, 3 * ROWS), BF16),
        nrm=vm((FR, ROWS, D), F32),
        rinv=vm((FR, ROWS, 1), F32),
        wv=vm((2, D, 3 * D), BF16),
        cv=vm((2, D, D), BF16),
        wt=vm((2, 2 * D, D), BF16),
        hm=vm((HEADS, BLOCK, D), BF16),
        q=vm((FR, ROWS, D), BF16),
        kv=vm((FR, 3 * ROWS, 2 * D), BF16),
        kt=vm((FR, D, 3 * ROWS), BF16),
        vt=vm((FR, HEADS // 2, PADS, 3 * ROWS), BF16),
        qs=vm((4, HEADS * BLOCK, D), BF16),
        dos=vm((4, HEADS * BLOCK, D), BF16),
        share=vm((4, HEADS, BLOCK), F32),
        delta=vm((4, HEADS, BLOCK), F32),
        probs=vm((4, KEYS, HEADS * BLOCK), BF16),
        ds=vm((KEYS, HEADS * BLOCK), BF16),
        s=vm((4, KEYS, 2 * BLOCK), F32),
        ot=vm((4, D, BLOCK), F32),
        otb=vm((D, 4 * BLOCK), BF16),
        att=vm((FR, ROWS, D), BF16),
        ms=vm((FR, ROWS, D), BF16),
        hist=vm((ntm, FR, part, D), BF16),
        hcot=vm((ntm, FR, part, D), BF16),
        xt=vm((GROUPS, BLOCK, D), F32),
        ct=vm((GROUPS, BLOCK, D), F32),
        tb=vm((BLOCK, 2 * BLOCK), F32),
        tnrm=vm((GROUPS * BLOCK, D), F32),
        trinv=vm((GROUPS * BLOCK, 1), F32),
        tact=vm((GROUPS * BLOCK, D), BF16),
        tp=vm((GROUPS * BLOCK, 3 * D), BF16),
        tkvt=vm((2 * D, GROUPS * BLOCK), BF16),
        tdo=vm((GROUPS * BLOCK, D), BF16),
        tdot=vm((D, GROUPS * BLOCK), BF16),
        tot=vm((D, GROUPS * BLOCK), BF16),
        tatt=vm((GROUPS * BLOCK, D), BF16),
        tdp=vm((GROUPS * BLOCK, 3 * D), BF16),
        tqs=vm((GROUPS, HEADS * BLOCK, D), BF16),
        tdos=vm((GROUPS, HEADS * BLOCK, D), BF16),
        tprobs=vm((GROUPS, BLOCK, HEADS * BLOCK), BF16),
        tds=vm((GROUPS, BLOCK, HEADS * BLOCK), BF16),
        tmix=vm((GROUPS, BLOCK, D), F32),
        tmf=vm((GROUPS, BLOCK, D), F32),
        mfs=vm((ntm, FR, part, D), BF16),
        mgs=vm((ntm, FR, part, D), BF16),
        mg=vm((FR, ROWS, D), BF16),
        dq=vm((FR, ROWS, D), BF16),
        dkv=vm((FR, 3 * ROWS, 2 * D), F32),
        dkvb=vm((FR, 3 * ROWS, 2 * D), BF16),
        eg=vm((FR, 2, ROWS, D), BF16),
        er=vm((FR, 2, ROWS, D), BF16),
        fg=vm((FR, ROWS, D), BF16),
        fgw=vm((FR, ROWS, D), F32),
        **{
            name + str(a): vm(shape + (lanes,), BF16)
            for a, lanes in enumerate(LANES)
            for name, shape in (
                ("g", (512,)),
                ("pr", (256,)),
                ("h", (256,)),
                ("rs", (npl - 1, chunk)),
                ("zb", (nz, chunk)),
                ("fin", (512,)),
            )
        },
        ld_sem=dma((7,)),
        halo_s=dma((FR, 2)),
        halo_r=dma((FR, 2)),
        cot_s=dma((ntm - 1,)),
        cot_r=dma((ntm - 1,)),
        ms_s=dma((FR, ntm - 1)),
        ms_r=dma((FR, ntm - 1)),
        mf_s=dma((ntm - 1,)),
        mf_r=dma((ntm - 1,)),
        mg_s=dma((2, ntm - 1)),
        mg_r=dma((2, ntm - 1)),
        ed_s=dma((FR, 2)),
        ed_r=dma((FR, 2)),
        pr_s=dma((4,)),
        pr_r=dma((4,)),
        pg_s=dma((4,)),
        pg_r=dma((4,)),
        out_s=dma((5,)),
        rs_s=dma((4,)),
        rs_r=dma((4,)),
        z_s=dma((4,)),
        z_r=dma((4,)),
        ag_s=dma((4,)),
        ag_r=dma((4,)),
    )


def step_kernel(ntm, nsp, names, lists, x_hbm, cot_hbm, w_hbm, c_hbm, mixed_out, fg_out, fin0_out, fin1_out, fin2_out, fin3_out, *refs):
    r = dict(zip(names, refs))
    nz = nsp // CORES
    npl = ntm * 2
    part = ROWS // ntm
    chunk = 256 // npl
    frames = FR * ntm
    per = BLOCK // frames

    tm = lax.axis_index("tm")
    sp = lax.axis_index("space")
    z = lax.div(sp, CORES)
    quarter = lax.rem(sp, CORES)
    core = lax.rem(sp, 2)
    partner = sp + 1 - 2 * core
    left = lax.rem(sp + (nsp - 1), nsp)
    right = lax.rem(sp + 1, nsp)
    place = tm * 2 + lax.div(quarter, 2)

    def plane_peer(d):
        other = lax.rem(place + d, npl)
        return (lax.div(other, 2), z * CORES + lax.rem(other, 2) * 2 + core), other

    def z_peer(d):
        return (tm, lax.rem(z + d, nz) * CORES + quarter)

    def remote(src, dst, send, recv, device):
        return pltpu.make_async_remote_copy(
            src_ref=src, dst_ref=dst, send_sem=send, recv_sem=recv, device_id=device, device_id_type=MESH
        )

    def loop(count, body):
        def wrapped(i, carry):
            body(i)
            return carry

        lax.fori_loop(0, count, wrapped, 0)

    barrier = pltpu.get_barrier_semaphore()
    pl.semaphore_signal(barrier, inc=1, device_id=(tm, left), device_id_type=MESH)
    pl.semaphore_signal(barrier, inc=1, device_id=(tm, right), device_id_type=MESH)
    loop(npl - 1, lambda i: pl.semaphore_signal(barrier, inc=1, device_id=plane_peer(i + 1)[0], device_id_type=MESH))
    loop(nz - 1, lambda i: pl.semaphore_signal(barrier, inc=1, device_id=z_peer(i + 1), device_id_type=MESH))

    ld = r["ld_sem"]
    own = pl.ds(pl.multiple_of(tm * part, part), part)
    loads = [
        pltpu.make_async_copy(w_hbm.at[0], r["wv"].at[0], ld.at[0]),
        pltpu.make_async_copy(x_hbm.at[0], r["xe"].at[1, 0], ld.at[1]),
        pltpu.make_async_copy(c_hbm, r["cv"], ld.at[2]),
        pltpu.make_async_copy(w_hbm.at[1], r["wv"].at[1], ld.at[3]),
        pltpu.make_async_copy(cot_hbm.at[:, own, :], r["hcot"].at[0], ld.at[4]),
        pltpu.make_async_copy(x_hbm.at[1], r["xe"].at[1, 1], ld.at[6]),
    ]
    for item in loads:
        item.start()

    lane_head = lax.broadcasted_iota(jnp.int32, (BLOCK, D), 1) // HD
    for h in range(HEADS):
        r["hm"][h] = jnp.where(lane_head == h, 1.0, 0.0).astype(BF16)
    key_pos = lax.broadcasted_iota(jnp.int32, (BLOCK, 2 * BLOCK), 0) % per
    query_pos = lax.broadcasted_iota(jnp.int32, (BLOCK, 2 * BLOCK), 1) % per
    r["tb"][...] = jnp.where(key_pos == query_pos, 0.0, NEG)

    r["vt"][:, :, 2 * HD :, :] = jnp.ones((FR, HEADS // 2, PADS - 2 * HD, 3 * ROWS), BF16)

    loads[0].wait()
    r["wt"][0] = r["wv"][0, :, D:].astype(F32).T.astype(BF16)

    pl.semaphore_wait(barrier, 2 + (npl - 1) + (nz - 1))

    def halos(f):
        return [
            remote(x_hbm.at[f], r["xe"].at[2, f], r["halo_s"].at[f, 0], r["halo_r"].at[f, 0], (tm, left)),
            remote(x_hbm.at[f], r["xe"].at[0, f], r["halo_s"].at[f, 1], r["halo_r"].at[f, 1], (tm, right)),
        ]

    for f in range(FR):
        for item in halos(f):
            item.start()

    def cot_copy(d):
        to = lax.rem(tm + d, ntm)
        rows = pl.ds(pl.multiple_of(to * part, part), part)
        return remote(
            cot_hbm.at[:, rows, :], r["hcot"].at[d], r["cot_s"].at[d - 1], r["cot_r"].at[d - 1], (to, sp)
        )

    def project(slot, f):
        normed, inverse = norm(r["xe"][slot, f].astype(F32))
        rows = slice(slot * ROWS, (slot + 1) * ROWS)
        act = normed.astype(BF16)
        r["act"][slot, f] = act
        if slot == 1:
            r["nrm"][f] = normed
            r["rinv"][f] = inverse
            r["q"][f] = nn(act, r["wv"][0, :, 0:D]).astype(BF16)
        r["kv"][f, rows, :] = nn(act, r["wv"][0, :, D:]).astype(BF16)
        turned = nt(r["wt"][0], act).astype(BF16)
        r["kt"][f, :, rows] = turned[0:D]
        for pair in range(HEADS // 2):
            r["vt"][f, pair, 0 : 2 * HD, rows] = turned[D + pair * 2 * HD : D + (pair + 1) * 2 * HD]

    loads[1].wait()
    project(1, 0)
    loads[5].wait()
    project(1, 1)
    for f in range(FR):
        for j in range(2):
            for h in range(HEADS):
                r["qs"][2 * f + j, h * BLOCK : (h + 1) * BLOCK, :] = (
                    r["q"][f, j * BLOCK : (j + 1) * BLOCK, :] * r["hm"][h]
                )

    def key_rows(j):
        return pl.ds(pl.multiple_of(j * BLOCK, BLOCK), KEYS)

    def biases(f, j):
        out = []
        first = sp * 2 + j - 2
        for e in range(SPAN):
            count = jnp.int32(0)
            for k in range(4):
                count = count + jnp.where(lists[f, j, k] == first + e, 1, 0)
            out.append(
                jnp.where(
                    count == 0,
                    NEG,
                    jnp.where(count == 1, 0.0, jnp.where(count == 2, 1.0, jnp.where(count == 3, math.log2(3.0), 2.0))),
                ).astype(F32)
            )
        return out

    def forward_block(f, j):
        i = 2 * f + j
        rows = key_rows(j)
        bias = biases(f, j)
        outs = []

        def scores(pair):
            cols = slice(pair * 2 * BLOCK, (pair + 1) * 2 * BLOCK)
            r["s"][pair] = nt(r["kv"][f, rows, 0:D], r["qs"][i, cols, :])

        scores(0)
        for pair in range(HEADS // 2):
            cols = slice(pair * 2 * BLOCK, (pair + 1) * 2 * BLOCK)
            if pair + 1 < HEADS // 2:
                scores(pair + 1)
            s = r["s"].at[pair]
            top = None
            for e in range(SPAN):
                here = jnp.max(s[e * BLOCK : (e + 1) * BLOCK, :], axis=0, keepdims=True) * SCALE2 + bias[e]
                top = here if top is None else jnp.maximum(top, here)
            for e in range(SPAN):
                block = slice(e * BLOCK, (e + 1) * BLOCK)
                r["probs"][i, block, cols] = jnp.exp2(s[block, :] * SCALE2 + (bias[e] - top)).astype(BF16)
            both = nn(r["vt"][f, pair, :, rows], r["probs"][i, :, cols])
            share = 1.0 / both[2 * HD : 2 * HD + 1, :]
            r["share"][i, 2 * pair : 2 * pair + 1, :] = share[:, 0:BLOCK]
            r["share"][i, 2 * pair + 1 : 2 * pair + 2, :] = share[:, BLOCK:]
            outs.append(diag(both[0 : 2 * HD] * share))
        out = jnp.concatenate(outs, axis=0)
        r["ot"][i] = out
        r["otb"][:, pl.ds(pl.multiple_of(i * BLOCK, BLOCK), BLOCK)] = out.astype(BF16)
        r["att"][f, pl.ds(pl.multiple_of(j * BLOCK, BLOCK), BLOCK), :] = out.T.astype(BF16)

    def ms_copy(f, d):
        to = lax.rem(tm + d, ntm)
        rows = pl.ds(pl.multiple_of(to * part, part), part)
        return remote(
            r["ms"].at[f, rows, :], r["hist"].at[d, f], r["ms_s"].at[f, d - 1], r["ms_r"].at[f, d - 1], (to, sp)
        )

    loads[2].wait()
    half = ntm // 2

    def forward_frame(f):
        for item in halos(f):
            item.wait_recv()

        @pl.when(f == FR - 1)
        def _():
            loop(ntm - 1, lambda i: cot_copy(i + 1).start())

        project(2, f)
        project(0, f)

        def block(j):
            forward_block(f, j)
            rows = pl.ds(pl.multiple_of(j * BLOCK, BLOCK), BLOCK)
            mixed = r["xe"][1, f, rows, :].astype(F32) + nn(r["att"][f, rows, :], r["cv"][0])
            r["ms"][f, rows, :] = mixed.astype(BF16)

            def send(i):
                to = j * half + i

                @pl.when(to != tm)
                def _():
                    ms_copy(f, lax.rem(to - tm + ntm, ntm)).start()

            loop(half, send)

        loop(2, block)
        r["hist"][0, f] = r["ms"][f, own, :]

    loop(FR, forward_frame)

    for f in range(FR):
        for slot in range(3):
            r["act_t"][f, :, slot * ROWS : (slot + 1) * ROWS] = r["act"][slot, f].astype(F32).T.astype(BF16)
    loads[3].wait()
    r["wt"][1] = r["wv"][1, :, D:].astype(F32).T.astype(BF16)
    loads[4].wait()
    loop(ntm - 1, lambda i: cot_copy(i + 1).wait_recv())

    def regroup(src, dst):
        for d in range(ntm):
            for f in range(FR):
                frame = d * FR + f
                rows = src[d, f].astype(F32)
                for g in range(GROUPS):
                    dst[g, frame * per : (frame + 1) * per, :] = rows[g * per : (g + 1) * per]

    def ungroup(src, dst, side):
        for d in range(ntm):
            for f in range(FR):
                frame = d * FR + f
                dst[d, f, side * 2 * per : (side + 1) * 2 * per, :] = jnp.concatenate(
                    [src[g, frame * per : (frame + 1) * per, :] for g in (2 * side, 2 * side + 1)], axis=0
                ).astype(BF16)

    regroup(r["hcot"], r["ct"])
    for g in range(GROUPS):
        rows = slice(g * BLOCK, (g + 1) * BLOCK)
        cot = r["ct"][g].astype(BF16)
        grad = nt(cot, r["cv"][1]).astype(BF16)
        for h in range(HEADS):
            r["tdos"][g, h * BLOCK : (h + 1) * BLOCK, :] = grad * r["hm"][h]
        r["tdot"][:, rows] = nt(r["cv"][1], cot).astype(BF16)

    for f in range(FR):
        loop(ntm - 1, lambda i, f=f: ms_copy(f, i + 1).wait_recv())
        for d in range(ntm):
            frame = d * FR + f
            block = r["hist"][d, f].astype(F32)
            normed, inverse = norm(block)
            for g in range(GROUPS):
                to = slice(frame * per, (frame + 1) * per)
                at = slice(g * BLOCK + frame * per, g * BLOCK + (frame + 1) * per)
                mine = slice(g * per, (g + 1) * per)
                r["xt"][g, to, :] = block[mine]
                r["tnrm"][at, :] = normed[mine]
                r["trinv"][at, :] = inverse[mine]
    r["tact"][...] = r["tnrm"][...].astype(BF16)
    r["tp"][...] = nn(r["tact"][...], r["wv"][1]).astype(BF16)
    r["tkvt"][...] = nt(r["wt"][1], r["tact"][...]).astype(BF16)

    def time_scores(g):
        rows = slice(g * BLOCK, (g + 1) * BLOCK)
        query = r["tp"][rows, 0:D]
        for h in range(HEADS):
            r["tqs"][g, h * BLOCK : (h + 1) * BLOCK, :] = query * r["hm"][h]
        for pair in range(HEADS // 2):
            cols = slice(pair * 2 * BLOCK, (pair + 1) * 2 * BLOCK)
            scores = nt(r["tp"][rows, D : 2 * D], r["tqs"][g, cols, :]) * SCALE2 + r["tb"][...]
            grown = jnp.exp2(scores - jnp.max(scores, axis=0, keepdims=True))
            share = 1.0 / jnp.sum(grown, axis=0, keepdims=True)
            r["tprobs"][g, :, cols] = (grown * share).astype(BF16)

    def time_out(g):
        rows = slice(g * BLOCK, (g + 1) * BLOCK)
        outs = []
        for pair in range(HEADS // 2):
            cols = slice(pair * 2 * BLOCK, (pair + 1) * 2 * BLOCK)
            values = r["tkvt"][D + pair * 2 * HD : D + (pair + 1) * 2 * HD, rows]
            outs.append(diag(nn(values, r["tprobs"][g, :, cols])))
        out = jnp.concatenate(outs, axis=0)
        r["tot"][:, rows] = out.astype(BF16)
        r["tatt"][rows, :] = out.T.astype(BF16)
        delta = head_sums(out * r["tdot"][:, rows].astype(F32))
        for pair in range(HEADS // 2):
            cols = slice(pair * 2 * BLOCK, (pair + 1) * 2 * BLOCK)
            dprob = nt(r["tp"][rows, 2 * D :], r["tdos"][g, cols, :])
            shift = jnp.concatenate([delta[2 * pair : 2 * pair + 1], delta[2 * pair + 1 : 2 * pair + 2]], axis=1)
            r["tds"][g, :, cols] = (r["tprobs"][g, :, cols].astype(F32) * (dprob - shift)).astype(BF16)

    def time_grads(g):
        rows = slice(g * BLOCK, (g + 1) * BLOCK)
        outs = []
        for pair in range(HEADS // 2):
            cols = slice(pair * 2 * BLOCK, (pair + 1) * 2 * BLOCK)
            outs.append(diag(nn(r["tkvt"][pair * 2 * HD : (pair + 1) * 2 * HD, rows], r["tds"][g, :, cols])))
        r["tdp"][rows, 0:D] = (jnp.concatenate(outs, axis=0) * SCALE).T.astype(BF16)
        r["tdp"][rows, D : 2 * D] = (nn(r["tds"][g], r["tqs"][g]) * SCALE).astype(BF16)
        r["tdp"][rows, 2 * D : 3 * D] = nn(r["tprobs"][g], r["tdos"][g]).astype(BF16)

    for g in range(GROUPS):
        time_scores(g)
    for g in range(GROUPS):
        time_out(g)
    def mg_copy(d, side):
        from_rows = pl.ds(side * 2 * per, 2 * per)
        to_rows = pl.ds(pl.multiple_of(tm * part + side * 2 * per, 2 * per), 2 * per)
        return remote(
            r["mgs"].at[d, :, from_rows, :], r["mg"].at[:, to_rows, :], r["mg_s"].at[side, d - 1],
            r["mg_r"].at[side, d - 1], (lax.rem(tm + (ntm - d), ntm), sp),
        )

    def mf_copy(d):
        return remote(
            r["mfs"].at[d], mixed_out.at[:, own, :], r["mf_s"].at[d - 1], r["mf_r"].at[d - 1],
            (lax.rem(tm + (ntm - d), ntm), sp),
        )

    for side in range(2):
        for g in (2 * side, 2 * side + 1):
            time_grads(g)
        for g in (2 * side, 2 * side + 1):
            rows = slice(g * BLOCK, (g + 1) * BLOCK)
            act_grad = nt(r["tdp"][rows, :], r["wv"][1])
            r["tmix"][g] = r["ct"][g] + norm_back(act_grad, r["tnrm"][rows, :], r["trinv"][rows, :])
        ungroup(r["tmix"], r["mgs"], side)
        loop(ntm - 1, lambda i, side=side: mg_copy(i + 1, side).start())
    r["mg"][:, own, :] = r["mgs"][0]

    for g in range(GROUPS):
        rows = slice(g * BLOCK, (g + 1) * BLOCK)
        r["tmf"][g] = r["xt"][g] + nn(r["tatt"][rows, :], r["cv"][1])
    for side in range(2):
        ungroup(r["tmf"], r["mfs"], side)
    keep = pltpu.make_async_copy(r["mfs"].at[0], mixed_out.at[:, own, :], ld.at[5])
    keep.start()

    turned = r["tact"][...].astype(F32).T.astype(BF16)
    r["g0"][0:D, :] = nn(turned, r["tdp"][:, D:]).astype(BF16)
    r["g0"][D:, 0:D] = nn(turned, r["tdp"][:, 0:D]).astype(BF16)
    cots = r["ct"][...].reshape(GROUPS * BLOCK, D).astype(BF16)
    r["g0"][D:, D:] = nn(r["tot"][...], cots).astype(BF16)

    my_half = pl.ds(pl.multiple_of(core * 256, 256), 256)
    other_half = pl.ds(pl.multiple_of((1 - core) * 256, 256), 256)
    in_half = pl.ds(pl.multiple_of(place * chunk, chunk), chunk)
    my_chunk = pl.ds(pl.multiple_of(core * 256 + place * chunk, chunk), chunk)

    def pair_copy(a):
        return remote(r["g" + str(a)].at[other_half, :], r["pr" + str(a)], r["pr_s"].at[a], r["pr_r"].at[a], (tm, partner))

    def rs_copy(a, d):
        device, other = plane_peer(d)
        rows = pl.ds(pl.multiple_of(other * chunk, chunk), chunk)
        return remote(r["h" + str(a)].at[rows, :], r["rs" + str(a)].at[d - 1], r["rs_s"].at[a], r["rs_r"].at[a], device)

    def z_copy(a, d):
        return remote(r["zb" + str(a)].at[z], r["zb" + str(a)].at[z], r["z_s"].at[a], r["z_r"].at[a], z_peer(d))

    def ag_copy(a, d):
        device, _ = plane_peer(d)
        return remote(r["fin" + str(a)].at[my_chunk, :], r["fin" + str(a)].at[my_chunk, :], r["ag_s"].at[a], r["ag_r"].at[a], device)

    def join_copy(a):
        return remote(
            r["fin" + str(a)].at[my_half, :], r["fin" + str(a)].at[my_half, :], r["pg_s"].at[a], r["pg_r"].at[a], (tm, partner)
        )

    def drain(ref, sem):
        pltpu.make_async_copy(ref, ref, sem).wait()

    def reduce_pair(a):
        pair_copy(a).wait_recv()
        r["h" + str(a)][...] = (r["g" + str(a)][my_half, :].astype(F32) + r["pr" + str(a)][...].astype(F32)).astype(BF16)
        loop(npl - 1, lambda i: rs_copy(a, i + 1).start())

    def reduce_middle(a):
        drain(r["rs" + str(a)], r["rs_r"].at[a])
        total = r["h" + str(a)][in_half, :].astype(F32)
        for d in range(npl - 1):
            total = total + r["rs" + str(a)][d].astype(F32)
        r["zb" + str(a)][z] = total.astype(BF16)
        loop(nz - 1, lambda i: z_copy(a, i + 1).start())

    def reduce_share(a):
        drain(r["zb" + str(a)].at[0 : nz - 1], r["z_r"].at[a])
        total = r["zb" + str(a)][0].astype(F32)
        for k in range(1, nz):
            total = total + r["zb" + str(a)][k].astype(F32)
        r["fin" + str(a)][my_chunk, :] = total.astype(BF16)
        loop(npl - 1, lambda i: ag_copy(a, i + 1).start())

    def reduce_join(a):
        drain(r["fin" + str(a)].at[0 : (npl - 1) * chunk, :], r["ag_r"].at[a])
        join_copy(a).start()

    def fin_copy(a):
        return pltpu.make_async_copy(r["fin" + str(a)], (fin0_out, fin1_out, fin2_out, fin3_out)[a], r["out_s"].at[a])

    def reduce_end(a):
        join_copy(a).wait_recv()
        fin_copy(a).start()

    def reduce_drain(a):
        pair_copy(a).wait_send()
        drain(r["rs" + str(a)], r["rs_s"].at[a])
        drain(r["zb" + str(a)].at[0 : nz - 1], r["z_s"].at[a])
        drain(r["fin" + str(a)].at[0 : (npl - 1) * chunk, :], r["ag_s"].at[a])
        join_copy(a).wait_send()

    pair_copy(0).start()

    r["dkv"][...] = jnp.zeros_like(r["dkv"])

    def mg_arrival(d, side):
        rows = pl.ds(pl.multiple_of(lax.rem(tm + d, ntm) * part + side * 2 * per, 2 * per), 2 * per)
        from_rows = pl.ds(side * 2 * per, 2 * per)
        return remote(
            r["mgs"].at[d, :, from_rows, :], r["mg"].at[:, rows, :], r["mg_s"].at[side, d - 1],
            r["mg_r"].at[side, d - 1], (tm, sp),
        )

    for side in range(2):
        loop(ntm - 1, lambda i, side=side: mg_arrival(i + 1, side).wait_recv())

    outward = nn(r["otb"][:, 0:ROWS], r["mg"][0]) + nn(r["otb"][:, ROWS:], r["mg"][1])
    r["g2"][0:D, :] = outward[:, 0:BLOCK].astype(BF16)
    r["g2"][D:, :] = outward[:, BLOCK:].astype(BF16)
    pair_copy(2).start()
    reduce_pair(0)

    for i in range(4):
        f, j = i // 2, i % 2
        turned = nt(r["cv"][0], r["mg"][f, j * BLOCK : (j + 1) * BLOCK, :])
        share = jnp.broadcast_to(r["share"][i][:, None, :], (HEADS, HD, BLOCK)).reshape(D, BLOCK)
        turned = turned * share
        r["delta"][i] = head_sums(r["ot"][i] * turned.astype(BF16).astype(F32))
        grad = turned.T.astype(BF16)
        for h in range(HEADS):
            r["dos"][i, h * BLOCK : (h + 1) * BLOCK, :] = grad * r["hm"][h]

    def edge_copy(f, side):
        return remote(
            r["eg"].at[f, side], r["er"].at[f, 1 - side], r["ed_s"].at[f, side], r["ed_r"].at[f, side],
            (tm, right if side else left),
        )

    def edge_send(f):
        for side in range(2):
            rows = slice(2 * ROWS * side, 2 * ROWS * side + ROWS)
            r["eg"][f, side] = nt(r["dkvb"][f, rows, :], r["wv"][0, :, D:]).astype(BF16)
            edge_copy(f, side).start()

    def backward_block(i):
        f = lax.div(i, 2)
        j = lax.rem(i, 2)
        rows = key_rows(j)
        mine = pl.ds(pl.multiple_of(j * BLOCK, BLOCK), BLOCK)
        delta = r["delta"][i]
        outs = []

        def grads(pair):
            cols = slice(pair * 2 * BLOCK, (pair + 1) * 2 * BLOCK)
            r["s"][pair] = nt(r["kv"][f, rows, D:], r["dos"][i, cols, :])

        grads(0)
        for pair in range(HEADS // 2):
            cols = slice(pair * 2 * BLOCK, (pair + 1) * 2 * BLOCK)
            s = r["s"].at[pair]
            if pair + 1 < HEADS // 2:
                grads(pair + 1)
            shift = jnp.concatenate([delta[2 * pair : 2 * pair + 1], delta[2 * pair + 1 : 2 * pair + 2]], axis=1)
            for e in range(SPAN):
                block = slice(e * BLOCK, (e + 1) * BLOCK)
                r["ds"][block, cols] = (r["probs"][i, block, cols].astype(F32) * (s[block, :] - shift)).astype(BF16)
            outs.append(diag(nn(r["kt"][f, pair * 2 * HD : (pair + 1) * 2 * HD, rows], r["ds"][:, cols])))
        r["dq"][f, mine, :] = (jnp.concatenate(outs, axis=0) * SCALE).T.astype(BF16)
        r["dkv"][f, rows, 0:D] += nn(r["ds"][...], r["qs"][i]) * SCALE
        r["dkv"][f, rows, D:] += nn(r["probs"][i], r["dos"][i])

        @pl.when(i == 0)
        def _():
            reduce_pair(2)

        @pl.when(i == 1)
        def _():
            r["dkvb"][0] = r["dkv"][0].astype(BF16)
            edge_send(0)
            loop(ntm - 1, lambda k: mf_copy(k + 1).start())

        @pl.when(i == 2)
        def _():
            reduce_middle(0)
            reduce_middle(2)

    loop(4, backward_block)

    inward = nn(r["act_t"][0, :, ROWS : 2 * ROWS], r["dq"][0]) + nn(r["act_t"][1, :, ROWS : 2 * ROWS], r["dq"][1])
    r["g3"][0:D, :] = inward[:, 0:BLOCK].astype(BF16)
    r["g3"][D:, :] = inward[:, BLOCK:].astype(BF16)
    pair_copy(3).start()
    r["dkvb"][1] = r["dkv"][1].astype(BF16)
    inward = nn(r["act_t"][0], r["dkvb"][0]) + nn(r["act_t"][1], r["dkvb"][1])
    r["g1"][0:D, :] = inward[:, 0:D].astype(BF16)
    r["g1"][D:, :] = inward[:, D:].astype(BF16)
    pair_copy(1).start()
    reduce_pair(3)
    reduce_pair(1)
    edge_send(1)
    for f in range(FR):
        r["fgw"][f] = nt(r["dq"][f], r["wv"][0, :, 0:D]) + nt(r["dkvb"][f, ROWS : 2 * ROWS, :], r["wv"][0, :, D:])
    reduce_share(0)
    reduce_share(2)
    reduce_middle(3)
    reduce_middle(1)
    reduce_share(3)
    reduce_share(1)
    for a in (0, 2):
        reduce_join(a)

    for f in range(FR):
        for side in range(2):
            edge_copy(f, side).wait_recv()
        act_grad = r["fgw"][f] + r["er"][f, 0].astype(F32) + r["er"][f, 1].astype(F32)
        r["fg"][f] = (r["mg"][f].astype(F32) + norm_back(act_grad, r["nrm"][f], r["rinv"][f])).astype(BF16)
    field_copy = pltpu.make_async_copy(r["fg"], fg_out, r["out_s"].at[4])
    field_copy.start()

    def mf_arrival(d):
        rows = pl.ds(pl.multiple_of(lax.rem(tm + d, ntm) * part, part), part)
        return remote(r["mfs"].at[d], mixed_out.at[:, rows, :], r["mf_s"].at[d - 1], r["mf_r"].at[d - 1], (tm, sp))

    keep.wait()
    loop(ntm - 1, lambda i: mf_arrival(i + 1).wait_recv())
    loop(ntm - 1, lambda i: mf_copy(i + 1).wait_send())
    for side in range(2):
        loop(ntm - 1, lambda i, side=side: mg_copy(i + 1, side).wait_send())
    loop(ntm - 1, lambda i: cot_copy(i + 1).wait_send())
    for f in range(FR):
        loop(ntm - 1, lambda i, f=f: ms_copy(f, i + 1).wait_send())
        for side in range(2):
            edge_copy(f, side).wait_send()
        for item in halos(f):
            item.wait_send()
    reduce_drain(0)
    reduce_drain(2)

    for a in (0, 2):
        reduce_end(a)
    reduce_join(3)
    reduce_join(1)
    reduce_end(3)
    reduce_end(1)
    reduce_drain(3)
    reduce_drain(1)
    field_copy.wait()
    for a in range(4):
        fin_copy(a).wait()


def finish_kernel(factor, mixed, field, fin0, fin1, fin2, fin3, mixed_out, field_out, project_out, combine_out):
    mixed_out[...] = mixed[...]
    field_out[...] = field[...]
    project_out[1, :, D:] = fin0[0:D, :].astype(F32) * factor
    project_out[1, :, 0:D] = fin0[D:, 0:D].astype(F32) * factor
    combine_out[1] = fin0[D:, D:].astype(F32) * factor
    project_out[0, :, 0:BLOCK] = fin3[0:D, :].astype(F32) * factor
    project_out[0, :, BLOCK:D] = fin3[D:, :].astype(F32) * factor
    project_out[0, :, D : 2 * D] = fin1[0:D, :].astype(F32) * factor
    project_out[0, :, 2 * D :] = fin1[D:, :].astype(F32) * factor
    combine_out[0, :, 0:BLOCK] = fin2[0:D, :].astype(F32) * factor
    combine_out[0, :, BLOCK:] = fin2[D:, :].astype(F32) * factor


def per_device(ntm, nsp, wave_field, cotangent, block_lists, project_weights, combine_weights):
    shapes = scratch_shapes(ntm, nsp)
    names = tuple(shapes)
    anywhere = pl.BlockSpec(memory_space=pl.ANY)
    vmem = pl.BlockSpec(memory_space=pltpu.VMEM)
    rows = jax.ShapeDtypeStruct((FR, ROWS, D), BF16)
    results = pl.pallas_call(
        functools.partial(step_kernel, ntm, nsp, names),
        out_shape=(rows, rows) + tuple(jax.ShapeDtypeStruct((512, lanes), BF16) for lanes in LANES),
        in_specs=[pl.BlockSpec(memory_space=pltpu.SMEM), anywhere, anywhere, anywhere, anywhere],
        out_specs=(anywhere,) * 6,
        scratch_shapes=list(shapes.values()),
        compiler_params=pltpu.CompilerParams(
            collective_id=0, has_side_effects=True, vmem_limit_bytes=LIMIT
        ),
        name="cuboid_step",
    )(block_lists, wave_field, cotangent, project_weights, combine_weights)
    factor = 1.0 / math.sqrt(FR * ntm * ROWS * nsp)
    return pl.pallas_call(
        functools.partial(finish_kernel, factor),
        out_shape=(
            rows,
            rows,
            jax.ShapeDtypeStruct((2, D, 3 * D), F32),
            jax.ShapeDtypeStruct((2, D, D), F32),
        ),
        in_specs=[vmem] * 6,
        out_specs=(vmem,) * 4,
        name="finish",
    )(*results)


def solution(mesh):
    in_specs = (P("tm", "space", None), P("tm", "space", None), P("tm", "space", None), P(), P())
    out_specs = (P("tm", "space", None), P("tm", "space", None), P(), P())
    return jax.shard_map(
        functools.partial(per_device, mesh.shape["tm"], mesh.shape["space"]),
        mesh=mesh,
        in_specs=in_specs,
        out_specs=out_specs,
        check_vma=False,
    )
```

```python
import functools
import math

import jax
import jax.numpy as jnp
from jax import lax
from jax.experimental import pallas as pl
from jax.experimental.pallas import tpu as pltpu
from jax.sharding import PartitionSpec as P

HEADS = 8
BLOCK = 128
SPAN = 5
KEYS = SPAN * BLOCK
D = 256
HD = 32
ROWS = 256
FR = 2
GROUPS = 4
CORES = 4
EPS = 1e-05
NEG = -1e30
PADS = 80
LIMIT = 60 * 1024 * 1024
LANES = (512, 256, 128, 128)
SCALE = 1.0 / math.sqrt(HD)
SCALE2 = SCALE * math.log2(math.e)

MESH = pl.DeviceIdType.MESH
F32 = jnp.float32
BF16 = jnp.bfloat16


def nn(left, right):
    return jnp.dot(left, right, preferred_element_type=F32)


def nt(left, right):
    return lax.dot_general(left, right, (((1,), (1,)), ((), ())), preferred_element_type=F32)


def norm(rows):
    centered = rows - jnp.mean(rows, axis=-1, keepdims=True)
    inverse = lax.rsqrt(jnp.mean(centered * centered, axis=-1, keepdims=True) + EPS)
    return centered * inverse, inverse


def norm_back(upstream, normed, inverse):
    mean_grad = jnp.mean(upstream, axis=-1, keepdims=True)
    mean_cross = jnp.mean(upstream * normed, axis=-1, keepdims=True)
    return inverse * (upstream - mean_grad - normed * mean_cross)


def diag(pair):
    return jnp.concatenate([pair[0:HD, 0:BLOCK], pair[HD : 2 * HD, BLOCK : 2 * BLOCK]], axis=0)


def head_sums(prod):
    return jnp.sum(prod.reshape(HEADS, HD, BLOCK), axis=1)


def scratch_shapes(ntm, nsp):
    nz = nsp // CORES
    npl = ntm * 2
    part = ROWS // ntm
    chunk = 256 // npl
    dma = pltpu.SemaphoreType.DMA
    vm = pltpu.VMEM
    return dict(
        xe=vm((3, FR, ROWS, D), BF16),
        act=vm((3, FR, ROWS, D), BF16),
        act_t=vm((FR, D, 3 * ROWS), BF16),
        nrm=vm((FR, ROWS, D), F32),
        rinv=vm((FR, ROWS, 1), F32),
        wv=vm((2, D, 3 * D), BF16),
        cv=vm((2, D, D), BF16),
        wt=vm((2, 2 * D, D), BF16),
        hm=vm((HEADS, BLOCK, D), BF16),
        q=vm((FR, ROWS, D), BF16),
        kv=vm((FR, 3 * ROWS, 2 * D), BF16),
        kt=vm((FR, D, 3 * ROWS), BF16),
        vt=vm((FR, HEADS // 2, PADS, 3 * ROWS), BF16),
        qs=vm((4, HEADS * BLOCK, D), BF16),
        dos=vm((4, HEADS * BLOCK, D), BF16),
        share=vm((4, HEADS, BLOCK), F32),
        delta=vm((4, HEADS, BLOCK), F32),
        probs=vm((4, KEYS, HEADS * BLOCK), BF16),
        ds=vm((KEYS, HEADS * BLOCK), BF16),
        s=vm((4, KEYS, 2 * BLOCK), F32),
        ot=vm((4, D, BLOCK), F32),
        otb=vm((D, 4 * BLOCK), BF16),
        att=vm((FR, ROWS, D), BF16),
        ms=vm((FR, ROWS, D), BF16),
        hist=vm((ntm, FR, part, D), BF16),
        hcot=vm((ntm, FR, part, D), BF16),
        xt=vm((GROUPS, BLOCK, D), F32),
        ct=vm((GROUPS, BLOCK, D), F32),
        tb=vm((BLOCK, 2 * BLOCK), F32),
        tnrm=vm((GROUPS * BLOCK, D), F32),
        trinv=vm((GROUPS * BLOCK, 1), F32),
        tact=vm((GROUPS * BLOCK, D), BF16),
        tp=vm((GROUPS * BLOCK, 3 * D), BF16),
        tkvt=vm((2 * D, GROUPS * BLOCK), BF16),
        tdo=vm((GROUPS * BLOCK, D), BF16),
        tdot=vm((D, GROUPS * BLOCK), BF16),
        tot=vm((D, GROUPS * BLOCK), BF16),
        tatt=vm((GROUPS * BLOCK, D), BF16),
        tdp=vm((GROUPS * BLOCK, 3 * D), BF16),
        tqs=vm((GROUPS, HEADS * BLOCK, D), BF16),
        tdos=vm((GROUPS, HEADS * BLOCK, D), BF16),
        tprobs=vm((GROUPS, BLOCK, HEADS * BLOCK), BF16),
        tds=vm((GROUPS, BLOCK, HEADS * BLOCK), BF16),
        tmix=vm((GROUPS, BLOCK, D), F32),
        tmf=vm((GROUPS, BLOCK, D), F32),
        mfs=vm((ntm, FR, part, D), BF16),
        mgs=vm((ntm, FR, part, D), BF16),
        mg=vm((FR, ROWS, D), BF16),
        dq=vm((FR, ROWS, D), BF16),
        dkv=vm((FR, 3 * ROWS, 2 * D), F32),
        dkvb=vm((FR, 3 * ROWS, 2 * D), BF16),
        eg=vm((FR, 2, ROWS, D), BF16),
        er=vm((FR, 2, ROWS, D), BF16),
        fg=vm((FR, ROWS, D), BF16),
        fgw=vm((FR, ROWS, D), F32),
        **{
            name + str(a): vm(shape + (lanes,), BF16)
            for a, lanes in enumerate(LANES)
            for name, shape in (
                ("g", (512,)),
                ("pr", (256,)),
                ("h", (256,)),
                ("rs", (npl - 1, chunk)),
                ("zb", (nz, chunk)),
                ("fin", (chunk,)),
            )
        },
        lists=pltpu.SMEM((FR, 2, 4), jnp.int32),
        ld_sem=dma((8,)),
        own_sem=dma((2, 2)),
        halo_s=dma((FR, 2)),
        halo_r=dma((FR, 2)),
        cot_s=dma((2, ntm - 1)),
        cot_r=dma((2, ntm - 1)),
        ms_s=dma((2, FR, ntm - 1)),
        ms_r=dma((2, FR, ntm - 1)),
        mf_s=dma((2, ntm - 1)),
        mf_r=dma((2, ntm - 1)),
        mg_s=dma((2, ntm - 1)),
        mg_r=dma((2, ntm - 1)),
        ed_s=dma((FR, 2)),
        ed_r=dma((FR, 2)),
        pr_s=dma((4,)),
        pr_r=dma((4,)),
        pg_s=dma((4,)),
        pg_r=dma((4,)),
        out_s=dma((5,)),
        rs_s=dma((4,)),
        rs_r=dma((4,)),
        z_s=dma((4,)),
        z_r=dma((4,)),
        ag_s=dma((4,)),
        ag_r=dma((4,)),
    )


def step_kernel(ntm, nsp, names, lists_hbm, x_hbm, cot_hbm, w_hbm, c_hbm, mixed_out, fg_out, fin0_out, fin1_out, fin2_out, fin3_out, *refs):
    r = dict(zip(names, refs))
    nz = nsp // CORES
    npl = ntm * 2
    hp = ROWS // ntm // 2
    chunk = 256 // npl
    frames = FR * ntm
    per = BLOCK // frames

    tm = lax.axis_index("tm")
    sp = lax.axis_index("space")
    z = lax.div(sp, CORES)
    quarter = lax.rem(sp, CORES)
    core = lax.rem(sp, 2)
    partner = sp + 1 - 2 * core
    left = lax.rem(sp + (nsp - 1), nsp)
    right = lax.rem(sp + 1, nsp)
    place = tm * 2 + lax.div(quarter, 2)

    def plane_peer(d):
        other = lax.rem(place + d, npl)
        return (lax.div(other, 2), z * CORES + lax.rem(other, 2) * 2 + core), other

    def z_peer(d):
        return (tm, lax.rem(z + d, nz) * CORES + quarter)

    def remote(src, dst, send, recv, device):
        return pltpu.make_async_remote_copy(
            src_ref=src, dst_ref=dst, send_sem=send, recv_sem=recv, device_id=device, device_id_type=MESH
        )

    def loop(count, body):
        def wrapped(i, carry):
            body(i)
            return carry

        lax.fori_loop(0, count, wrapped, 0)

    barrier = pltpu.get_barrier_semaphore()
    pl.semaphore_signal(barrier, inc=1, device_id=(tm, left), device_id_type=MESH)
    pl.semaphore_signal(barrier, inc=1, device_id=(tm, right), device_id_type=MESH)
    loop(npl - 1, lambda i: pl.semaphore_signal(barrier, inc=1, device_id=plane_peer(i + 1)[0], device_id_type=MESH))
    loop(nz - 1, lambda i: pl.semaphore_signal(barrier, inc=1, device_id=z_peer(i + 1), device_id_type=MESH))

    ld = r["ld_sem"]

    def side_rows(device, side):
        return pl.ds(pl.multiple_of(side * BLOCK + device * hp, hp), hp)

    def in_part(side):
        return pl.ds(side * hp, hp)

    loads = [
        pltpu.make_async_copy(w_hbm.at[0], r["wv"].at[0], ld.at[0]),
        pltpu.make_async_copy(x_hbm.at[0], r["xe"].at[1, 0], ld.at[1]),
        pltpu.make_async_copy(c_hbm, r["cv"], ld.at[2]),
        pltpu.make_async_copy(w_hbm.at[1], r["wv"].at[1], ld.at[3]),
        pltpu.make_async_copy(
            cot_hbm.at[:, side_rows(tm, 0), :], r["hcot"].at[0, :, in_part(0), :], r["own_sem"].at[0, 0]
        ),
        pltpu.make_async_copy(x_hbm.at[1], r["xe"].at[1, 1], ld.at[6]),
        pltpu.make_async_copy(lists_hbm, r["lists"], ld.at[7]),
        pltpu.make_async_copy(
            cot_hbm.at[:, side_rows(tm, 1), :], r["hcot"].at[0, :, in_part(1), :], r["own_sem"].at[0, 1]
        ),
    ]
    for item in loads:
        item.start()

    lane_head = lax.broadcasted_iota(jnp.int32, (BLOCK, D), 1) // HD
    for h in range(HEADS):
        r["hm"][h] = jnp.where(lane_head == h, 1.0, 0.0).astype(BF16)
    key_pos = lax.broadcasted_iota(jnp.int32, (BLOCK, 2 * BLOCK), 0) % per
    query_pos = lax.broadcasted_iota(jnp.int32, (BLOCK, 2 * BLOCK), 1) % per
    r["tb"][...] = jnp.where(key_pos == query_pos, 0.0, NEG)

    r["vt"][:, :, 2 * HD :, :] = jnp.ones((FR, HEADS // 2, PADS - 2 * HD, 3 * ROWS), BF16)

    loads[0].wait()
    r["wt"][0] = r["wv"][0, :, D:].astype(F32).T.astype(BF16)

    pl.semaphore_wait(barrier, 2 + (npl - 1) + (nz - 1))

    def halos(f):
        return [
            remote(x_hbm.at[f], r["xe"].at[2, f], r["halo_s"].at[f, 0], r["halo_r"].at[f, 0], (tm, left)),
            remote(x_hbm.at[f], r["xe"].at[0, f], r["halo_s"].at[f, 1], r["halo_r"].at[f, 1], (tm, right)),
        ]

    for f in range(FR):
        for item in halos(f):
            item.start()

    def cot_copy(d, side):
        to = lax.rem(tm + d, ntm)
        return remote(
            cot_hbm.at[:, side_rows(to, side), :], r["hcot"].at[d, :, in_part(side), :], r["cot_s"].at[side, d - 1],
            r["cot_r"].at[side, d - 1], (to, sp),
        )

    def project(slot, f):
        normed, inverse = norm(r["xe"][slot, f].astype(F32))
        rows = slice(slot * ROWS, (slot + 1) * ROWS)
        act = normed.astype(BF16)
        r["act"][slot, f] = act
        if slot == 1:
            r["nrm"][f] = normed
            r["rinv"][f] = inverse
            r["q"][f] = nn(act, r["wv"][0, :, 0:D]).astype(BF16)
        r["kv"][f, rows, :] = nn(act, r["wv"][0, :, D:]).astype(BF16)
        turned = nt(r["wt"][0], act).astype(BF16)
        r["kt"][f, :, rows] = turned[0:D]
        for pair in range(HEADS // 2):
            r["vt"][f, pair, 0 : 2 * HD, rows] = turned[D + pair * 2 * HD : D + (pair + 1) * 2 * HD]

    loads[1].wait()
    project(1, 0)
    loads[5].wait()
    project(1, 1)
    for f in range(FR):
        for j in range(2):
            for h in range(HEADS):
                r["qs"][2 * f + j, h * BLOCK : (h + 1) * BLOCK, :] = (
                    r["q"][f, j * BLOCK : (j + 1) * BLOCK, :] * r["hm"][h]
                )

    def key_rows(j):
        return pl.ds(pl.multiple_of(j * BLOCK, BLOCK), KEYS)

    def biases(f, j):
        out = []
        first = sp * 2 + j - 2
        for e in range(SPAN):
            count = jnp.int32(0)
            for k in range(4):
                count = count + jnp.where(r["lists"][f, j, k] == first + e, 1, 0)
            out.append(
                jnp.where(
                    count == 0,
                    NEG,
                    jnp.where(count == 1, 0.0, jnp.where(count == 2, 1.0, jnp.where(count == 3, math.log2(3.0), 2.0))),
                ).astype(F32)
            )
        return out

    def forward_block(f, j):
        i = 2 * f + j
        rows = key_rows(j)
        bias = biases(f, j)
        outs = []

        def scores(pair):
            cols = slice(pair * 2 * BLOCK, (pair + 1) * 2 * BLOCK)
            r["s"][pair] = nt(r["kv"][f, rows, 0:D], r["qs"][i, cols, :])

        scores(0)
        for pair in range(HEADS // 2):
            cols = slice(pair * 2 * BLOCK, (pair + 1) * 2 * BLOCK)
            if pair + 1 < HEADS // 2:
                scores(pair + 1)
            s = r["s"].at[pair]
            top = None
            for e in range(SPAN):
                here = jnp.max(s[e * BLOCK : (e + 1) * BLOCK, :], axis=0, keepdims=True) * SCALE2 + bias[e]
                top = here if top is None else jnp.maximum(top, here)
            for e in range(SPAN):
                block = slice(e * BLOCK, (e + 1) * BLOCK)
                r["probs"][i, block, cols] = jnp.exp2(s[block, :] * SCALE2 + (bias[e] - top)).astype(BF16)
            both = nn(r["vt"][f, pair, :, rows], r["probs"][i, :, cols])
            share = 1.0 / both[2 * HD : 2 * HD + 1, :]
            r["share"][i, 2 * pair : 2 * pair + 1, :] = share[:, 0:BLOCK]
            r["share"][i, 2 * pair + 1 : 2 * pair + 2, :] = share[:, BLOCK:]
            outs.append(diag(both[0 : 2 * HD] * share))
        out = jnp.concatenate(outs, axis=0)
        r["ot"][i] = out
        r["otb"][:, pl.ds(pl.multiple_of(i * BLOCK, BLOCK), BLOCK)] = out.astype(BF16)
        r["att"][f, pl.ds(pl.multiple_of(j * BLOCK, BLOCK), BLOCK), :] = out.T.astype(BF16)

    def ms_copy(f, side, d):
        to = lax.rem(tm + d, ntm)
        return remote(
            r["ms"].at[f, side_rows(to, side), :],
            r["hist"].at[d, f, pl.ds(pl.multiple_of(side * hp, hp), hp), :],
            r["ms_s"].at[side, f, d - 1],
            r["ms_r"].at[side, f, d - 1],
            (to, sp),
        )

    loads[3].wait()
    r["wt"][1] = r["wv"][1, :, D:].astype(F32).T.astype(BF16)
    loads[2].wait()
    loads[6].wait()

    def forward(o):
        f = lax.rem(o, FR)
        j = lax.div(o, FR)

        @pl.when(j == 0)
        def _():
            for item in halos(f):
                item.wait_recv()

        @pl.when(o == FR - 1)
        def _():
            for side in range(2):
                loop(ntm - 1, lambda i, side=side: cot_copy(i + 1, side).start())

        @pl.when(j == 0)
        def _():
            project(2, f)
            project(0, f)

        forward_block(f, j)
        rows = pl.ds(pl.multiple_of(j * BLOCK, BLOCK), BLOCK)
        mixed = r["xe"][1, f, rows, :].astype(F32) + nn(r["att"][f, rows, :], r["cv"][0])
        r["ms"][f, rows, :] = mixed.astype(BF16)
        loop(ntm - 1, lambda i: ms_copy(f, j, i + 1).start())
        r["hist"][0, f, pl.ds(pl.multiple_of(j * hp, hp), hp), :] = r["ms"][f, side_rows(tm, j), :]

    loop(2 * FR, forward)

    def ungroup(src, dst, side):
        for d in range(ntm):
            for f in range(FR):
                frame = d * FR + f
                dst[d, f, side * 2 * per : (side + 1) * 2 * per, :] = jnp.concatenate(
                    [src[g, frame * per : (frame + 1) * per, :] for g in (2 * side, 2 * side + 1)], axis=0
                ).astype(BF16)

    def time_inputs(side):
        mine = slice(side * hp, (side + 1) * hp)
        groups = (2 * side, 2 * side + 1)
        loads[(4, 7)[side]].wait()
        loop(ntm - 1, lambda i: cot_copy(i + 1, side).wait_recv())
        for d in range(ntm):
            for f in range(FR):
                frame = d * FR + f
                block = r["hcot"][d, f, mine, :].astype(F32)
                for k, g in enumerate(groups):
                    r["ct"][g, frame * per : (frame + 1) * per, :] = block[k * per : (k + 1) * per]
        for g in groups:
            rows = slice(g * BLOCK, (g + 1) * BLOCK)
            cot = r["ct"][g].astype(BF16)
            grad = nt(cot, r["cv"][1]).astype(BF16)
            for h in range(HEADS):
                r["tdos"][g, h * BLOCK : (h + 1) * BLOCK, :] = grad * r["hm"][h]
            r["tdot"][:, rows] = nt(r["cv"][1], cot).astype(BF16)
        for f in range(FR):
            loop(ntm - 1, lambda i, f=f: ms_copy(f, side, i + 1).wait_recv())
            for d in range(ntm):
                frame = d * FR + f
                block = r["hist"][d, f, mine, :].astype(F32)
                normed, inverse = norm(block)
                for k, g in enumerate(groups):
                    to = slice(frame * per, (frame + 1) * per)
                    at = slice(g * BLOCK + frame * per, g * BLOCK + (frame + 1) * per)
                    piece = slice(k * per, (k + 1) * per)
                    r["xt"][g, to, :] = block[piece]
                    r["tnrm"][at, :] = normed[piece]
                    r["trinv"][at, :] = inverse[piece]
        rows = slice(side * 2 * BLOCK, (side + 1) * 2 * BLOCK)
        r["tact"][rows, :] = r["tnrm"][rows, :].astype(BF16)
        r["tp"][rows, :] = nn(r["tact"][rows, :], r["wv"][1]).astype(BF16)
        r["tkvt"][:, rows] = nt(r["wt"][1], r["tact"][rows, :]).astype(BF16)

    def time_scores(g):
        rows = slice(g * BLOCK, (g + 1) * BLOCK)
        query = r["tp"][rows, 0:D]
        for h in range(HEADS):
            r["tqs"][g, h * BLOCK : (h + 1) * BLOCK, :] = query * r["hm"][h]
        for pair in range(HEADS // 2):
            cols = slice(pair * 2 * BLOCK, (pair + 1) * 2 * BLOCK)
            scores = nt(r["tp"][rows, D : 2 * D], r["tqs"][g, cols, :]) * SCALE2 + r["tb"][...]
            grown = jnp.exp2(scores - jnp.max(scores, axis=0, keepdims=True))
            share = 1.0 / jnp.sum(grown, axis=0, keepdims=True)
            r["tprobs"][g, :, cols] = (grown * share).astype(BF16)

    def time_out(g):
        rows = slice(g * BLOCK, (g + 1) * BLOCK)
        outs = []
        for pair in range(HEADS // 2):
            cols = slice(pair * 2 * BLOCK, (pair + 1) * 2 * BLOCK)
            values = r["tkvt"][D + pair * 2 * HD : D + (pair + 1) * 2 * HD, rows]
            outs.append(diag(nn(values, r["tprobs"][g, :, cols])))
        out = jnp.concatenate(outs, axis=0)
        r["tot"][:, rows] = out.astype(BF16)
        r["tatt"][rows, :] = out.T.astype(BF16)
        delta = head_sums(out * r["tdot"][:, rows].astype(F32))
        for pair in range(HEADS // 2):
            cols = slice(pair * 2 * BLOCK, (pair + 1) * 2 * BLOCK)
            dprob = nt(r["tp"][rows, 2 * D :], r["tdos"][g, cols, :])
            shift = jnp.concatenate([delta[2 * pair : 2 * pair + 1], delta[2 * pair + 1 : 2 * pair + 2]], axis=1)
            r["tds"][g, :, cols] = (r["tprobs"][g, :, cols].astype(F32) * (dprob - shift)).astype(BF16)

    def time_grads(g):
        rows = slice(g * BLOCK, (g + 1) * BLOCK)
        outs = []
        for pair in range(HEADS // 2):
            cols = slice(pair * 2 * BLOCK, (pair + 1) * 2 * BLOCK)
            outs.append(diag(nn(r["tkvt"][pair * 2 * HD : (pair + 1) * 2 * HD, rows], r["tds"][g, :, cols])))
        r["tdp"][rows, 0:D] = (jnp.concatenate(outs, axis=0) * SCALE).T.astype(BF16)
        r["tdp"][rows, D : 2 * D] = (nn(r["tds"][g], r["tqs"][g]) * SCALE).astype(BF16)
        r["tdp"][rows, 2 * D : 3 * D] = nn(r["tprobs"][g], r["tdos"][g]).astype(BF16)

    def mg_copy(d, side):
        return remote(
            r["mgs"].at[d, :, in_part(side), :], r["mg"].at[:, side_rows(tm, side), :], r["mg_s"].at[side, d - 1],
            r["mg_r"].at[side, d - 1], (lax.rem(tm + (ntm - d), ntm), sp),
        )

    def mf_copy(d, side):
        return remote(
            r["mfs"].at[d, :, in_part(side), :], mixed_out.at[:, side_rows(tm, side), :], r["mf_s"].at[side, d - 1],
            r["mf_r"].at[side, d - 1], (lax.rem(tm + (ntm - d), ntm), sp),
        )

    def keep(side):
        return pltpu.make_async_copy(
            r["mfs"].at[0, :, in_part(side), :], mixed_out.at[:, side_rows(tm, side), :], r["own_sem"].at[1, side]
        )

    for side in range(2):
        groups = (2 * side, 2 * side + 1)
        time_inputs(side)
        for g in groups:
            time_scores(g)
        for g in groups:
            time_out(g)
        for g in groups:
            time_grads(g)
        for g in groups:
            rows = slice(g * BLOCK, (g + 1) * BLOCK)
            act_grad = nt(r["tdp"][rows, :], r["wv"][1])
            r["tmix"][g] = r["ct"][g] + norm_back(act_grad, r["tnrm"][rows, :], r["trinv"][rows, :])
        ungroup(r["tmix"], r["mgs"], side)
        loop(ntm - 1, lambda i, side=side: mg_copy(i + 1, side).start())
        r["mg"][:, side_rows(tm, side), :] = r["mgs"][0, :, side * hp : (side + 1) * hp, :]

    turned = r["tact"][...].astype(F32).T.astype(BF16)
    r["g0"][0:D, :] = nn(turned, r["tdp"][:, D:]).astype(BF16)
    r["g0"][D:, 0:D] = nn(turned, r["tdp"][:, 0:D]).astype(BF16)
    cots = r["ct"][...].reshape(GROUPS * BLOCK, D).astype(BF16)
    r["g0"][D:, D:] = nn(r["tot"][...], cots).astype(BF16)

    my_half = pl.ds(pl.multiple_of(core * 256, 256), 256)
    other_half = pl.ds(pl.multiple_of((1 - core) * 256, 256), 256)
    in_half = pl.ds(pl.multiple_of(place * chunk, chunk), chunk)
    my_chunk = pl.ds(pl.multiple_of(core * 256 + place * chunk, chunk), chunk)

    def pair_copy(a):
        return remote(r["g" + str(a)].at[other_half, :], r["pr" + str(a)], r["pr_s"].at[a], r["pr_r"].at[a], (tm, partner))

    def rs_copy(a, d):
        device, other = plane_peer(d)
        rows = pl.ds(pl.multiple_of(other * chunk, chunk), chunk)
        return remote(r["h" + str(a)].at[rows, :], r["rs" + str(a)].at[d - 1], r["rs_s"].at[a], r["rs_r"].at[a], device)

    def z_copy(a, d):
        return remote(r["zb" + str(a)].at[z], r["zb" + str(a)].at[z], r["z_s"].at[a], r["z_r"].at[a], z_peer(d))

    outs = (fin0_out, fin1_out, fin2_out, fin3_out)

    def ag_copy(a, d):
        device, _ = plane_peer(d)
        return remote(r["fin" + str(a)], outs[a].at[my_chunk, :], r["ag_s"].at[a], r["ag_r"].at[a], device)

    def fin_copy(a):
        return pltpu.make_async_copy(r["fin" + str(a)], outs[a].at[my_chunk, :], r["out_s"].at[a])

    def join_copy(a):
        return remote(outs[a].at[my_half, :], outs[a].at[my_half, :], r["pg_s"].at[a], r["pg_r"].at[a], (tm, partner))

    def drain(ref, sem):
        pltpu.make_async_copy(ref, ref, sem).wait()

    def reduce_pair(a):
        pair_copy(a).wait_recv()
        r["h" + str(a)][...] = (r["g" + str(a)][my_half, :].astype(F32) + r["pr" + str(a)][...].astype(F32)).astype(BF16)

    def reduce_plane(a):
        loop(npl - 1, lambda i: rs_copy(a, i + 1).start())

    def reduce_middle(a):
        drain(r["rs" + str(a)], r["rs_r"].at[a])
        total = r["h" + str(a)][in_half, :].astype(F32)
        for d in range(npl - 1):
            total = total + r["rs" + str(a)][d].astype(F32)
        r["zb" + str(a)][z] = total.astype(BF16)
        loop(nz - 1, lambda i: z_copy(a, i + 1).start())

    def reduce_share(a):
        drain(r["zb" + str(a)].at[0 : nz - 1], r["z_r"].at[a])
        total = r["zb" + str(a)][0].astype(F32)
        for k in range(1, nz):
            total = total + r["zb" + str(a)][k].astype(F32)
        r["fin" + str(a)][...] = total.astype(BF16)
        fin_copy(a).start()
        loop(npl - 1, lambda i: ag_copy(a, i + 1).start())

    def reduce_join(a):
        fin_copy(a).wait()
        drain(outs[a].at[0 : (npl - 1) * chunk, :], r["ag_r"].at[a])
        join_copy(a).start()

    def reduce_end(a):
        join_copy(a).wait_recv()

    def reduce_drain(a):
        pair_copy(a).wait_send()
        drain(r["rs" + str(a)], r["rs_s"].at[a])
        drain(r["zb" + str(a)].at[0 : nz - 1], r["z_s"].at[a])
        drain(outs[a].at[0 : (npl - 1) * chunk, :], r["ag_s"].at[a])
        join_copy(a).wait_send()

    pair_copy(0).start()

    r["dkv"][...] = jnp.zeros_like(r["dkv"])

    for g in range(GROUPS):
        rows = slice(g * BLOCK, (g + 1) * BLOCK)
        r["tmf"][g] = r["xt"][g] + nn(r["tatt"][rows, :], r["cv"][1])
    for side in range(2):
        ungroup(r["tmf"], r["mfs"], side)
        keep(side).start()
    for f in range(FR):
        for slot in range(3):
            r["act_t"][f, :, slot * ROWS : (slot + 1) * ROWS] = r["act"][slot, f].astype(F32).T.astype(BF16)

    def mg_arrival(d, side):
        return remote(
            r["mgs"].at[d, :, in_part(side), :], r["mg"].at[:, side_rows(lax.rem(tm + d, ntm), side), :],
            r["mg_s"].at[side, d - 1], r["mg_r"].at[side, d - 1], (tm, sp),
        )

    def grads_in(j):
        loop(ntm - 1, lambda k: mg_arrival(k + 1, j).wait_recv())
        for f in range(FR):
            i = 2 * f + j
            turned = nt(r["cv"][0], r["mg"][f, j * BLOCK : (j + 1) * BLOCK, :])
            share = jnp.broadcast_to(r["share"][i][:, None, :], (HEADS, HD, BLOCK)).reshape(D, BLOCK)
            turned = turned * share
            r["delta"][i] = head_sums(r["ot"][i] * turned.astype(BF16).astype(F32))
            grad = turned.T.astype(BF16)
            for h in range(HEADS):
                r["dos"][i, h * BLOCK : (h + 1) * BLOCK, :] = grad * r["hm"][h]

    grads_in(0)
    reduce_pair(0)
    reduce_plane(0)

    def edge_copy(f, side):
        return remote(
            r["eg"].at[f, side], r["er"].at[f, 1 - side], r["ed_s"].at[f, side], r["ed_r"].at[f, side],
            (tm, right if side else left),
        )

    def edge_make(f):
        for side in range(2):
            rows = slice(2 * ROWS * side, 2 * ROWS * side + ROWS)
            r["eg"][f, side] = nt(r["dkvb"][f, rows, :], r["wv"][0, :, D:]).astype(BF16)

    def backward_block(o):
        f = lax.rem(o, FR)
        j = lax.div(o, FR)
        i = 2 * f + j
        rows = key_rows(j)
        mine = pl.ds(pl.multiple_of(j * BLOCK, BLOCK), BLOCK)
        delta = r["delta"][i]
        outs = []

        def grads(pair):
            cols = slice(pair * 2 * BLOCK, (pair + 1) * 2 * BLOCK)
            r["s"][pair] = nt(r["kv"][f, rows, D:], r["dos"][i, cols, :])

        grads(0)
        r["dkv"][f, rows, D:] += nn(r["probs"][i], r["dos"][i])
        for pair in range(HEADS // 2):
            cols = slice(pair * 2 * BLOCK, (pair + 1) * 2 * BLOCK)
            s = r["s"].at[pair]
            if pair + 1 < HEADS // 2:
                grads(pair + 1)
            shift = jnp.concatenate([delta[2 * pair : 2 * pair + 1], delta[2 * pair + 1 : 2 * pair + 2]], axis=1)
            for e in range(SPAN):
                block = slice(e * BLOCK, (e + 1) * BLOCK)
                r["ds"][block, cols] = (r["probs"][i, block, cols].astype(F32) * (s[block, :] - shift)).astype(BF16)
            outs.append(diag(nn(r["kt"][f, pair * 2 * HD : (pair + 1) * 2 * HD, rows], r["ds"][:, cols])))
        r["dq"][f, mine, :] = (jnp.concatenate(outs, axis=0) * SCALE).T.astype(BF16)
        r["dkv"][f, rows, 0:D] += nn(r["ds"][...], r["qs"][i]) * SCALE

        @pl.when(o == 1)
        def _():
            grads_in(1)
            outward = nn(r["otb"][:, 0:ROWS], r["mg"][0]) + nn(r["otb"][:, ROWS:], r["mg"][1])
            r["g2"][0:D, :] = outward[:, 0:BLOCK].astype(BF16)
            r["g2"][D:, :] = outward[:, BLOCK:].astype(BF16)
            pair_copy(2).start()

        @pl.when(o == 2)
        def _():
            reduce_middle(0)
            reduce_pair(2)
            reduce_plane(2)
            r["dkvb"][0] = r["dkv"][0].astype(BF16)
            edge_make(0)
            for side in range(2):
                edge_copy(0, side).start()
            for side in range(2):
                loop(ntm - 1, lambda k, side=side: mf_copy(k + 1, side).start())

    loop(4, backward_block)

    inward = nn(r["act_t"][0, :, ROWS : 2 * ROWS], r["dq"][0]) + nn(r["act_t"][1, :, ROWS : 2 * ROWS], r["dq"][1])
    r["g3"][0:D, :] = inward[:, 0:BLOCK].astype(BF16)
    r["g3"][D:, :] = inward[:, BLOCK:].astype(BF16)
    pair_copy(3).start()
    r["dkvb"][1] = r["dkv"][1].astype(BF16)
    inward = nn(r["act_t"][0], r["dkvb"][0]) + nn(r["act_t"][1], r["dkvb"][1])
    r["g1"][0:D, :] = inward[:, 0:D].astype(BF16)
    r["g1"][D:, :] = inward[:, D:].astype(BF16)
    pair_copy(1).start()
    reduce_pair(3)
    reduce_plane(3)
    reduce_pair(1)
    reduce_plane(1)
    edge_make(1)
    for f in range(FR):
        r["fgw"][f] = nt(r["dq"][f], r["wv"][0, :, 0:D]) + nt(r["dkvb"][f, ROWS : 2 * ROWS, :], r["wv"][0, :, D:])
    reduce_middle(2)
    reduce_share(0)
    reduce_middle(3)
    reduce_middle(1)
    reduce_share(2)
    for side in range(2):
        edge_copy(1, side).start()
    reduce_share(3)
    reduce_share(1)
    for a in (0, 2):
        reduce_join(a)

    for f in range(FR):
        for side in range(2):
            edge_copy(f, side).wait_recv()
        act_grad = r["fgw"][f] + r["er"][f, 0].astype(F32) + r["er"][f, 1].astype(F32)
        r["fg"][f] = (r["mg"][f].astype(F32) + norm_back(act_grad, r["nrm"][f], r["rinv"][f])).astype(BF16)
    field_copy = pltpu.make_async_copy(r["fg"], fg_out, r["out_s"].at[4])
    field_copy.start()

    def mf_arrival(d, side):
        return remote(
            r["mfs"].at[d, :, in_part(side), :], mixed_out.at[:, side_rows(lax.rem(tm + d, ntm), side), :],
            r["mf_s"].at[side, d - 1], r["mf_r"].at[side, d - 1], (tm, sp),
        )

    for side in range(2):
        keep(side).wait()
        loop(ntm - 1, lambda i, side=side: mf_arrival(i + 1, side).wait_recv())
        loop(ntm - 1, lambda i, side=side: mf_copy(i + 1, side).wait_send())
        loop(ntm - 1, lambda i, side=side: mg_copy(i + 1, side).wait_send())
        loop(ntm - 1, lambda i, side=side: cot_copy(i + 1, side).wait_send())
    for f in range(FR):
        for side in range(2):
            loop(ntm - 1, lambda i, f=f, side=side: ms_copy(f, side, i + 1).wait_send())
        for side in range(2):
            edge_copy(f, side).wait_send()
        for item in halos(f):
            item.wait_send()
    reduce_drain(0)
    reduce_drain(2)

    for a in (0, 2):
        reduce_end(a)
    reduce_join(3)
    reduce_join(1)
    reduce_end(3)
    reduce_end(1)
    reduce_drain(3)
    reduce_drain(1)
    field_copy.wait()


def finish_kernel(factor, *refs):
    ins, outs = refs[:6], refs[6:10]
    held, made = refs[10:16], refs[16:18]
    in_sem, out_sem = refs[18:20]
    loads = [pltpu.make_async_copy(src, dst, in_sem.at[i]) for i, (src, dst) in enumerate(zip(ins, held))]
    order = (2, 4, 3, 5, 0, 1)
    for i in order:
        loads[i].start()
    fin0, fin1, fin2, fin3 = held[2:6]
    project, combine = made
    stores = [
        pltpu.make_async_copy(project.at[1], outs[2].at[1], out_sem.at[0]),
        pltpu.make_async_copy(combine, outs[3], out_sem.at[1]),
        pltpu.make_async_copy(project.at[0], outs[2].at[0], out_sem.at[2]),
        pltpu.make_async_copy(held[0], outs[0], out_sem.at[3]),
        pltpu.make_async_copy(held[1], outs[1], out_sem.at[4]),
    ]
    loads[2].wait()
    project[1, :, D:] = fin0[0:D, :].astype(F32) * factor
    project[1, :, 0:D] = fin0[D:, 0:D].astype(F32) * factor
    stores[0].start()
    combine[1] = fin0[D:, D:].astype(F32) * factor
    loads[4].wait()
    combine[0, :, 0:BLOCK] = fin2[0:D, :].astype(F32) * factor
    combine[0, :, BLOCK:] = fin2[D:, :].astype(F32) * factor
    stores[1].start()
    loads[3].wait()
    project[0, :, D : 2 * D] = fin1[0:D, :].astype(F32) * factor
    project[0, :, 2 * D :] = fin1[D:, :].astype(F32) * factor
    loads[5].wait()
    project[0, :, 0:BLOCK] = fin3[0:D, :].astype(F32) * factor
    project[0, :, BLOCK:D] = fin3[D:, :].astype(F32) * factor
    stores[2].start()
    for i in range(2):
        loads[i].wait()
        stores[3 + i].start()
    for item in stores:
        item.wait()


def per_device(ntm, nsp, wave_field, cotangent, block_lists, project_weights, combine_weights):
    shapes = scratch_shapes(ntm, nsp)
    names = tuple(shapes)
    anywhere = pl.BlockSpec(memory_space=pl.ANY)
    rows = jax.ShapeDtypeStruct((FR, ROWS, D), BF16)
    results = pl.pallas_call(
        functools.partial(step_kernel, ntm, nsp, names),
        out_shape=(rows, rows) + tuple(jax.ShapeDtypeStruct((512, lanes), BF16) for lanes in LANES),
        in_specs=[anywhere] * 5,
        out_specs=(anywhere,) * 6,
        scratch_shapes=list(shapes.values()),
        compiler_params=pltpu.CompilerParams(
            collective_id=0, has_side_effects=True, vmem_limit_bytes=LIMIT
        ),
        name="cuboid_step",
    )(block_lists, wave_field, cotangent, project_weights, combine_weights)
    factor = 1.0 / math.sqrt(FR * ntm * ROWS * nsp)
    return pl.pallas_call(
        functools.partial(finish_kernel, factor),
        out_shape=(
            rows,
            rows,
            jax.ShapeDtypeStruct((2, D, 3 * D), F32),
            jax.ShapeDtypeStruct((2, D, D), F32),
        ),
        in_specs=[anywhere] * 6,
        out_specs=(anywhere,) * 4,
        scratch_shapes=[pltpu.VMEM((FR, ROWS, D), BF16)] * 2
        + [pltpu.VMEM((512, lanes), BF16) for lanes in LANES]
        + [
            pltpu.VMEM((2, D, 3 * D), F32),
            pltpu.VMEM((2, D, D), F32),
            pltpu.SemaphoreType.DMA((6,)),
            pltpu.SemaphoreType.DMA((5,)),
        ],
        compiler_params=pltpu.CompilerParams(vmem_limit_bytes=LIMIT),
        name="finish",
    )(*results)


def solution(mesh):
    in_specs = (P("tm", "space", None), P("tm", "space", None), P("tm", "space", None), P(), P())
    out_specs = (P("tm", "space", None), P("tm", "space", None), P(), P())
    return jax.shard_map(
        functools.partial(per_device, mesh.shape["tm"], mesh.shape["space"]),
        mesh=mesh,
        in_specs=in_specs,
        out_specs=out_specs,
        check_vma=False,
    )
```

```python
import functools
import math

import jax
import jax.numpy as jnp
from jax import lax
from jax.experimental import pallas as pl
from jax.experimental.pallas import tpu as pltpu
from jax.sharding import PartitionSpec as P

HEADS = 8
BLOCK = 128
SPAN = 5
KEYS = SPAN * BLOCK
D = 256
HD = 32
ROWS = 256
FR = 2
GROUPS = 4
CORES = 4
EPS = 1e-05
NEG = -1e30
PADS = 80
LIMIT = 60 * 1024 * 1024
LANES = (512, 256, 128, 128)
SCALE = 1.0 / math.sqrt(HD)
SCALE2 = SCALE * math.log2(math.e)

MESH = pl.DeviceIdType.MESH
F32 = jnp.float32
BF16 = jnp.bfloat16


def nn(left, right):
    return jnp.dot(left, right, preferred_element_type=F32)


def nt(left, right):
    return lax.dot_general(left, right, (((1,), (1,)), ((), ())), preferred_element_type=F32)


def norm(rows):
    centered = rows - jnp.mean(rows, axis=-1, keepdims=True)
    inverse = lax.rsqrt(jnp.mean(centered * centered, axis=-1, keepdims=True) + EPS)
    return centered * inverse, inverse


def norm_back(upstream, normed, inverse):
    mean_grad = jnp.mean(upstream, axis=-1, keepdims=True)
    mean_cross = jnp.mean(upstream * normed, axis=-1, keepdims=True)
    return inverse * (upstream - mean_grad - normed * mean_cross)


def diag(pair):
    return jnp.concatenate([pair[0:HD, 0:BLOCK], pair[HD : 2 * HD, BLOCK : 2 * BLOCK]], axis=0)


def head_sums(prod):
    return jnp.sum(prod.reshape(HEADS, HD, BLOCK), axis=1)


def scratch_shapes(ntm, nsp):
    nz = nsp // CORES
    npl = ntm * 2
    part = ROWS // ntm
    chunk = 256 // npl
    dma = pltpu.SemaphoreType.DMA
    vm = pltpu.VMEM
    return dict(
        xe=vm((3, FR, ROWS, D), BF16),
        act=vm((3, FR, ROWS, D), BF16),
        act_t=vm((FR, D, 3 * ROWS), BF16),
        nrm=vm((FR, ROWS, D), F32),
        rinv=vm((FR, ROWS, 1), F32),
        wv=vm((2, D, 3 * D), BF16),
        cv=vm((2, D, D), BF16),
        wt=vm((2, 2 * D, D), BF16),
        hm=vm((HEADS, BLOCK, D), BF16),
        q=vm((FR, ROWS, D), BF16),
        kv=vm((FR, 3 * ROWS, 2 * D), BF16),
        kt=vm((FR, D, 3 * ROWS), BF16),
        vt=vm((FR, HEADS // 2, PADS, 3 * ROWS), BF16),
        qs=vm((4, HEADS * BLOCK, D), BF16),
        dos=vm((4, HEADS * BLOCK, D), BF16),
        share=vm((4, HEADS, BLOCK), F32),
        delta=vm((4, HEADS, BLOCK), F32),
        probs=vm((4, KEYS, HEADS * BLOCK), BF16),
        ds=vm((KEYS, HEADS * BLOCK), BF16),
        s=vm((4, KEYS, 2 * BLOCK), F32),
        ot=vm((4, D, BLOCK), F32),
        otb=vm((D, 4 * BLOCK), BF16),
        att=vm((FR, ROWS, D), BF16),
        ms=vm((FR, ROWS, D), BF16),
        hist=vm((ntm, FR, part, D), BF16),
        hcot=vm((ntm, FR, part, D), BF16),
        xt=vm((GROUPS, BLOCK, D), F32),
        ct=vm((GROUPS, BLOCK, D), F32),
        tb=vm((BLOCK, 2 * BLOCK), F32),
        tnrm=vm((GROUPS * BLOCK, D), F32),
        trinv=vm((GROUPS * BLOCK, 1), F32),
        tact=vm((GROUPS * BLOCK, D), BF16),
        tp=vm((GROUPS * BLOCK, 3 * D), BF16),
        tkvt=vm((2 * D, GROUPS * BLOCK), BF16),
        tdo=vm((GROUPS * BLOCK, D), BF16),
        tdot=vm((D, GROUPS * BLOCK), BF16),
        tot=vm((D, GROUPS * BLOCK), BF16),
        tatt=vm((GROUPS * BLOCK, D), BF16),
        tdp=vm((GROUPS * BLOCK, 3 * D), BF16),
        tqs=vm((GROUPS, HEADS * BLOCK, D), BF16),
        tdos=vm((GROUPS, HEADS * BLOCK, D), BF16),
        tprobs=vm((GROUPS, BLOCK, HEADS * BLOCK), BF16),
        tds=vm((GROUPS, BLOCK, HEADS * BLOCK), BF16),
        tmix=vm((GROUPS, BLOCK, D), F32),
        tmf=vm((GROUPS, BLOCK, D), F32),
        mfs=vm((ntm, FR, part, D), BF16),
        mgs=vm((ntm, FR, part, D), BF16),
        mg=vm((FR, ROWS, D), BF16),
        dq=vm((FR, ROWS, D), BF16),
        dkv=vm((FR, 3 * ROWS, 2 * D), F32),
        dkvb=vm((FR, 3 * ROWS, 2 * D), BF16),
        eg=vm((FR, 2, ROWS, D), BF16),
        er=vm((FR, 2, ROWS, D), BF16),
        fg=vm((FR, ROWS, D), BF16),
        fgw=vm((FR, ROWS, D), F32),
        **{
            name + str(a): vm(shape + (lanes,), BF16)
            for a, lanes in enumerate(LANES)
            for name, shape in (
                ("g", (512,)),
                ("pr", (256,)),
                ("h", (256,)),
                ("rs", (npl - 1, chunk)),
                ("zb", (nz, chunk)),
                ("fin", (chunk,)),
            )
        },
        lists=pltpu.SMEM((FR, 2, 4), jnp.int32),
        ld_sem=dma((8,)),
        own_sem=dma((2, 2)),
        halo_s=dma((FR, 2)),
        halo_r=dma((FR, 2)),
        cot_s=dma((2, ntm - 1)),
        cot_r=dma((2, ntm - 1)),
        ms_s=dma((2, FR, ntm - 1)),
        ms_r=dma((2, FR, ntm - 1)),
        mf_s=dma((2, ntm - 1)),
        mf_r=dma((2, ntm - 1)),
        mg_s=dma((2, ntm - 1)),
        mg_r=dma((2, ntm - 1)),
        ed_s=dma((FR, 2)),
        ed_r=dma((FR, 2)),
        pr_s=dma((4,)),
        pr_r=dma((4,)),
        pg_s=dma((4,)),
        pg_r=dma((4,)),
        out_s=dma((5,)),
        rs_s=dma((4,)),
        rs_r=dma((4,)),
        z_s=dma((4,)),
        z_r=dma((4,)),
        ag_s=dma((4,)),
        ag_r=dma((4,)),
    )


def step_kernel(ntm, nsp, names, lists_hbm, x_hbm, cot_hbm, w_hbm, c_hbm, mixed_out, fg_out, fin0_out, fin1_out, fin2_out, fin3_out, *refs):
    r = dict(zip(names, refs))
    nz = nsp // CORES
    npl = ntm * 2
    hp = ROWS // ntm // 2
    chunk = 256 // npl
    frames = FR * ntm
    per = BLOCK // frames

    tm = lax.axis_index("tm")
    sp = lax.axis_index("space")
    z = lax.div(sp, CORES)
    quarter = lax.rem(sp, CORES)
    core = lax.rem(sp, 2)
    partner = sp + 1 - 2 * core
    left = lax.rem(sp + (nsp - 1), nsp)
    right = lax.rem(sp + 1, nsp)
    place = tm * 2 + lax.div(quarter, 2)

    def plane_peer(d):
        other = lax.rem(place + d, npl)
        return (lax.div(other, 2), z * CORES + lax.rem(other, 2) * 2 + core), other

    def z_peer(d):
        return (tm, lax.rem(z + d, nz) * CORES + quarter)

    def remote(src, dst, send, recv, device):
        return pltpu.make_async_remote_copy(
            src_ref=src, dst_ref=dst, send_sem=send, recv_sem=recv, device_id=device, device_id_type=MESH
        )

    def loop(count, body):
        def wrapped(i, carry):
            body(i)
            return carry

        lax.fori_loop(0, count, wrapped, 0)

    barrier = pltpu.get_barrier_semaphore()
    pl.semaphore_signal(barrier, inc=1, device_id=(tm, left), device_id_type=MESH)
    pl.semaphore_signal(barrier, inc=1, device_id=(tm, right), device_id_type=MESH)
    loop(npl - 1, lambda i: pl.semaphore_signal(barrier, inc=1, device_id=plane_peer(i + 1)[0], device_id_type=MESH))
    loop(nz - 1, lambda i: pl.semaphore_signal(barrier, inc=1, device_id=z_peer(i + 1), device_id_type=MESH))

    ld = r["ld_sem"]

    def side_rows(device, side):
        return pl.ds(pl.multiple_of(side * BLOCK + device * hp, hp), hp)

    def in_part(side):
        return pl.ds(side * hp, hp)

    loads = [
        pltpu.make_async_copy(w_hbm.at[0], r["wv"].at[0], ld.at[0]),
        pltpu.make_async_copy(x_hbm.at[0], r["xe"].at[1, 0], ld.at[1]),
        pltpu.make_async_copy(c_hbm, r["cv"], ld.at[2]),
        pltpu.make_async_copy(w_hbm.at[1], r["wv"].at[1], ld.at[3]),
        pltpu.make_async_copy(
            cot_hbm.at[:, side_rows(tm, 0), :], r["hcot"].at[0, :, in_part(0), :], r["own_sem"].at[0, 0]
        ),
        pltpu.make_async_copy(x_hbm.at[1], r["xe"].at[1, 1], ld.at[6]),
        pltpu.make_async_copy(lists_hbm, r["lists"], ld.at[7]),
        pltpu.make_async_copy(
            cot_hbm.at[:, side_rows(tm, 1), :], r["hcot"].at[0, :, in_part(1), :], r["own_sem"].at[0, 1]
        ),
    ]
    for item in loads:
        item.start()

    lane_head = lax.broadcasted_iota(jnp.int32, (BLOCK, D), 1) // HD
    for h in range(HEADS):
        r["hm"][h] = jnp.where(lane_head == h, 1.0, 0.0).astype(BF16)
    key_pos = lax.broadcasted_iota(jnp.int32, (BLOCK, 2 * BLOCK), 0) % per
    query_pos = lax.broadcasted_iota(jnp.int32, (BLOCK, 2 * BLOCK), 1) % per
    r["tb"][...] = jnp.where(key_pos == query_pos, 0.0, NEG)

    r["vt"][:, :, 2 * HD :, :] = jnp.ones((FR, HEADS // 2, PADS - 2 * HD, 3 * ROWS), BF16)

    loads[0].wait()
    r["wt"][0] = r["wv"][0, :, D:].astype(F32).T.astype(BF16)

    pl.semaphore_wait(barrier, 2 + (npl - 1) + (nz - 1))

    def halos(f):
        return [
            remote(x_hbm.at[f], r["xe"].at[2, f], r["halo_s"].at[f, 0], r["halo_r"].at[f, 0], (tm, left)),
            remote(x_hbm.at[f], r["xe"].at[0, f], r["halo_s"].at[f, 1], r["halo_r"].at[f, 1], (tm, right)),
        ]

    for f in range(FR):
        for item in halos(f):
            item.start()

    def cot_copy(d, side):
        to = lax.rem(tm + d, ntm)
        return remote(
            cot_hbm.at[:, side_rows(to, side), :], r["hcot"].at[d, :, in_part(side), :], r["cot_s"].at[side, d - 1],
            r["cot_r"].at[side, d - 1], (to, sp),
        )

    def project(slot, f):
        normed, inverse = norm(r["xe"][slot, f].astype(F32))
        rows = slice(slot * ROWS, (slot + 1) * ROWS)
        act = normed.astype(BF16)
        r["act"][slot, f] = act
        if slot == 1:
            r["nrm"][f] = normed
            r["rinv"][f] = inverse
            r["q"][f] = nn(act, r["wv"][0, :, 0:D]).astype(BF16)
        r["kv"][f, rows, :] = nn(act, r["wv"][0, :, D:]).astype(BF16)
        turned = nt(r["wt"][0], act).astype(BF16)
        r["kt"][f, :, rows] = turned[0:D]
        for pair in range(HEADS // 2):
            r["vt"][f, pair, 0 : 2 * HD, rows] = turned[D + pair * 2 * HD : D + (pair + 1) * 2 * HD]

    loads[1].wait()
    project(1, 0)
    loads[5].wait()
    project(1, 1)
    for f in range(FR):
        for j in range(2):
            for h in range(HEADS):
                r["qs"][2 * f + j, h * BLOCK : (h + 1) * BLOCK, :] = (
                    r["q"][f, j * BLOCK : (j + 1) * BLOCK, :] * r["hm"][h]
                )

    def key_rows(j):
        return pl.ds(pl.multiple_of(j * BLOCK, BLOCK), KEYS)

    def biases(f, j):
        out = []
        first = sp * 2 + j - 2
        for e in range(SPAN):
            count = jnp.int32(0)
            for k in range(4):
                count = count + jnp.where(r["lists"][f, j, k] == first + e, 1, 0)
            out.append(
                jnp.where(
                    count == 0,
                    NEG,
                    jnp.where(count == 1, 0.0, jnp.where(count == 2, 1.0, jnp.where(count == 3, math.log2(3.0), 2.0))),
                ).astype(F32)
            )
        return out

    def forward_block(f, j):
        i = 2 * f + j
        rows = key_rows(j)
        bias = biases(f, j)
        outs = []

        def scores(pair):
            cols = slice(pair * 2 * BLOCK, (pair + 1) * 2 * BLOCK)
            r["s"][pair] = nt(r["kv"][f, rows, 0:D], r["qs"][i, cols, :])

        scores(0)
        for pair in range(HEADS // 2):
            cols = slice(pair * 2 * BLOCK, (pair + 1) * 2 * BLOCK)
            if pair + 1 < HEADS // 2:
                scores(pair + 1)
            s = r["s"].at[pair]
            top = None
            for e in range(SPAN):
                here = jnp.max(s[e * BLOCK : (e + 1) * BLOCK, :], axis=0, keepdims=True) * SCALE2 + bias[e]
                top = here if top is None else jnp.maximum(top, here)
            for e in range(SPAN):
                block = slice(e * BLOCK, (e + 1) * BLOCK)
                r["probs"][i, block, cols] = jnp.exp2(s[block, :] * SCALE2 + (bias[e] - top)).astype(BF16)
            both = nn(r["vt"][f, pair, :, rows], r["probs"][i, :, cols])
            share = 1.0 / both[2 * HD : 2 * HD + 1, :]
            r["share"][i, 2 * pair : 2 * pair + 1, :] = share[:, 0:BLOCK]
            r["share"][i, 2 * pair + 1 : 2 * pair + 2, :] = share[:, BLOCK:]
            outs.append(diag(both[0 : 2 * HD] * share))
        out = jnp.concatenate(outs, axis=0)
        r["ot"][i] = out
        r["otb"][:, pl.ds(pl.multiple_of(i * BLOCK, BLOCK), BLOCK)] = out.astype(BF16)
        r["att"][f, pl.ds(pl.multiple_of(j * BLOCK, BLOCK), BLOCK), :] = out.T.astype(BF16)

    def ms_copy(f, side, d):
        to = lax.rem(tm + d, ntm)
        return remote(
            r["ms"].at[f, side_rows(to, side), :],
            r["hist"].at[d, f, pl.ds(pl.multiple_of(side * hp, hp), hp), :],
            r["ms_s"].at[side, f, d - 1],
            r["ms_r"].at[side, f, d - 1],
            (to, sp),
        )

    loads[3].wait()
    r["wt"][1] = r["wv"][1, :, D:].astype(F32).T.astype(BF16)
    loads[2].wait()
    loads[6].wait()

    def forward(o):
        f = lax.rem(o, FR)
        j = lax.div(o, FR)

        @pl.when(j == 0)
        def _():
            for item in halos(f):
                item.wait_recv()

        @pl.when(o == FR - 1)
        def _():
            for side in range(2):
                loop(ntm - 1, lambda i, side=side: cot_copy(i + 1, side).start())

        @pl.when(j == 0)
        def _():
            project(2, f)
            project(0, f)

        forward_block(f, j)
        rows = pl.ds(pl.multiple_of(j * BLOCK, BLOCK), BLOCK)
        mixed = r["xe"][1, f, rows, :].astype(F32) + nn(r["att"][f, rows, :], r["cv"][0])
        r["ms"][f, rows, :] = mixed.astype(BF16)
        loop(ntm - 1, lambda i: ms_copy(f, j, i + 1).start())
        r["hist"][0, f, pl.ds(pl.multiple_of(j * hp, hp), hp), :] = r["ms"][f, side_rows(tm, j), :]

    loop(2 * FR, forward)

    def ungroup(src, dst, side):
        for d in range(ntm):
            for f in range(FR):
                frame = d * FR + f
                dst[d, f, side * 2 * per : (side + 1) * 2 * per, :] = jnp.concatenate(
                    [src[g, frame * per : (frame + 1) * per, :] for g in (2 * side, 2 * side + 1)], axis=0
                ).astype(BF16)

    def time_inputs(side):
        mine = slice(side * hp, (side + 1) * hp)
        groups = (2 * side, 2 * side + 1)
        loads[(4, 7)[side]].wait()
        loop(ntm - 1, lambda i: cot_copy(i + 1, side).wait_recv())
        for d in range(ntm):
            for f in range(FR):
                frame = d * FR + f
                block = r["hcot"][d, f, mine, :].astype(F32)
                for k, g in enumerate(groups):
                    r["ct"][g, frame * per : (frame + 1) * per, :] = block[k * per : (k + 1) * per]
        for g in groups:
            rows = slice(g * BLOCK, (g + 1) * BLOCK)
            cot = r["ct"][g].astype(BF16)
            grad = nt(cot, r["cv"][1]).astype(BF16)
            for h in range(HEADS):
                r["tdos"][g, h * BLOCK : (h + 1) * BLOCK, :] = grad * r["hm"][h]
            r["tdot"][:, rows] = nt(r["cv"][1], cot).astype(BF16)
        for f in range(FR):
            loop(ntm - 1, lambda i, f=f: ms_copy(f, side, i + 1).wait_recv())
            for d in range(ntm):
                frame = d * FR + f
                block = r["hist"][d, f, mine, :].astype(F32)
                normed, inverse = norm(block)
                for k, g in enumerate(groups):
                    to = slice(frame * per, (frame + 1) * per)
                    at = slice(g * BLOCK + frame * per, g * BLOCK + (frame + 1) * per)
                    piece = slice(k * per, (k + 1) * per)
                    r["xt"][g, to, :] = block[piece]
                    r["tnrm"][at, :] = normed[piece]
                    r["trinv"][at, :] = inverse[piece]
        rows = slice(side * 2 * BLOCK, (side + 1) * 2 * BLOCK)
        r["tact"][rows, :] = r["tnrm"][rows, :].astype(BF16)
        r["tp"][rows, :] = nn(r["tact"][rows, :], r["wv"][1]).astype(BF16)
        r["tkvt"][:, rows] = nt(r["wt"][1], r["tact"][rows, :]).astype(BF16)

    def time_scores(g):
        rows = slice(g * BLOCK, (g + 1) * BLOCK)
        query = r["tp"][rows, 0:D]
        for h in range(HEADS):
            r["tqs"][g, h * BLOCK : (h + 1) * BLOCK, :] = query * r["hm"][h]
        for pair in range(HEADS // 2):
            cols = slice(pair * 2 * BLOCK, (pair + 1) * 2 * BLOCK)
            scores = nt(r["tp"][rows, D : 2 * D], r["tqs"][g, cols, :]) * SCALE2 + r["tb"][...]
            grown = jnp.exp2(scores - jnp.max(scores, axis=0, keepdims=True))
            share = 1.0 / jnp.sum(grown, axis=0, keepdims=True)
            r["tprobs"][g, :, cols] = (grown * share).astype(BF16)

    def time_out(g):
        rows = slice(g * BLOCK, (g + 1) * BLOCK)
        outs = []
        for pair in range(HEADS // 2):
            cols = slice(pair * 2 * BLOCK, (pair + 1) * 2 * BLOCK)
            values = r["tkvt"][D + pair * 2 * HD : D + (pair + 1) * 2 * HD, rows]
            outs.append(diag(nn(values, r["tprobs"][g, :, cols])))
        out = jnp.concatenate(outs, axis=0)
        r["tot"][:, rows] = out.astype(BF16)
        r["tatt"][rows, :] = out.T.astype(BF16)
        delta = head_sums(out * r["tdot"][:, rows].astype(F32))
        for pair in range(HEADS // 2):
            cols = slice(pair * 2 * BLOCK, (pair + 1) * 2 * BLOCK)
            dprob = nt(r["tp"][rows, 2 * D :], r["tdos"][g, cols, :])
            shift = jnp.concatenate([delta[2 * pair : 2 * pair + 1], delta[2 * pair + 1 : 2 * pair + 2]], axis=1)
            r["tds"][g, :, cols] = (r["tprobs"][g, :, cols].astype(F32) * (dprob - shift)).astype(BF16)

    def time_grads(g):
        rows = slice(g * BLOCK, (g + 1) * BLOCK)
        outs = []
        for pair in range(HEADS // 2):
            cols = slice(pair * 2 * BLOCK, (pair + 1) * 2 * BLOCK)
            outs.append(diag(nn(r["tkvt"][pair * 2 * HD : (pair + 1) * 2 * HD, rows], r["tds"][g, :, cols])))
        r["tdp"][rows, 0:D] = (jnp.concatenate(outs, axis=0) * SCALE).T.astype(BF16)
        r["tdp"][rows, D : 2 * D] = (nn(r["tds"][g], r["tqs"][g]) * SCALE).astype(BF16)
        r["tdp"][rows, 2 * D : 3 * D] = nn(r["tprobs"][g], r["tdos"][g]).astype(BF16)

    def mg_copy(d, side):
        return remote(
            r["mgs"].at[d, :, in_part(side), :], r["mg"].at[:, side_rows(tm, side), :], r["mg_s"].at[side, d - 1],
            r["mg_r"].at[side, d - 1], (lax.rem(tm + (ntm - d), ntm), sp),
        )

    def mf_copy(d, side):
        return remote(
            r["mfs"].at[d, :, in_part(side), :], mixed_out.at[:, side_rows(tm, side), :], r["mf_s"].at[side, d - 1],
            r["mf_r"].at[side, d - 1], (lax.rem(tm + (ntm - d), ntm), sp),
        )

    def keep(side):
        return pltpu.make_async_copy(
            r["mfs"].at[0, :, in_part(side), :], mixed_out.at[:, side_rows(tm, side), :], r["own_sem"].at[1, side]
        )

    for side in range(2):
        groups = (2 * side, 2 * side + 1)
        time_inputs(side)
        for g in groups:
            time_scores(g)
        for g in groups:
            time_out(g)
        for g in groups:
            time_grads(g)
        for g in groups:
            rows = slice(g * BLOCK, (g + 1) * BLOCK)
            act_grad = nt(r["tdp"][rows, :], r["wv"][1])
            r["tmix"][g] = r["ct"][g] + norm_back(act_grad, r["tnrm"][rows, :], r["trinv"][rows, :])
        ungroup(r["tmix"], r["mgs"], side)
        loop(ntm - 1, lambda i, side=side: mg_copy(i + 1, side).start())
        r["mg"][:, side_rows(tm, side), :] = r["mgs"][0, :, side * hp : (side + 1) * hp, :]

    turned = r["tact"][...].astype(F32).T.astype(BF16)
    r["g0"][0:D, :] = nn(turned, r["tdp"][:, D:]).astype(BF16)
    r["g0"][D:, 0:D] = nn(turned, r["tdp"][:, 0:D]).astype(BF16)
    cots = r["ct"][...].reshape(GROUPS * BLOCK, D).astype(BF16)
    r["g0"][D:, D:] = nn(r["tot"][...], cots).astype(BF16)

    my_half = pl.ds(pl.multiple_of(core * 256, 256), 256)
    other_half = pl.ds(pl.multiple_of((1 - core) * 256, 256), 256)
    in_half = pl.ds(pl.multiple_of(place * chunk, chunk), chunk)
    my_chunk = pl.ds(pl.multiple_of(core * 256 + place * chunk, chunk), chunk)

    def pair_copy(a):
        return remote(r["g" + str(a)].at[other_half, :], r["pr" + str(a)], r["pr_s"].at[a], r["pr_r"].at[a], (tm, partner))

    def rs_copy(a, d):
        device, other = plane_peer(d)
        rows = pl.ds(pl.multiple_of(other * chunk, chunk), chunk)
        return remote(r["h" + str(a)].at[rows, :], r["rs" + str(a)].at[d - 1], r["rs_s"].at[a], r["rs_r"].at[a], device)

    def z_copy(a, d):
        return remote(r["zb" + str(a)].at[z], r["zb" + str(a)].at[z], r["z_s"].at[a], r["z_r"].at[a], z_peer(d))

    outs = (fin0_out, fin1_out, fin2_out, fin3_out)

    def ag_copy(a, d):
        device, _ = plane_peer(d)
        return remote(r["fin" + str(a)], outs[a].at[my_chunk, :], r["ag_s"].at[a], r["ag_r"].at[a], device)

    def fin_copy(a):
        return pltpu.make_async_copy(r["fin" + str(a)], outs[a].at[my_chunk, :], r["out_s"].at[a])

    def join_copy(a):
        return remote(outs[a].at[my_half, :], outs[a].at[my_half, :], r["pg_s"].at[a], r["pg_r"].at[a], (tm, partner))

    def drain(ref, sem):
        pltpu.make_async_copy(ref, ref, sem).wait()

    def reduce_pair(a):
        pair_copy(a).wait_recv()
        r["h" + str(a)][...] = (r["g" + str(a)][my_half, :].astype(F32) + r["pr" + str(a)][...].astype(F32)).astype(BF16)

    def reduce_plane(a):
        loop(npl - 1, lambda i: rs_copy(a, i + 1).start())

    def reduce_middle(a):
        drain(r["rs" + str(a)], r["rs_r"].at[a])
        total = r["h" + str(a)][in_half, :].astype(F32)
        for d in range(npl - 1):
            total = total + r["rs" + str(a)][d].astype(F32)
        r["zb" + str(a)][z] = total.astype(BF16)
        loop(nz - 1, lambda i: z_copy(a, i + 1).start())

    def reduce_share(a):
        drain(r["zb" + str(a)].at[0 : nz - 1], r["z_r"].at[a])
        total = r["zb" + str(a)][0].astype(F32)
        for k in range(1, nz):
            total = total + r["zb" + str(a)][k].astype(F32)
        r["fin" + str(a)][...] = total.astype(BF16)
        fin_copy(a).start()
        loop(npl - 1, lambda i: ag_copy(a, i + 1).start())

    def reduce_join(a):
        fin_copy(a).wait()
        drain(outs[a].at[0 : (npl - 1) * chunk, :], r["ag_r"].at[a])
        join_copy(a).start()

    def reduce_end(a):
        join_copy(a).wait_recv()

    def reduce_drain(a):
        pair_copy(a).wait_send()
        drain(r["rs" + str(a)], r["rs_s"].at[a])
        drain(r["zb" + str(a)].at[0 : nz - 1], r["z_s"].at[a])
        drain(outs[a].at[0 : (npl - 1) * chunk, :], r["ag_s"].at[a])
        join_copy(a).wait_send()

    pair_copy(0).start()

    r["dkv"][...] = jnp.zeros_like(r["dkv"])

    for g in range(GROUPS):
        rows = slice(g * BLOCK, (g + 1) * BLOCK)
        r["tmf"][g] = r["xt"][g] + nn(r["tatt"][rows, :], r["cv"][1])
    for side in range(2):
        ungroup(r["tmf"], r["mfs"], side)
        keep(side).start()
    for f in range(FR):
        for slot in range(3):
            r["act_t"][f, :, slot * ROWS : (slot + 1) * ROWS] = r["act"][slot, f].astype(F32).T.astype(BF16)

    def mg_arrival(d, side):
        return remote(
            r["mgs"].at[d, :, in_part(side), :], r["mg"].at[:, side_rows(lax.rem(tm + d, ntm), side), :],
            r["mg_s"].at[side, d - 1], r["mg_r"].at[side, d - 1], (tm, sp),
        )

    def grads_in(j):
        loop(ntm - 1, lambda k: mg_arrival(k + 1, j).wait_recv())
        for f in range(FR):
            i = 2 * f + j
            turned = nt(r["cv"][0], r["mg"][f, j * BLOCK : (j + 1) * BLOCK, :])
            share = jnp.broadcast_to(r["share"][i][:, None, :], (HEADS, HD, BLOCK)).reshape(D, BLOCK)
            turned = turned * share
            r["delta"][i] = head_sums(r["ot"][i] * turned.astype(BF16).astype(F32))
            grad = turned.T.astype(BF16)
            for h in range(HEADS):
                r["dos"][i, h * BLOCK : (h + 1) * BLOCK, :] = grad * r["hm"][h]

    reduce_pair(0)
    reduce_plane(0)
    for side in range(2):
        loop(ntm - 1, lambda k, side=side: mf_copy(k + 1, side).start())
    grads_in(0)

    def edge_copy(f, side):
        return remote(
            r["eg"].at[f, side], r["er"].at[f, 1 - side], r["ed_s"].at[f, side], r["ed_r"].at[f, side],
            (tm, right if side else left),
        )

    def edge_make(f):
        for side in range(2):
            rows = slice(2 * ROWS * side, 2 * ROWS * side + ROWS)
            r["eg"][f, side] = nt(r["dkvb"][f, rows, :], r["wv"][0, :, D:]).astype(BF16)

    def backward_block(o):
        f = lax.rem(o, FR)
        j = lax.div(o, FR)
        i = 2 * f + j
        rows = key_rows(j)
        mine = pl.ds(pl.multiple_of(j * BLOCK, BLOCK), BLOCK)
        delta = r["delta"][i]
        outs = []

        def grads(pair):
            cols = slice(pair * 2 * BLOCK, (pair + 1) * 2 * BLOCK)
            r["s"][pair] = nt(r["kv"][f, rows, D:], r["dos"][i, cols, :])

        grads(0)
        r["dkv"][f, rows, D:] += nn(r["probs"][i], r["dos"][i])
        for pair in range(HEADS // 2):
            cols = slice(pair * 2 * BLOCK, (pair + 1) * 2 * BLOCK)
            s = r["s"].at[pair]
            if pair + 1 < HEADS // 2:
                grads(pair + 1)
            shift = jnp.concatenate([delta[2 * pair : 2 * pair + 1], delta[2 * pair + 1 : 2 * pair + 2]], axis=1)
            for e in range(SPAN):
                block = slice(e * BLOCK, (e + 1) * BLOCK)
                r["ds"][block, cols] = (r["probs"][i, block, cols].astype(F32) * (s[block, :] - shift)).astype(BF16)
            outs.append(diag(nn(r["kt"][f, pair * 2 * HD : (pair + 1) * 2 * HD, rows], r["ds"][:, cols])))
        r["dq"][f, mine, :] = (jnp.concatenate(outs, axis=0) * SCALE).T.astype(BF16)
        r["dkv"][f, rows, 0:D] += nn(r["ds"][...], r["qs"][i]) * SCALE

        @pl.when(o == 1)
        def _():
            grads_in(1)
            outward = nn(r["otb"][:, 0:ROWS], r["mg"][0]) + nn(r["otb"][:, ROWS:], r["mg"][1])
            r["g2"][0:D, :] = outward[:, 0:BLOCK].astype(BF16)
            r["g2"][D:, :] = outward[:, BLOCK:].astype(BF16)
            pair_copy(2).start()

        @pl.when(o == 2)
        def _():
            reduce_middle(0)
            reduce_pair(2)
            reduce_plane(2)
            r["dkvb"][0] = r["dkv"][0].astype(BF16)
            edge_make(0)
            for side in range(2):
                edge_copy(0, side).start()

    loop(4, backward_block)

    inward = nn(r["act_t"][0, :, ROWS : 2 * ROWS], r["dq"][0]) + nn(r["act_t"][1, :, ROWS : 2 * ROWS], r["dq"][1])
    r["g3"][0:D, :] = inward[:, 0:BLOCK].astype(BF16)
    r["g3"][D:, :] = inward[:, BLOCK:].astype(BF16)
    pair_copy(3).start()
    r["dkvb"][1] = r["dkv"][1].astype(BF16)
    inward = nn(r["act_t"][0], r["dkvb"][0]) + nn(r["act_t"][1], r["dkvb"][1])
    r["g1"][0:D, :] = inward[:, 0:D].astype(BF16)
    r["g1"][D:, :] = inward[:, D:].astype(BF16)
    pair_copy(1).start()
    reduce_pair(3)
    reduce_plane(3)
    reduce_pair(1)
    reduce_plane(1)
    edge_make(1)
    for f in range(FR):
        r["fgw"][f] = nt(r["dq"][f], r["wv"][0, :, 0:D]) + nt(r["dkvb"][f, ROWS : 2 * ROWS, :], r["wv"][0, :, D:])
    reduce_middle(2)
    reduce_share(0)
    reduce_middle(3)
    reduce_middle(1)
    reduce_share(2)
    for side in range(2):
        edge_copy(1, side).start()
    reduce_share(3)
    reduce_share(1)
    for a in (0, 2):
        reduce_join(a)

    for f in range(FR):
        for side in range(2):
            edge_copy(f, side).wait_recv()
        act_grad = r["fgw"][f] + r["er"][f, 0].astype(F32) + r["er"][f, 1].astype(F32)
        r["fg"][f] = (r["mg"][f].astype(F32) + norm_back(act_grad, r["nrm"][f], r["rinv"][f])).astype(BF16)
    field_copy = pltpu.make_async_copy(r["fg"], fg_out, r["out_s"].at[4])
    field_copy.start()

    def mf_arrival(d, side):
        return remote(
            r["mfs"].at[d, :, in_part(side), :], mixed_out.at[:, side_rows(lax.rem(tm + d, ntm), side), :],
            r["mf_s"].at[side, d - 1], r["mf_r"].at[side, d - 1], (tm, sp),
        )

    for side in range(2):
        keep(side).wait()
        loop(ntm - 1, lambda i, side=side: mf_arrival(i + 1, side).wait_recv())
        loop(ntm - 1, lambda i, side=side: mf_copy(i + 1, side).wait_send())
        loop(ntm - 1, lambda i, side=side: mg_copy(i + 1, side).wait_send())
        loop(ntm - 1, lambda i, side=side: cot_copy(i + 1, side).wait_send())
    for f in range(FR):
        for side in range(2):
            loop(ntm - 1, lambda i, f=f, side=side: ms_copy(f, side, i + 1).wait_send())
        for side in range(2):
            edge_copy(f, side).wait_send()
        for item in halos(f):
            item.wait_send()
    reduce_drain(0)
    reduce_drain(2)

    for a in (0, 2):
        reduce_end(a)
    reduce_join(3)
    reduce_join(1)
    reduce_end(3)
    reduce_end(1)
    reduce_drain(3)
    reduce_drain(1)
    field_copy.wait()


def finish_kernel(factor, *refs):
    ins, outs = refs[:6], refs[6:10]
    held, made = refs[10:16], refs[16:18]
    in_sem, out_sem = refs[18:20]
    loads = [pltpu.make_async_copy(src, dst, in_sem.at[i]) for i, (src, dst) in enumerate(zip(ins, held))]
    order = (2, 4, 3, 5, 0, 1)
    for i in order:
        loads[i].start()
    fin0, fin1, fin2, fin3 = held[2:6]
    project, combine = made
    stores = [
        pltpu.make_async_copy(project.at[1], outs[2].at[1], out_sem.at[0]),
        pltpu.make_async_copy(combine, outs[3], out_sem.at[1]),
        pltpu.make_async_copy(project.at[0], outs[2].at[0], out_sem.at[2]),
        pltpu.make_async_copy(held[0], outs[0], out_sem.at[3]),
        pltpu.make_async_copy(held[1], outs[1], out_sem.at[4]),
    ]
    loads[2].wait()
    project[1, :, D:] = fin0[0:D, :].astype(F32) * factor
    project[1, :, 0:D] = fin0[D:, 0:D].astype(F32) * factor
    stores[0].start()
    combine[1] = fin0[D:, D:].astype(F32) * factor
    loads[4].wait()
    combine[0, :, 0:BLOCK] = fin2[0:D, :].astype(F32) * factor
    combine[0, :, BLOCK:] = fin2[D:, :].astype(F32) * factor
    stores[1].start()
    loads[3].wait()
    project[0, :, D : 2 * D] = fin1[0:D, :].astype(F32) * factor
    project[0, :, 2 * D :] = fin1[D:, :].astype(F32) * factor
    loads[5].wait()
    project[0, :, 0:BLOCK] = fin3[0:D, :].astype(F32) * factor
    project[0, :, BLOCK:D] = fin3[D:, :].astype(F32) * factor
    stores[2].start()
    for i in range(2):
        loads[i].wait()
        stores[3 + i].start()
    for item in stores:
        item.wait()


def per_device(ntm, nsp, wave_field, cotangent, block_lists, project_weights, combine_weights):
    shapes = scratch_shapes(ntm, nsp)
    names = tuple(shapes)
    anywhere = pl.BlockSpec(memory_space=pl.ANY)
    rows = jax.ShapeDtypeStruct((FR, ROWS, D), BF16)
    results = pl.pallas_call(
        functools.partial(step_kernel, ntm, nsp, names),
        out_shape=(rows, rows) + tuple(jax.ShapeDtypeStruct((512, lanes), BF16) for lanes in LANES),
        in_specs=[anywhere] * 5,
        out_specs=(anywhere,) * 6,
        scratch_shapes=list(shapes.values()),
        compiler_params=pltpu.CompilerParams(
            collective_id=0, has_side_effects=True, vmem_limit_bytes=LIMIT
        ),
        name="cuboid_step",
    )(block_lists, wave_field, cotangent, project_weights, combine_weights)
    factor = 1.0 / math.sqrt(FR * ntm * ROWS * nsp)
    return pl.pallas_call(
        functools.partial(finish_kernel, factor),
        out_shape=(
            rows,
            rows,
            jax.ShapeDtypeStruct((2, D, 3 * D), F32),
            jax.ShapeDtypeStruct((2, D, D), F32),
        ),
        in_specs=[anywhere] * 6,
        out_specs=(anywhere,) * 4,
        scratch_shapes=[pltpu.VMEM((FR, ROWS, D), BF16)] * 2
        + [pltpu.VMEM((512, lanes), BF16) for lanes in LANES]
        + [
            pltpu.VMEM((2, D, 3 * D), F32),
            pltpu.VMEM((2, D, D), F32),
            pltpu.SemaphoreType.DMA((6,)),
            pltpu.SemaphoreType.DMA((5,)),
        ],
        compiler_params=pltpu.CompilerParams(vmem_limit_bytes=LIMIT),
        name="finish",
    )(*results)


def solution(mesh):
    in_specs = (P("tm", "space", None), P("tm", "space", None), P("tm", "space", None), P(), P())
    out_specs = (P("tm", "space", None), P("tm", "space", None), P(), P())
    return jax.shard_map(
        functools.partial(per_device, mesh.shape["tm"], mesh.shape["space"]),
        mesh=mesh,
        in_specs=in_specs,
        out_specs=out_specs,
        check_vma=False,
    )
```

```python
import functools
import math

import jax
import jax.numpy as jnp
from jax import lax
from jax.experimental import pallas as pl
from jax.experimental.pallas import tpu as pltpu
from jax.sharding import PartitionSpec as P

HEADS = 8
BLOCK = 128
SPAN = 5
KEYS = SPAN * BLOCK
D = 256
HD = 32
ROWS = 256
FR = 2
GROUPS = 4
CORES = 4
EPS = 1e-05
NEG = -1e30
PADS = 80
LIMIT = 60 * 1024 * 1024
LANES = (512, 256, 128, 128)
SCALE = 1.0 / math.sqrt(HD)
SCALE2 = SCALE * math.log2(math.e)

MESH = pl.DeviceIdType.MESH
F32 = jnp.float32
BF16 = jnp.bfloat16


def nn(left, right):
    return jnp.dot(left, right, preferred_element_type=F32)


def nt(left, right):
    return lax.dot_general(left, right, (((1,), (1,)), ((), ())), preferred_element_type=F32)


def norm(rows):
    centered = rows - jnp.mean(rows, axis=-1, keepdims=True)
    inverse = lax.rsqrt(jnp.mean(centered * centered, axis=-1, keepdims=True) + EPS)
    return centered * inverse, inverse


def norm_back(upstream, normed, inverse):
    mean_grad = jnp.mean(upstream, axis=-1, keepdims=True)
    mean_cross = jnp.mean(upstream * normed, axis=-1, keepdims=True)
    return inverse * (upstream - mean_grad - normed * mean_cross)


def diag(pair):
    return jnp.concatenate([pair[0:HD, 0:BLOCK], pair[HD : 2 * HD, BLOCK : 2 * BLOCK]], axis=0)


def head_sums(prod):
    return jnp.sum(prod.reshape(HEADS, HD, BLOCK), axis=1)


def scratch_shapes(ntm, nsp):
    nz = nsp // CORES
    npl = ntm * 2
    part = ROWS // ntm
    chunk = 256 // npl
    dma = pltpu.SemaphoreType.DMA
    vm = pltpu.VMEM
    return dict(
        xe=vm((3, FR, ROWS, D), BF16),
        act=vm((3, FR, ROWS, D), BF16),
        act_t=vm((FR, D, 3 * ROWS), BF16),
        nrm=vm((FR, ROWS, D), F32),
        rinv=vm((FR, ROWS, 1), F32),
        wv=vm((2, D, 3 * D), BF16),
        cv=vm((2, D, D), BF16),
        wt=vm((2, 2 * D, D), BF16),
        hm=vm((HEADS, BLOCK, D), BF16),
        q=vm((FR, ROWS, D), BF16),
        kv=vm((FR, 3 * ROWS, 2 * D), BF16),
        kt=vm((FR, D, 3 * ROWS), BF16),
        vt=vm((FR, HEADS // 2, PADS, 3 * ROWS), BF16),
        qs=vm((4, HEADS * BLOCK, D), BF16),
        dos=vm((4, HEADS * BLOCK, D), BF16),
        share=vm((4, HEADS, BLOCK), F32),
        delta=vm((4, HEADS, BLOCK), F32),
        probs=vm((4, KEYS, HEADS * BLOCK), BF16),
        ds=vm((KEYS, HEADS * BLOCK), BF16),
        s=vm((4, KEYS, 2 * BLOCK), F32),
        ot=vm((4, D, BLOCK), F32),
        otb=vm((D, 4 * BLOCK), BF16),
        att=vm((FR, ROWS, D), BF16),
        ms=vm((FR, ROWS, D), BF16),
        hist=vm((ntm, FR, part, D), BF16),
        hcot=vm((ntm, FR, part, D), BF16),
        xt=vm((GROUPS, BLOCK, D), F32),
        ct=vm((GROUPS, BLOCK, D), F32),
        tb=vm((BLOCK, 2 * BLOCK), F32),
        tnrm=vm((GROUPS * BLOCK, D), F32),
        trinv=vm((GROUPS * BLOCK, 1), F32),
        tact=vm((GROUPS * BLOCK, D), BF16),
        tp=vm((GROUPS * BLOCK, 3 * D), BF16),
        tkvt=vm((2 * D, GROUPS * BLOCK), BF16),
        tdo=vm((GROUPS * BLOCK, D), BF16),
        tdot=vm((D, GROUPS * BLOCK), BF16),
        tot=vm((D, GROUPS * BLOCK), BF16),
        tatt=vm((GROUPS * BLOCK, D), BF16),
        tdp=vm((GROUPS * BLOCK, 3 * D), BF16),
        tqs=vm((GROUPS, HEADS * BLOCK, D), BF16),
        tdos=vm((GROUPS, HEADS * BLOCK, D), BF16),
        tprobs=vm((GROUPS, BLOCK, HEADS * BLOCK), BF16),
        tds=vm((GROUPS, BLOCK, HEADS * BLOCK), BF16),
        tmix=vm((GROUPS, BLOCK, D), F32),
        tmf=vm((GROUPS, BLOCK, D), F32),
        mfs=vm((ntm, FR, part, D), BF16),
        mgs=vm((ntm, FR, part, D), BF16),
        mg=vm((FR, ROWS, D), BF16),
        dq=vm((FR, ROWS, D), BF16),
        dkv=vm((FR, 3 * ROWS, 2 * D), F32),
        dkvb=vm((FR, 3 * ROWS, 2 * D), BF16),
        eg=vm((FR, 2, ROWS, D), BF16),
        er=vm((FR, 2, ROWS, D), BF16),
        fg=vm((FR, ROWS, D), BF16),
        fgw=vm((FR, ROWS, D), F32),
        **{
            name + str(a): vm(shape + (lanes,), BF16)
            for a, lanes in enumerate(LANES)
            for name, shape in (
                ("g", (512,)),
                ("pr", (256,)),
                ("h", (256,)),
                ("rs", (npl - 1, chunk)),
                ("zb", (nz, chunk)),
                ("fin", (chunk,)),
            )
        },
        lists=pltpu.SMEM((FR, 2, 4), jnp.int32),
        ld_sem=dma((8,)),
        own_sem=dma((2, 2)),
        halo_s=dma((FR, 2)),
        halo_r=dma((FR, 2)),
        cot_s=dma((2, ntm - 1)),
        cot_r=dma((2, ntm - 1)),
        ms_s=dma((2, FR, ntm - 1)),
        ms_r=dma((2, FR, ntm - 1)),
        mf_s=dma((2, ntm - 1)),
        mf_r=dma((2, ntm - 1)),
        mg_s=dma((2, ntm - 1)),
        mg_r=dma((2, ntm - 1)),
        ed_s=dma((FR, 2)),
        ed_r=dma((FR, 2)),
        pr_s=dma((4,)),
        pr_r=dma((4,)),
        pg_s=dma((4,)),
        pg_r=dma((4,)),
        out_s=dma((5,)),
        rs_s=dma((4,)),
        rs_r=dma((4,)),
        z_s=dma((4,)),
        z_r=dma((4,)),
        col_s=dma((1,)),
        col_r=dma((1,)),
        ag_s=dma((4,)),
        ag_r=dma((4,)),
    )


def step_kernel(ntm, nsp, names, lists_hbm, x_hbm, cot_hbm, w_hbm, c_hbm, mixed_out, fg_out, fin0_out, fin1_out, fin2_out, fin3_out, *refs):
    r = dict(zip(names, refs))
    nz = nsp // CORES
    npl = ntm * 2
    hp = ROWS // ntm // 2
    chunk = 256 // npl
    frames = FR * ntm
    per = BLOCK // frames

    tm = lax.axis_index("tm")
    sp = lax.axis_index("space")
    z = lax.div(sp, CORES)
    quarter = lax.rem(sp, CORES)
    core = lax.rem(sp, 2)
    partner = sp + 1 - 2 * core
    left = lax.rem(sp + (nsp - 1), nsp)
    right = lax.rem(sp + 1, nsp)
    place = tm * 2 + lax.div(quarter, 2)

    def plane_peer(d):
        other = lax.rem(place + d, npl)
        return (lax.div(other, 2), z * CORES + lax.rem(other, 2) * 2 + core), other

    def z_peer(d):
        return (tm, lax.rem(z + d, nz) * CORES + quarter)

    def remote(src, dst, send, recv, device):
        return pltpu.make_async_remote_copy(
            src_ref=src, dst_ref=dst, send_sem=send, recv_sem=recv, device_id=device, device_id_type=MESH
        )

    def loop(count, body):
        def wrapped(i, carry):
            body(i)
            return carry

        lax.fori_loop(0, count, wrapped, 0)

    barrier = pltpu.get_barrier_semaphore()
    pl.semaphore_signal(barrier, inc=1, device_id=(tm, left), device_id_type=MESH)
    pl.semaphore_signal(barrier, inc=1, device_id=(tm, right), device_id_type=MESH)
    loop(npl - 1, lambda i: pl.semaphore_signal(barrier, inc=1, device_id=plane_peer(i + 1)[0], device_id_type=MESH))
    loop(nz - 1, lambda i: pl.semaphore_signal(barrier, inc=1, device_id=z_peer(i + 1), device_id_type=MESH))

    ld = r["ld_sem"]

    def side_rows(device, side):
        return pl.ds(pl.multiple_of(side * BLOCK + device * hp, hp), hp)

    def in_part(side):
        return pl.ds(side * hp, hp)

    loads = [
        pltpu.make_async_copy(w_hbm.at[0], r["wv"].at[0], ld.at[0]),
        pltpu.make_async_copy(x_hbm.at[0], r["xe"].at[1, 0], ld.at[1]),
        pltpu.make_async_copy(c_hbm, r["cv"], ld.at[2]),
        pltpu.make_async_copy(w_hbm.at[1], r["wv"].at[1], ld.at[3]),
        pltpu.make_async_copy(
            cot_hbm.at[:, side_rows(tm, 0), :], r["hcot"].at[0, :, in_part(0), :], r["own_sem"].at[0, 0]
        ),
        pltpu.make_async_copy(x_hbm.at[1], r["xe"].at[1, 1], ld.at[6]),
        pltpu.make_async_copy(lists_hbm, r["lists"], ld.at[7]),
        pltpu.make_async_copy(
            cot_hbm.at[:, side_rows(tm, 1), :], r["hcot"].at[0, :, in_part(1), :], r["own_sem"].at[0, 1]
        ),
    ]
    for item in loads:
        item.start()

    lane_head = lax.broadcasted_iota(jnp.int32, (BLOCK, D), 1) // HD
    for h in range(HEADS):
        r["hm"][h] = jnp.where(lane_head == h, 1.0, 0.0).astype(BF16)
    key_pos = lax.broadcasted_iota(jnp.int32, (BLOCK, 2 * BLOCK), 0) % per
    query_pos = lax.broadcasted_iota(jnp.int32, (BLOCK, 2 * BLOCK), 1) % per
    r["tb"][...] = jnp.where(key_pos == query_pos, 0.0, NEG)

    r["vt"][:, :, 2 * HD :, :] = jnp.ones((FR, HEADS // 2, PADS - 2 * HD, 3 * ROWS), BF16)

    loads[0].wait()
    r["wt"][0] = r["wv"][0, :, D:].astype(F32).T.astype(BF16)

    pl.semaphore_wait(barrier, 2 + (npl - 1) + (nz - 1))

    def halos(f):
        return [
            remote(x_hbm.at[f], r["xe"].at[2, f], r["halo_s"].at[f, 0], r["halo_r"].at[f, 0], (tm, left)),
            remote(x_hbm.at[f], r["xe"].at[0, f], r["halo_s"].at[f, 1], r["halo_r"].at[f, 1], (tm, right)),
        ]

    for f in range(FR):
        for item in halos(f):
            item.start()

    def cot_copy(d, side):
        to = lax.rem(tm + d, ntm)
        return remote(
            cot_hbm.at[:, side_rows(to, side), :], r["hcot"].at[d, :, in_part(side), :], r["cot_s"].at[side, d - 1],
            r["cot_r"].at[side, d - 1], (to, sp),
        )

    def project(slot, f):
        normed, inverse = norm(r["xe"][slot, f].astype(F32))
        rows = slice(slot * ROWS, (slot + 1) * ROWS)
        act = normed.astype(BF16)
        r["act"][slot, f] = act
        if slot == 1:
            r["nrm"][f] = normed
            r["rinv"][f] = inverse
            r["q"][f] = nn(act, r["wv"][0, :, 0:D]).astype(BF16)
        r["kv"][f, rows, :] = nn(act, r["wv"][0, :, D:]).astype(BF16)
        turned = nt(r["wt"][0], act).astype(BF16)
        r["kt"][f, :, rows] = turned[0:D]
        for pair in range(HEADS // 2):
            r["vt"][f, pair, 0 : 2 * HD, rows] = turned[D + pair * 2 * HD : D + (pair + 1) * 2 * HD]

    loads[1].wait()
    project(1, 0)
    loads[5].wait()
    project(1, 1)
    for f in range(FR):
        for j in range(2):
            for h in range(HEADS):
                r["qs"][2 * f + j, h * BLOCK : (h + 1) * BLOCK, :] = (
                    r["q"][f, j * BLOCK : (j + 1) * BLOCK, :] * r["hm"][h]
                )

    def key_rows(j):
        return pl.ds(pl.multiple_of(j * BLOCK, BLOCK), KEYS)

    def biases(f, j):
        out = []
        first = sp * 2 + j - 2
        for e in range(SPAN):
            count = jnp.int32(0)
            for k in range(4):
                count = count + jnp.where(r["lists"][f, j, k] == first + e, 1, 0)
            out.append(
                jnp.where(
                    count == 0,
                    NEG,
                    jnp.where(count == 1, 0.0, jnp.where(count == 2, 1.0, jnp.where(count == 3, math.log2(3.0), 2.0))),
                ).astype(F32)
            )
        return out

    def forward_block(f, j):
        i = 2 * f + j
        rows = key_rows(j)
        bias = biases(f, j)
        outs = []

        def scores(pair):
            cols = slice(pair * 2 * BLOCK, (pair + 1) * 2 * BLOCK)
            r["s"][pair] = nt(r["kv"][f, rows, 0:D], r["qs"][i, cols, :])

        scores(0)
        for pair in range(HEADS // 2):
            cols = slice(pair * 2 * BLOCK, (pair + 1) * 2 * BLOCK)
            if pair + 1 < HEADS // 2:
                scores(pair + 1)
            s = r["s"].at[pair]
            top = None
            for e in range(SPAN):
                here = jnp.max(s[e * BLOCK : (e + 1) * BLOCK, :], axis=0, keepdims=True) * SCALE2 + bias[e]
                top = here if top is None else jnp.maximum(top, here)
            for e in range(SPAN):
                block = slice(e * BLOCK, (e + 1) * BLOCK)
                r["probs"][i, block, cols] = jnp.exp2(s[block, :] * SCALE2 + (bias[e] - top)).astype(BF16)
            both = nn(r["vt"][f, pair, :, rows], r["probs"][i, :, cols])
            share = 1.0 / both[2 * HD : 2 * HD + 1, :]
            r["share"][i, 2 * pair : 2 * pair + 1, :] = share[:, 0:BLOCK]
            r["share"][i, 2 * pair + 1 : 2 * pair + 2, :] = share[:, BLOCK:]
            outs.append(diag(both[0 : 2 * HD] * share))
        out = jnp.concatenate(outs, axis=0)
        r["ot"][i] = out
        r["otb"][:, pl.ds(pl.multiple_of(i * BLOCK, BLOCK), BLOCK)] = out.astype(BF16)
        r["att"][f, pl.ds(pl.multiple_of(j * BLOCK, BLOCK), BLOCK), :] = out.T.astype(BF16)

    def ms_copy(f, side, d):
        to = lax.rem(tm + d, ntm)
        return remote(
            r["ms"].at[f, side_rows(to, side), :],
            r["hist"].at[d, f, pl.ds(pl.multiple_of(side * hp, hp), hp), :],
            r["ms_s"].at[side, f, d - 1],
            r["ms_r"].at[side, f, d - 1],
            (to, sp),
        )

    loads[3].wait()
    r["wt"][1] = r["wv"][1, :, D:].astype(F32).T.astype(BF16)
    loads[2].wait()
    loads[6].wait()

    def forward(o):
        f = lax.rem(o, FR)
        j = lax.div(o, FR)

        @pl.when(j == 0)
        def _():
            for item in halos(f):
                item.wait_recv()

        @pl.when(o == FR - 1)
        def _():
            for side in range(2):
                loop(ntm - 1, lambda i, side=side: cot_copy(i + 1, side).start())

        @pl.when(j == 0)
        def _():
            project(2, f)
            project(0, f)

        forward_block(f, j)
        rows = pl.ds(pl.multiple_of(j * BLOCK, BLOCK), BLOCK)
        mixed = r["xe"][1, f, rows, :].astype(F32) + nn(r["att"][f, rows, :], r["cv"][0])
        r["ms"][f, rows, :] = mixed.astype(BF16)
        loop(ntm - 1, lambda i: ms_copy(f, j, i + 1).start())
        r["hist"][0, f, pl.ds(pl.multiple_of(j * hp, hp), hp), :] = r["ms"][f, side_rows(tm, j), :]

    loop(2 * FR, forward)

    def ungroup(src, dst, side):
        for d in range(ntm):
            for f in range(FR):
                frame = d * FR + f
                dst[d, f, side * 2 * per : (side + 1) * 2 * per, :] = jnp.concatenate(
                    [src[g, frame * per : (frame + 1) * per, :] for g in (2 * side, 2 * side + 1)], axis=0
                ).astype(BF16)

    def time_inputs(side):
        mine = slice(side * hp, (side + 1) * hp)
        groups = (2 * side, 2 * side + 1)
        loads[(4, 7)[side]].wait()
        loop(ntm - 1, lambda i: cot_copy(i + 1, side).wait_recv())
        for d in range(ntm):
            for f in range(FR):
                frame = d * FR + f
                block = r["hcot"][d, f, mine, :].astype(F32)
                for k, g in enumerate(groups):
                    r["ct"][g, frame * per : (frame + 1) * per, :] = block[k * per : (k + 1) * per]
        for g in groups:
            rows = slice(g * BLOCK, (g + 1) * BLOCK)
            cot = r["ct"][g].astype(BF16)
            grad = nt(cot, r["cv"][1]).astype(BF16)
            for h in range(HEADS):
                r["tdos"][g, h * BLOCK : (h + 1) * BLOCK, :] = grad * r["hm"][h]
            r["tdot"][:, rows] = nt(r["cv"][1], cot).astype(BF16)
        for f in range(FR):
            loop(ntm - 1, lambda i, f=f: ms_copy(f, side, i + 1).wait_recv())
            for d in range(ntm):
                frame = d * FR + f
                block = r["hist"][d, f, mine, :].astype(F32)
                normed, inverse = norm(block)
                for k, g in enumerate(groups):
                    to = slice(frame * per, (frame + 1) * per)
                    at = slice(g * BLOCK + frame * per, g * BLOCK + (frame + 1) * per)
                    piece = slice(k * per, (k + 1) * per)
                    r["xt"][g, to, :] = block[piece]
                    r["tnrm"][at, :] = normed[piece]
                    r["trinv"][at, :] = inverse[piece]
        rows = slice(side * 2 * BLOCK, (side + 1) * 2 * BLOCK)
        r["tact"][rows, :] = r["tnrm"][rows, :].astype(BF16)
        r["tp"][rows, :] = nn(r["tact"][rows, :], r["wv"][1]).astype(BF16)
        r["tkvt"][:, rows] = nt(r["wt"][1], r["tact"][rows, :]).astype(BF16)

    def time_scores(g):
        rows = slice(g * BLOCK, (g + 1) * BLOCK)
        query = r["tp"][rows, 0:D]
        for h in range(HEADS):
            r["tqs"][g, h * BLOCK : (h + 1) * BLOCK, :] = query * r["hm"][h]
        for pair in range(HEADS // 2):
            cols = slice(pair * 2 * BLOCK, (pair + 1) * 2 * BLOCK)
            scores = nt(r["tp"][rows, D : 2 * D], r["tqs"][g, cols, :]) * SCALE2 + r["tb"][...]
            grown = jnp.exp2(scores - jnp.max(scores, axis=0, keepdims=True))
            share = 1.0 / jnp.sum(grown, axis=0, keepdims=True)
            r["tprobs"][g, :, cols] = (grown * share).astype(BF16)

    def time_out(g):
        rows = slice(g * BLOCK, (g + 1) * BLOCK)
        outs = []
        for pair in range(HEADS // 2):
            cols = slice(pair * 2 * BLOCK, (pair + 1) * 2 * BLOCK)
            values = r["tkvt"][D + pair * 2 * HD : D + (pair + 1) * 2 * HD, rows]
            outs.append(diag(nn(values, r["tprobs"][g, :, cols])))
        out = jnp.concatenate(outs, axis=0)
        r["tot"][:, rows] = out.astype(BF16)
        r["tatt"][rows, :] = out.T.astype(BF16)
        delta = head_sums(out * r["tdot"][:, rows].astype(F32))
        for pair in range(HEADS // 2):
            cols = slice(pair * 2 * BLOCK, (pair + 1) * 2 * BLOCK)
            dprob = nt(r["tp"][rows, 2 * D :], r["tdos"][g, cols, :])
            shift = jnp.concatenate([delta[2 * pair : 2 * pair + 1], delta[2 * pair + 1 : 2 * pair + 2]], axis=1)
            r["tds"][g, :, cols] = (r["tprobs"][g, :, cols].astype(F32) * (dprob - shift)).astype(BF16)

    def time_grads(g):
        rows = slice(g * BLOCK, (g + 1) * BLOCK)
        outs = []
        for pair in range(HEADS // 2):
            cols = slice(pair * 2 * BLOCK, (pair + 1) * 2 * BLOCK)
            outs.append(diag(nn(r["tkvt"][pair * 2 * HD : (pair + 1) * 2 * HD, rows], r["tds"][g, :, cols])))
        r["tdp"][rows, 0:D] = (jnp.concatenate(outs, axis=0) * SCALE).T.astype(BF16)
        r["tdp"][rows, D : 2 * D] = (nn(r["tds"][g], r["tqs"][g]) * SCALE).astype(BF16)
        r["tdp"][rows, 2 * D : 3 * D] = nn(r["tprobs"][g], r["tdos"][g]).astype(BF16)

    def mg_copy(d, side):
        return remote(
            r["mgs"].at[d, :, in_part(side), :], r["mg"].at[:, side_rows(tm, side), :], r["mg_s"].at[side, d - 1],
            r["mg_r"].at[side, d - 1], (lax.rem(tm + (ntm - d), ntm), sp),
        )

    def mf_copy(d, side):
        return remote(
            r["mfs"].at[d, :, in_part(side), :], mixed_out.at[:, side_rows(tm, side), :], r["mf_s"].at[side, d - 1],
            r["mf_r"].at[side, d - 1], (lax.rem(tm + (ntm - d), ntm), sp),
        )

    def keep(side):
        return pltpu.make_async_copy(
            r["mfs"].at[0, :, in_part(side), :], mixed_out.at[:, side_rows(tm, side), :], r["own_sem"].at[1, side]
        )

    for side in range(2):
        groups = (2 * side, 2 * side + 1)
        time_inputs(side)
        for g in groups:
            time_scores(g)
        for g in groups:
            time_out(g)
        for g in groups:
            time_grads(g)
        for g in groups:
            rows = slice(g * BLOCK, (g + 1) * BLOCK)
            act_grad = nt(r["tdp"][rows, :], r["wv"][1])
            r["tmix"][g] = r["ct"][g] + norm_back(act_grad, r["tnrm"][rows, :], r["trinv"][rows, :])
        ungroup(r["tmix"], r["mgs"], side)
        loop(ntm - 1, lambda i, side=side: mg_copy(i + 1, side).start())
        r["mg"][:, side_rows(tm, side), :] = r["mgs"][0, :, side * hp : (side + 1) * hp, :]

    turned = r["tact"][...].astype(F32).T.astype(BF16)
    r["g0"][0:D, :] = nn(turned, r["tdp"][:, D:]).astype(BF16)
    r["g0"][D:, 0:D] = nn(turned, r["tdp"][:, 0:D]).astype(BF16)
    cots = r["ct"][...].reshape(GROUPS * BLOCK, D).astype(BF16)
    r["g0"][D:, D:] = nn(r["tot"][...], cots).astype(BF16)

    my_half = pl.ds(pl.multiple_of(core * 256, 256), 256)
    other_half = pl.ds(pl.multiple_of((1 - core) * 256, 256), 256)
    in_half = pl.ds(pl.multiple_of(place * chunk, chunk), chunk)
    my_chunk = pl.ds(pl.multiple_of(core * 256 + place * chunk, chunk), chunk)

    def pair_copy(a):
        return remote(r["g" + str(a)].at[other_half, :], r["pr" + str(a)], r["pr_s"].at[a], r["pr_r"].at[a], (tm, partner))

    def rs_copy(a, d):
        device, other = plane_peer(d)
        rows = pl.ds(pl.multiple_of(other * chunk, chunk), chunk)
        return remote(r["h" + str(a)].at[rows, :], r["rs" + str(a)].at[d - 1], r["rs_s"].at[a], r["rs_r"].at[a], device)

    def z_copy(a, d):
        return remote(r["zb" + str(a)].at[z], r["zb" + str(a)].at[z], r["z_s"].at[a], r["z_r"].at[a], z_peer(d))

    outs = (fin0_out, fin1_out, fin2_out, fin3_out)

    def ag_copy(a, d):
        device, _ = plane_peer(d)
        return remote(r["fin" + str(a)], outs[a].at[my_chunk, :], r["ag_s"].at[a], r["ag_r"].at[a], device)

    along = lax.rem(place, 4)
    line = lax.div(place, 4)
    lines = npl // 4
    my_line = pl.ds(pl.multiple_of(core * 256 + line * 4 * chunk, 4 * chunk), 4 * chunk)

    def place_device(other):
        return (lax.div(other, 2), z * CORES + lax.rem(other, 2) * 2 + core)

    def row_copy(d):
        device = place_device(line * 4 + lax.rem(along + d, 4))
        return remote(r["fin0"], outs[0].at[my_chunk, :], r["ag_s"].at[0], r["ag_r"].at[0], device)

    def col_copy(d):
        device = place_device(lax.rem(line + d, lines) * 4 + along)
        return remote(
            outs[0].at[my_line, :], outs[0].at[my_line, :], r["col_s"].at[0], r["col_r"].at[0], device
        )

    def share_rows():
        drain(r["zb0"].at[0 : nz - 1], r["z_r"].at[0])
        total = r["zb0"][0].astype(F32)
        for k in range(1, nz):
            total = total + r["zb0"][k].astype(F32)
        r["fin0"][...] = total.astype(BF16)
        fin_copy(0).start()
        loop(3, lambda i: row_copy(i + 1).start())

    def share_columns():
        fin_copy(0).wait()
        drain(outs[0].at[0 : 3 * chunk, :], r["ag_r"].at[0])
        loop(lines - 1, lambda i: col_copy(i + 1).start())

    def join_columns():
        drain(outs[0].at[0 : (lines - 1) * 4 * chunk, :], r["col_r"].at[0])
        join_copy(0).start()

    def fin_copy(a):
        return pltpu.make_async_copy(r["fin" + str(a)], outs[a].at[my_chunk, :], r["out_s"].at[a])

    def join_copy(a):
        return remote(outs[a].at[my_half, :], outs[a].at[my_half, :], r["pg_s"].at[a], r["pg_r"].at[a], (tm, partner))

    def drain(ref, sem):
        pltpu.make_async_copy(ref, ref, sem).wait()

    def reduce_pair(a):
        pair_copy(a).wait_recv()
        r["h" + str(a)][...] = (r["g" + str(a)][my_half, :].astype(F32) + r["pr" + str(a)][...].astype(F32)).astype(BF16)

    def reduce_plane(a):
        loop(npl - 1, lambda i: rs_copy(a, i + 1).start())

    def reduce_middle(a):
        drain(r["rs" + str(a)], r["rs_r"].at[a])
        total = r["h" + str(a)][in_half, :].astype(F32)
        for d in range(npl - 1):
            total = total + r["rs" + str(a)][d].astype(F32)
        r["zb" + str(a)][z] = total.astype(BF16)
        loop(nz - 1, lambda i: z_copy(a, i + 1).start())

    def reduce_share(a):
        drain(r["zb" + str(a)].at[0 : nz - 1], r["z_r"].at[a])
        total = r["zb" + str(a)][0].astype(F32)
        for k in range(1, nz):
            total = total + r["zb" + str(a)][k].astype(F32)
        r["fin" + str(a)][...] = total.astype(BF16)
        fin_copy(a).start()
        loop(npl - 1, lambda i: ag_copy(a, i + 1).start())

    def reduce_join(a):
        fin_copy(a).wait()
        drain(outs[a].at[0 : (npl - 1) * chunk, :], r["ag_r"].at[a])
        join_copy(a).start()

    def reduce_end(a):
        join_copy(a).wait_recv()

    def reduce_drain(a):
        pair_copy(a).wait_send()
        drain(r["rs" + str(a)], r["rs_s"].at[a])
        drain(r["zb" + str(a)].at[0 : nz - 1], r["z_s"].at[a])
        if a == 0:
            drain(outs[0].at[0 : 3 * chunk, :], r["ag_s"].at[0])
            drain(outs[0].at[0 : (lines - 1) * 4 * chunk, :], r["col_s"].at[0])
        else:
            drain(outs[a].at[0 : (npl - 1) * chunk, :], r["ag_s"].at[a])
        join_copy(a).wait_send()

    pair_copy(0).start()

    r["dkv"][...] = jnp.zeros_like(r["dkv"])

    for g in range(GROUPS):
        rows = slice(g * BLOCK, (g + 1) * BLOCK)
        r["tmf"][g] = r["xt"][g] + nn(r["tatt"][rows, :], r["cv"][1])
    for side in range(2):
        ungroup(r["tmf"], r["mfs"], side)
        keep(side).start()
    for f in range(FR):
        for slot in range(3):
            r["act_t"][f, :, slot * ROWS : (slot + 1) * ROWS] = r["act"][slot, f].astype(F32).T.astype(BF16)

    def mg_arrival(d, side):
        return remote(
            r["mgs"].at[d, :, in_part(side), :], r["mg"].at[:, side_rows(lax.rem(tm + d, ntm), side), :],
            r["mg_s"].at[side, d - 1], r["mg_r"].at[side, d - 1], (tm, sp),
        )

    def grads_in(j):
        loop(ntm - 1, lambda k: mg_arrival(k + 1, j).wait_recv())
        for f in range(FR):
            i = 2 * f + j
            turned = nt(r["cv"][0], r["mg"][f, j * BLOCK : (j + 1) * BLOCK, :])
            share = jnp.broadcast_to(r["share"][i][:, None, :], (HEADS, HD, BLOCK)).reshape(D, BLOCK)
            turned = turned * share
            r["delta"][i] = head_sums(r["ot"][i] * turned.astype(BF16).astype(F32))
            grad = turned.T.astype(BF16)
            for h in range(HEADS):
                r["dos"][i, h * BLOCK : (h + 1) * BLOCK, :] = grad * r["hm"][h]

    reduce_pair(0)
    reduce_plane(0)
    for side in range(2):
        loop(ntm - 1, lambda k, side=side: mf_copy(k + 1, side).start())
    grads_in(0)

    def edge_copy(f, side):
        return remote(
            r["eg"].at[f, side], r["er"].at[f, 1 - side], r["ed_s"].at[f, side], r["ed_r"].at[f, side],
            (tm, right if side else left),
        )

    def edge_make(f):
        for side in range(2):
            rows = slice(2 * ROWS * side, 2 * ROWS * side + ROWS)
            r["eg"][f, side] = nt(r["dkvb"][f, rows, :], r["wv"][0, :, D:]).astype(BF16)

    def backward_block(o):
        f = lax.rem(o, FR)
        j = lax.div(o, FR)
        i = 2 * f + j
        rows = key_rows(j)
        mine = pl.ds(pl.multiple_of(j * BLOCK, BLOCK), BLOCK)
        delta = r["delta"][i]
        outs = []

        def grads(pair):
            cols = slice(pair * 2 * BLOCK, (pair + 1) * 2 * BLOCK)
            r["s"][pair] = nt(r["kv"][f, rows, D:], r["dos"][i, cols, :])

        grads(0)
        r["dkv"][f, rows, D:] += nn(r["probs"][i], r["dos"][i])
        for pair in range(HEADS // 2):
            cols = slice(pair * 2 * BLOCK, (pair + 1) * 2 * BLOCK)
            s = r["s"].at[pair]
            if pair + 1 < HEADS // 2:
                grads(pair + 1)
            shift = jnp.concatenate([delta[2 * pair : 2 * pair + 1], delta[2 * pair + 1 : 2 * pair + 2]], axis=1)
            for e in range(SPAN):
                block = slice(e * BLOCK, (e + 1) * BLOCK)
                r["ds"][block, cols] = (r["probs"][i, block, cols].astype(F32) * (s[block, :] - shift)).astype(BF16)
            outs.append(diag(nn(r["kt"][f, pair * 2 * HD : (pair + 1) * 2 * HD, rows], r["ds"][:, cols])))
        r["dq"][f, mine, :] = (jnp.concatenate(outs, axis=0) * SCALE).T.astype(BF16)
        r["dkv"][f, rows, 0:D] += nn(r["ds"][...], r["qs"][i]) * SCALE

        @pl.when(o == 1)
        def _():
            grads_in(1)
            outward = nn(r["otb"][:, 0:ROWS], r["mg"][0]) + nn(r["otb"][:, ROWS:], r["mg"][1])
            r["g2"][0:D, :] = outward[:, 0:BLOCK].astype(BF16)
            r["g2"][D:, :] = outward[:, BLOCK:].astype(BF16)
            pair_copy(2).start()

        @pl.when(o == 2)
        def _():
            reduce_middle(0)
            reduce_pair(2)
            reduce_plane(2)
            r["dkvb"][0] = r["dkv"][0].astype(BF16)
            edge_make(0)
            for side in range(2):
                edge_copy(0, side).start()

    loop(4, backward_block)

    inward = nn(r["act_t"][0, :, ROWS : 2 * ROWS], r["dq"][0]) + nn(r["act_t"][1, :, ROWS : 2 * ROWS], r["dq"][1])
    r["g3"][0:D, :] = inward[:, 0:BLOCK].astype(BF16)
    r["g3"][D:, :] = inward[:, BLOCK:].astype(BF16)
    pair_copy(3).start()
    r["dkvb"][1] = r["dkv"][1].astype(BF16)
    inward = nn(r["act_t"][0], r["dkvb"][0]) + nn(r["act_t"][1], r["dkvb"][1])
    r["g1"][0:D, :] = inward[:, 0:D].astype(BF16)
    r["g1"][D:, :] = inward[:, D:].astype(BF16)
    pair_copy(1).start()
    reduce_pair(3)
    reduce_plane(3)
    reduce_pair(1)
    reduce_plane(1)
    edge_make(1)
    for f in range(FR):
        r["fgw"][f] = nt(r["dq"][f], r["wv"][0, :, 0:D]) + nt(r["dkvb"][f, ROWS : 2 * ROWS, :], r["wv"][0, :, D:])
    reduce_middle(2)
    share_rows()
    reduce_middle(3)
    reduce_middle(1)
    share_columns()
    reduce_share(2)
    for side in range(2):
        edge_copy(1, side).start()
    reduce_share(3)
    reduce_share(1)
    join_columns()
    reduce_join(2)

    for f in range(FR):
        for side in range(2):
            edge_copy(f, side).wait_recv()
        act_grad = r["fgw"][f] + r["er"][f, 0].astype(F32) + r["er"][f, 1].astype(F32)
        r["fg"][f] = (r["mg"][f].astype(F32) + norm_back(act_grad, r["nrm"][f], r["rinv"][f])).astype(BF16)
    field_copy = pltpu.make_async_copy(r["fg"], fg_out, r["out_s"].at[4])
    field_copy.start()

    def mf_arrival(d, side):
        return remote(
            r["mfs"].at[d, :, in_part(side), :], mixed_out.at[:, side_rows(lax.rem(tm + d, ntm), side), :],
            r["mf_s"].at[side, d - 1], r["mf_r"].at[side, d - 1], (tm, sp),
        )

    for side in range(2):
        keep(side).wait()
        loop(ntm - 1, lambda i, side=side: mf_arrival(i + 1, side).wait_recv())
        loop(ntm - 1, lambda i, side=side: mf_copy(i + 1, side).wait_send())
        loop(ntm - 1, lambda i, side=side: mg_copy(i + 1, side).wait_send())
        loop(ntm - 1, lambda i, side=side: cot_copy(i + 1, side).wait_send())
    for f in range(FR):
        for side in range(2):
            loop(ntm - 1, lambda i, f=f, side=side: ms_copy(f, side, i + 1).wait_send())
        for side in range(2):
            edge_copy(f, side).wait_send()
        for item in halos(f):
            item.wait_send()
    reduce_drain(0)
    reduce_drain(2)

    for a in (0, 2):
        reduce_end(a)
    reduce_join(3)
    reduce_join(1)
    reduce_end(3)
    reduce_end(1)
    reduce_drain(3)
    reduce_drain(1)
    field_copy.wait()


def finish_kernel(factor, *refs):
    ins, outs = refs[:6], refs[6:10]
    held, made = refs[10:16], refs[16:18]
    in_sem, out_sem = refs[18:20]
    loads = [pltpu.make_async_copy(src, dst, in_sem.at[i]) for i, (src, dst) in enumerate(zip(ins, held))]
    order = (2, 4, 3, 5, 0, 1)
    for i in order:
        loads[i].start()
    fin0, fin1, fin2, fin3 = held[2:6]
    project, combine = made
    stores = [
        pltpu.make_async_copy(project.at[1], outs[2].at[1], out_sem.at[0]),
        pltpu.make_async_copy(combine, outs[3], out_sem.at[1]),
        pltpu.make_async_copy(project.at[0], outs[2].at[0], out_sem.at[2]),
        pltpu.make_async_copy(held[0], outs[0], out_sem.at[3]),
        pltpu.make_async_copy(held[1], outs[1], out_sem.at[4]),
    ]
    loads[2].wait()
    project[1, :, D:] = fin0[0:D, :].astype(F32) * factor
    project[1, :, 0:D] = fin0[D:, 0:D].astype(F32) * factor
    stores[0].start()
    combine[1] = fin0[D:, D:].astype(F32) * factor
    loads[4].wait()
    combine[0, :, 0:BLOCK] = fin2[0:D, :].astype(F32) * factor
    combine[0, :, BLOCK:] = fin2[D:, :].astype(F32) * factor
    stores[1].start()
    loads[3].wait()
    project[0, :, D : 2 * D] = fin1[0:D, :].astype(F32) * factor
    project[0, :, 2 * D :] = fin1[D:, :].astype(F32) * factor
    loads[5].wait()
    project[0, :, 0:BLOCK] = fin3[0:D, :].astype(F32) * factor
    project[0, :, BLOCK:D] = fin3[D:, :].astype(F32) * factor
    stores[2].start()
    for i in range(2):
        loads[i].wait()
        stores[3 + i].start()
    for item in stores:
        item.wait()


def per_device(ntm, nsp, wave_field, cotangent, block_lists, project_weights, combine_weights):
    shapes = scratch_shapes(ntm, nsp)
    names = tuple(shapes)
    anywhere = pl.BlockSpec(memory_space=pl.ANY)
    rows = jax.ShapeDtypeStruct((FR, ROWS, D), BF16)
    results = pl.pallas_call(
        functools.partial(step_kernel, ntm, nsp, names),
        out_shape=(rows, rows) + tuple(jax.ShapeDtypeStruct((512, lanes), BF16) for lanes in LANES),
        in_specs=[anywhere] * 5,
        out_specs=(anywhere,) * 6,
        scratch_shapes=list(shapes.values()),
        compiler_params=pltpu.CompilerParams(
            collective_id=0, has_side_effects=True, vmem_limit_bytes=LIMIT
        ),
        name="cuboid_step",
    )(block_lists, wave_field, cotangent, project_weights, combine_weights)
    factor = 1.0 / math.sqrt(FR * ntm * ROWS * nsp)
    return pl.pallas_call(
        functools.partial(finish_kernel, factor),
        out_shape=(
            rows,
            rows,
            jax.ShapeDtypeStruct((2, D, 3 * D), F32),
            jax.ShapeDtypeStruct((2, D, D), F32),
        ),
        in_specs=[anywhere] * 6,
        out_specs=(anywhere,) * 4,
        scratch_shapes=[pltpu.VMEM((FR, ROWS, D), BF16)] * 2
        + [pltpu.VMEM((512, lanes), BF16) for lanes in LANES]
        + [
            pltpu.VMEM((2, D, 3 * D), F32),
            pltpu.VMEM((2, D, D), F32),
            pltpu.SemaphoreType.DMA((6,)),
            pltpu.SemaphoreType.DMA((5,)),
        ],
        compiler_params=pltpu.CompilerParams(vmem_limit_bytes=LIMIT),
        name="finish",
    )(*results)


def solution(mesh):
    in_specs = (P("tm", "space", None), P("tm", "space", None), P("tm", "space", None), P(), P())
    out_specs = (P("tm", "space", None), P("tm", "space", None), P(), P())
    return jax.shard_map(
        functools.partial(per_device, mesh.shape["tm"], mesh.shape["space"]),
        mesh=mesh,
        in_specs=in_specs,
        out_specs=out_specs,
        check_vma=False,
    )
```
